256 devices in a mesh: tm: 8 (over z), row: 8 (over x, core), obs: 4 (over y).
Axes of the slice: x: 4, y: 4, z: 8, core: 2. Of those that a mesh axis runs over, the one named last changes fastest.
Arguments:
- dyn_pattern: int32 [16, 8, 3], P('tm'), may hold values from 0 to 7
- dyn_values: float32 [16, 1024, 384], P('tm', ('row', 'obs')), may hold values from -0.3125 to 0.3125
- offsets: float32 [16, 1024], P('tm', ('row', 'obs')), may hold values from -6 to 6
- covariance: float32 [16, 1024, 1024], P('tm', ('row', 'obs')), may hold values from -1 to 14, as said below
- obs_block: int32 [16, 128], P('tm'), may hold values from 0 to 7
- obs_matrix: float32 [16, 128, 256], P('tm', 'obs'), may hold values from -0.375 to 0.375
- obs_data: float32 [16, 128], P('tm', 'obs'), may hold values from -6 to 6
Outputs:
- scan_dynamics: float32 [8, 1024, 1024], P('tm', ('row', 'obs'))
- scan_offset: float32 [8, 1024], P('tm', ('row', 'obs'))
- scan_covariance: float32 [8, 1024, 1024], P('tm', ('row', 'obs'))
- scan_factor: float32 [8, 1024, 512], P('tm', ('row', 'obs'))
- scan_information: float32 [8, 1024], P('tm', ('row', 'obs'))
The draws below stay inside these ranges and needn't reach their ends.
Inputs may be any that keep to these rules, and one draw needn't show every extreme that they name: `dyn_pattern`: each entry names a block column. `obs_block`: each entry names a state block. Each covariance is symmetric and positive definite.
All inputs are finite; a program needn't handle non-finite values.
Results may differ from the reference program's by a relative error of at most 0.00019.
Values sent between devices are 32-bit elements; how exact they have to be, the bound alone decides.
A program may use at most 128 MiB of HBM per device.

```python
import math
import jax
import jax.numpy as jnp
from jax import lax

STATES = 1024
BLK = 128
KBLK = 3
NBLK = 8
OBS = 128
ELEMS = 16
N_TM = 8


def draw_covariance(key, part):
    keys = jax.random.split(jax.random.fold_in(key, 17), 2)
    spread_scale = 1.5 / math.sqrt(STATES)
    raw = jax.random.uniform(keys[0], (ELEMS, STATES, STATES), jnp.float32, -1.0, 1.0) * spread_scale
    symmetric = 0.5 * (raw + jnp.swapaxes(raw, 1, 2))
    diagonal = jax.random.uniform(keys[1], (ELEMS, STATES), jnp.float32, 2.0, 3.5)
    positions = jnp.arange(STATES)
    on_diagonal = positions[:, None] == positions[None, :]
    matrix = jnp.where(on_diagonal[None, :, :], diagonal[:, :, None], symmetric)
    return matrix


def touch_ends(array, rng, least, largest):
    index_at = [jax.random.randint(jax.random.fold_in(rng, axis), (), 0, length) for axis, length in enumerate(array.shape)]
    widest = array.shape.index(max(array.shape))
    beside = index_at[:widest] + [(index_at[widest] + 1) % array.shape[widest]] + index_at[widest + 1:]
    return array.at[tuple(index_at)].set(least).at[tuple(beside)].set(largest)


def block_levels(own_key, dims, shards, least, top_value):
    def one(dim, shards_of):
        draws = jax.random.uniform(jax.random.fold_in(jax.random.fold_in(own_key, 6), dim), (shards_of,), jnp.float32, least / len(shards), top_value / len(shards))
        return jnp.repeat(jnp.exp(draws), dims[dim] // shards_of).reshape((-1,) + (1,) * (len(dims) - dim - 1))

    gain = one(*shards[0])
    for cut in shards[1:]:
        gain = gain * one(*cut)
    return gain


def scatter_about(rng, extent, width, most, shards=(), kind=jnp.bfloat16):
    level = block_levels(rng, extent, shards, -0.22, 0.18) if shards else 1.0
    array = jax.random.normal(rng, extent, jnp.float32) * width * level
    return jnp.minimum(jnp.maximum(array, -most), most).astype(kind)


def setup_inputs(seed: int = 0) -> dict:
    splits = jax.random.split(jax.random.key(seed), 8)
    return {
        "dyn_pattern": touch_ends(jax.random.randint(splits[0], (ELEMS, NBLK, KBLK), 0, NBLK), jax.random.fold_in(splits[0], 1), 0, NBLK - 1).astype(jnp.int32),
        "dyn_values": scatter_about(splits[1], (ELEMS, STATES, KBLK * BLK), (KBLK * BLK) ** -0.5, 0.3125, ((0, 8), (1, 32)), jnp.float32),
        "offsets": scatter_about(splits[2], (ELEMS, STATES), 1.0, 6.0, ((0, 8), (1, 32)), jnp.float32),
        "covariance": draw_covariance(jax.random.fold_in(splits[7], 71), 0),
        "obs_block": touch_ends(jax.random.randint(splits[4], (ELEMS, OBS), 0, NBLK), jax.random.fold_in(splits[4], 1), 0, NBLK - 1).astype(jnp.int32),
        "obs_matrix": scatter_about(splits[5], (ELEMS, OBS, 2 * BLK), (2 * BLK) ** -0.5, 0.375, ((0, 8), (1, 4)), jnp.float32),
        "obs_data": scatter_about(splits[6], (ELEMS, OBS), 1.0, 6.0, ((0, 8), (1, 4)), jnp.float32),
    }


largest_value = lax.Precision.HIGHEST

def product(left, right):
    return jnp.dot(left.astype(jnp.float32), right.astype(jnp.float32), precision=largest_value, preferred_element_type=jnp.float32)

def lower_solve(lower, rhs):
    return lax.linalg.triangular_solve(lower, rhs, left_side=True, lower=True)

def assemble_dynamics(pattern, values):
    number_of_blocks = pattern.shape[0]
    per_row = pattern.shape[1]
    states = values.shape[0]
    block_extent = states // number_of_blocks
    indicator_matrix = (pattern[:, :, None] == jnp.arange(number_of_blocks, dtype=jnp.int32)[None, None, :]).astype(jnp.float32)
    blocks = values.reshape(number_of_blocks, block_extent, per_row, block_extent)
    return jnp.einsum('ckd,cikj->cidj', indicator_matrix, blocks, precision=largest_value).reshape(states, states)

def assemble_factor(indices, matrix, number_of_blocks):
    item_count = matrix.shape[0]
    block_extent = matrix.shape[1] // 2
    reach = (indices[:, None] + jnp.arange(2, dtype=jnp.int32)[None, :]) % number_of_blocks
    indicator_matrix = (reach[:, :, None] == jnp.arange(number_of_blocks, dtype=jnp.int32)[None, None, :]).astype(jnp.float32)
    piece_list = matrix.reshape(item_count, 2, block_extent)
    return jnp.einsum('onr,onz->rzo', indicator_matrix, piece_list, precision=largest_value).reshape(number_of_blocks * block_extent, item_count)

def combine(prior_dyn, prior_offsets, prior_cov, prior_factor, prior_zeta, own_dyn, own_offsets, own_cov, own_factor, own_zeta):
    rank_width = own_factor.shape[1]
    gain_rows = product(prior_cov, own_factor)
    system = jnp.eye(rank_width, dtype=jnp.float32) + product(own_factor.T, gain_rows)
    lower = jnp.linalg.cholesky(system)
    carried = product(own_dyn, gain_rows)
    observed = product(prior_dyn.T, own_factor)
    upper_part = lower_solve(lower, observed.T)
    weights = lower_solve(lower, carried.T).T
    new_dyn = product(own_dyn, prior_dyn) - product(weights, upper_part)
    new_cov = product(own_dyn, product(prior_cov, own_dyn.T)) - product(weights, weights.T) + own_cov
    residual = own_zeta - product(own_factor.T, prior_offsets)
    solved = lower_solve(lower, residual[:, None])[:, 0]
    new_offsets = product(own_dyn, prior_offsets) + product(weights, solved) + own_offsets
    new_factor = jnp.concatenate([upper_part.T, prior_factor], axis=1)
    new_zeta = jnp.concatenate([solved, prior_zeta])
    return (new_dyn, new_offsets, new_cov, new_factor, new_zeta)

def reference(dyn_pattern, dyn_values, offsets, covariance, obs_block, obs_matrix, obs_data):
    level_one = []
    for pair_index in range(N_TM):
        elements = []
        for slot_index in range(2):
            element_index = 2 * pair_index + slot_index
            dynamics = assemble_dynamics(dyn_pattern[element_index], dyn_values[element_index])
            factor = assemble_factor(obs_block[element_index], obs_matrix[element_index], NBLK)
            elements.append((dynamics, offsets[element_index], covariance[element_index], factor, obs_data[element_index]))
        level_one.append(combine(*elements[0], *elements[1]))
    level_two = []
    for quad_index in range(N_TM // 2):
        level_two.append(combine(*level_one[2 * quad_index], *level_one[2 * quad_index + 1]))
    dyn_list, off_list, cov_list, fac_list, info_list = ([], [], [], [], [])
    for turn_index in range(N_TM):
        if turn_index % 2 == 0:
            dynamics, offset_vec, cov_mat, factor, zeta_vec = level_two[turn_index // 2]
        else:
            dynamics, offset_vec, cov_mat, factor, zeta_vec = level_one[turn_index]
            factor = jnp.concatenate([factor, jnp.zeros((STATES, 2 * OBS), jnp.float32)], axis=1)
            zeta_vec = jnp.concatenate([zeta_vec, jnp.zeros((2 * OBS,), jnp.float32)])
        dyn_list.append(dynamics)
        off_list.append(offset_vec)
        cov_list.append(cov_mat)
        fac_list.append(factor)
        info_list.append(product(factor, zeta_vec))
    return (jnp.stack(dyn_list), jnp.stack(off_list), jnp.stack(cov_list), jnp.stack(fac_list), jnp.stack(info_list))
```

```python
import functools

import jax
import jax.numpy as jnp
from jax import lax
from jax.experimental import pallas as pl
from jax.experimental.pallas import tpu as pltpu
from jax.sharding import PartitionSpec as P

F32 = jnp.float32
BF = jnp.bfloat16
NN = (((1,), (0,)), ((), ()))
NT = (((1,), (1,)), ((), ()))
TN = (((0,), (0,)), ((), ()))
MESH = pl.DeviceIdType.MESH
VM = pl.BlockSpec(memory_space=pltpu.VMEM)
SM = pl.BlockSpec(memory_space=pltpu.SMEM)
ANY = pl.BlockSpec(memory_space=pl.ANY)
NB = 8
BW = 128
GROUP = 32
OBS_DEV = 4
TM_DEV = 8
PAN = 32
INTERPRET = False


def halves(x):
    hi = x.astype(BF)
    return hi, (x - hi.astype(F32)).astype(BF)


def mm(a, b, dims):
    ah, al = a if isinstance(a, tuple) else halves(a)
    bh, bl = b if isinstance(b, tuple) else halves(b)
    d = functools.partial(lax.dot_general, dimension_numbers=dims, preferred_element_type=F32)
    return d(ah, bh) + (d(ah, bl) + d(al, bh))


def local(body, outs, scratch=(), specs=None, vmem=48 << 20):
    def call(*args):
        return pl.pallas_call(
            body,
            out_shape=[jax.ShapeDtypeStruct(s, F32) for s in outs],
            in_specs=specs if specs else [VM] * len(args),
            out_specs=[VM] * len(outs),
            scratch_shapes=list(scratch),
            compiler_params=pltpu.CompilerParams(vmem_limit_bytes=vmem),
            interpret=INTERPRET,
        )(*args)

    return call


def chol_inverse(s_ref, n_ref, n):
    rows = lax.broadcasted_iota(jnp.int32, (n, n), 0)
    cols = lax.broadcasted_iota(jnp.int32, (n, n), 1)
    n_ref[...] = jnp.where(rows == cols, 1.0, 0.0).astype(F32)
    sub = lax.broadcasted_iota(jnp.int32, (8, 1), 0)
    lane = lax.broadcasted_iota(jnp.int32, (8, n), 1)
    for k0 in range(0, n, 8):
        r = s_ref[k0 : k0 + 8, :]
        m = n_ref[k0 : k0 + 8, :]
        c = [r[:, k0 + j : k0 + j + 1] for j in range(8)]
        for j in range(8):
            piv = c[j][j : j + 1, :]
            inv = lax.rsqrt(piv)
            inv = inv * (1.5 - 0.5 * piv * inv * inv)
            low = jnp.where(sub > j, c[j] * inv, 0.0)
            row = r[j : j + 1, :] * inv
            mrow = m[j : j + 1, :] * inv
            r = jnp.where(sub == j, row, r - low * row)
            m = jnp.where(sub == j, mrow, m - low * mrow)
            for q in range(j + 1, 8):
                c[q] = c[q] - low * (c[q][j : j + 1, :] * inv)
        n_ref[k0 : k0 + 8, :] = m
        if k0 + 8 < n:
            later = jnp.where(lane >= k0 + 8, r, 0.0)
            both = jnp.concatenate([later, m], axis=1)
            change = lax.dot_general(
                later, both, TN, precision=lax.Precision.HIGHEST, preferred_element_type=F32
            )
            s_ref[k0 + 8 :, :] = s_ref[k0 + 8 :, :] - change[k0 + 8 :, :n]
            n_ref[k0 + 8 :, :] = n_ref[k0 + 8 :, :] - change[k0 + 8 :, n:]


def eye(n):
    rows = lax.broadcasted_iota(jnp.int32, (n, n), 0)
    cols = lax.broadcasted_iota(jnp.int32, (n, n), 1)
    return jnp.where(rows == cols, 1.0, 0.0).astype(F32)


def block_row(v_ref, c, e):
    return v_ref[pl.ds(4 * c, 4), e].reshape(BW, 3 * BW)


def times_dyn_t(x_ref, pat, v_ref, e):
    out = []
    for c in range(NB):
        xs = jnp.concatenate([x_ref[pat[e, c, k]] for k in range(3)], axis=1)
        out.append(mm(xs, block_row(v_ref, c, e), NT))
    return out


def put_blocks(ref, x):
    for d in range(NB):
        ref[d] = x[:, d * BW : (d + 1) * BW]


def pack(y):
    return [
        jnp.concatenate([y[s * 8 : s * 8 + 8, q * PAN : q * PAN + PAN] for s in range(4)], axis=1)
        for q in range(GROUP)
    ]


def unpack(rec_ref, base, z_ref):
    for s in range(4):
        z_ref[:, s * 8 : s * 8 + 8, :] = rec_ref[:, base : base + 8, s * PAN : s * PAN + PAN]


def factor_body(blk_ref, obs_ref, cov_ref, phi_ref, g_ref):
    for e in range(2):
        mat = obs_ref[:, e].reshape(BW, 2 * BW)
        blk = blk_ref[e]
        nxt = lax.rem(blk + 1, NB)
        for d in range(NB):
            phi_ref[e, :, d * BW : (d + 1) * BW] = jnp.where(blk == d, mat[:, :BW], 0.0) + jnp.where(
                nxt == d, mat[:, BW:], 0.0
            )
    g_ref[...] = mm(cov_ref[0], phi_ref[1], NT)


def first_system_body(me, phi_ref, g_ref, cov_ref, offs_ref, zeta_ref, linv_ref, k_ref, p_ref, x_ref, solved_ref, s_ref):
    g = g_ref[...].reshape(NB * BW, BW)
    phi = phi_ref[1]
    s_ref[...] = eye(BW) + mm(phi, g, NN)
    chol_inverse(s_ref, linv_ref, BW)
    linv = halves(linv_ref[...])
    k = mm(g, linv, NT)
    k_ref[...] = k
    kh = halves(k)
    row0 = pl.multiple_of((me[0] * OBS_DEV + me[1]) * PAN, PAN)
    p_ref[...] = cov_ref[0] - mm(k_ref[pl.ds(row0, PAN), :], kh, NT)
    b = jnp.broadcast_to(offs_ref[0:1, :], (8, NB * BW))
    z = jnp.broadcast_to(zeta_ref[1:2, :], (8, BW))
    solved = mm(z - mm(b, phi, NT), linv, NT)
    solved_ref[...] = solved
    x_ref[...] = b + mm(solved, kh, NT)


def first_step_body(
    me, pat, v_ref, vals_ref, phi_ref, linv_ref, k_ref, p_ref, x_ref, solved_ref, offs_ref, zeta_ref,
    pk_ref, lamt_ref, b_ref, u_ref, lam_ref, fac_ref, info_ref,
    o_ref, xt_ref, t_ref, acc_ref,
):
    row, col = me[0], me[1]
    lo = pl.multiple_of(col * PAN, PAN)
    o_ref[...] = jnp.zeros_like(o_ref)
    for c in range(NB):
        t = mm(phi_ref[1, :, c * BW : (c + 1) * BW], block_row(v_ref, c, 0), NN)
        for k in range(3):
            d = pat[0, c, k]
            o_ref[d] = o_ref[d] + t[:, k * BW : (k + 1) * BW]
    linv = halves(linv_ref[...])
    for d in range(NB):
        u_ref[d] = mm(linv, o_ref[d], NN)
    t_ref[...] = u_ref[row].T
    upper = t_ref[pl.ds(lo, PAN), :]
    kh = halves(k_ref[...])
    drop = mm(upper, kh, NT)
    p = p_ref[...]
    x = x_ref[...]
    for c in range(NB):
        blk = block_row(v_ref, c, 0)
        w = jnp.zeros((BW, BW), F32)
        for k in range(3):
            w = w + jnp.where(pat[0, c, k] == row, blk[:, k * BW : (k + 1) * BW], 0.0)
        t_ref[...] = w.T
        sl = slice(c * BW, (c + 1) * BW)
        xt_ref[c] = jnp.concatenate([p[:, sl], t_ref[pl.ds(lo, PAN), :] - drop[:, sl], x[:, sl]], axis=0)
    y = jnp.concatenate(times_dyn_t(xt_ref, pat, v_ref, 1), axis=1)
    lamt_ref[...] = y[PAN : 2 * PAN, :]
    b_ref[...] = y[2 * PAN :, :] + offs_ref[1:2, :]
    for q, blk in enumerate(pack(y[:PAN, :])):
        pk_ref[q] = blk
    acc_ref[...] = jnp.zeros_like(acc_ref)
    ak = jnp.zeros((PAN, BW), F32)
    for k in range(3):
        b = pat[1, row, k]
        mine = halves(vals_ref[1, :, k * BW : (k + 1) * BW])
        t = mm(mine, block_row(v_ref, b, 0), NN)
        for k2 in range(3):
            d = pat[0, b, k2]
            acc_ref[d] = acc_ref[d] + t[:, k2 * BW : (k2 + 1) * BW]
        ak = ak + mm(mine, k_ref[pl.ds(pl.multiple_of(b * BW, BW), BW), :], NN)
    akh = halves(ak)
    for d in range(NB):
        lam_ref[:, d * BW : (d + 1) * BW] = acc_ref[d] - mm(akh, u_ref[d], NN)
    o_ref[0] = phi_ref[0, :, 0:BW]
    for d in range(NB):
        o_ref[d] = phi_ref[0, :, d * BW : (d + 1) * BW]
    t_ref[...] = o_ref[row].T
    prior = t_ref[pl.ds(lo, PAN), :]
    fac_ref[:, :BW] = upper
    fac_ref[:, BW:] = prior
    zeta = jnp.broadcast_to(zeta_ref[0:1, :], (8, BW))
    info_ref[...] = mm(solved_ref[...], upper, NT) + mm(zeta, prior, NT)


def dyn_times(z_ref, pat, v_ref, e, c):
    zs = jnp.concatenate([z_ref[pl.ds(4 * pat[e, c, k], 4)].reshape(BW, PAN) for k in range(3)], axis=0)
    return mm(block_row(v_ref, c, e), zs, NN)


def first_cov_body(pat, v_ref, rec_ref, cov_ref, c_ref, z_ref):
    unpack(rec_ref, 0, z_ref)
    for c in range(NB):
        sl = slice(c * BW, (c + 1) * BW)
        c_ref[:, sl] = dyn_times(z_ref, pat, v_ref, 1, c).T + cov_ref[1, :, sl]


def both_factors(u_ref, phi_ref):
    u = jnp.concatenate([u_ref[d] for d in range(NB)], axis=1)
    return jnp.concatenate([u, phi_ref[0]], axis=0)


def second_gain_body(ca_ref, u_ref, phi_ref, g_ref):
    g_ref[...] = mm(ca_ref[...], both_factors(u_ref, phi_ref), NT)


def second_step_body(
    me, pat, v_ref, g_ref, u_ref, phi_ref, k_ref, ca_ref, lamta_ref, ba_ref, solved_ref, zeta_ref, bb_ref,
    pk_ref, up_ref, b_ref, info_ref,
    s_ref, linv_ref, k2_ref, xt_ref,
):
    g = g_ref[...].reshape(NB * BW, 2 * BW)
    phi = halves(both_factors(u_ref, phi_ref))
    s_ref[...] = eye(2 * BW) + mm(phi, g, NN)
    chol_inverse(s_ref, linv_ref, 2 * BW)
    linv = halves(linv_ref[...])
    k2 = mm(g, linv, NT)
    k2_ref[...] = k2
    k2h = halves(k2)
    row0 = pl.multiple_of((me[0] * OBS_DEV + me[1]) * PAN, PAN)
    ca = ca_ref[...]
    p = ca - mm(k2_ref[pl.ds(row0, PAN), :], k2h, NT)
    lamta = lamta_ref[...]
    upper = mm(mm(lamta, phi, NT), linv, NT)
    up_ref[...] = upper
    mt = lamta - mm(upper, k2h, NT)
    zeta = jnp.concatenate([solved_ref[...], jnp.broadcast_to(zeta_ref[0:1, :], (8, BW))], axis=1)
    ba = ba_ref[...]
    solved = mm(zeta - mm(ba, phi, NT), linv, NT)
    info_ref[...] = mm(solved, upper, NT)
    xt = jnp.concatenate([p, mt, ba + mm(solved, k2h, NT)], axis=0)
    put_blocks(xt_ref, xt)
    u = jnp.concatenate([u_ref[d] for d in range(NB)], axis=1)
    h = jnp.concatenate(times_dyn_t(xt_ref, pat, v_ref, 0), axis=1)
    put_blocks(xt_ref, h - mm(mm(xt, u, NT), k_ref[...], NT))
    y = jnp.concatenate(times_dyn_t(xt_ref, pat, v_ref, 1), axis=1)
    b_ref[...] = y[2 * PAN :, :] + bb_ref[1:2, :]
    for q, blk in enumerate(pack(y[:PAN, :])):
        pk_ref[q, 0:8] = blk
    for q, blk in enumerate(pack(y[PAN : 2 * PAN, :])):
        pk_ref[q, 8:16] = blk


def second_cov_body(pat, v_ref, rec_ref, u_ref, k_ref, cb_ref, c_ref, lam_ref, z_ref, z2_ref):
    unpack(rec_ref, 8, z_ref)
    for c in range(NB):
        lam_ref[:, c * BW : (c + 1) * BW] = z_ref[4 * c : 4 * c + 4].reshape(BW, PAN).T
    unpack(rec_ref, 0, z_ref)
    uz = jnp.zeros((BW, PAN), F32)
    for d in range(NB):
        uz = uz + mm(u_ref[d], z_ref[4 * d : 4 * d + 4].reshape(BW, PAN), NN)
    kz = mm(k_ref[...], uz, NN)
    for c in range(NB):
        part = dyn_times(z_ref, pat, v_ref, 0, c) - kz[c * BW : (c + 1) * BW, :]
        z2_ref[4 * c : 4 * c + 4] = part.reshape(4, PAN, PAN)
    for c in range(NB):
        sl = slice(c * BW, (c + 1) * BW)
        c_ref[:, sl] = dyn_times(z2_ref, pat, v_ref, 1, c).T + cb_ref[:, sl]


def exchange_body(kinds, *refs):
    n = len(kinds)
    src, dst = refs[:n], refs[n : 2 * n]
    send, recv, own = refs[2 * n :]
    tm, row, obs = lax.axis_index("tm"), lax.axis_index("row"), lax.axis_index("obs")
    me = row * OBS_DEV + obs
    steps = [kind for kind in kinds if isinstance(kind, int)]
    wide = any(kind in ("gather", "all") for kind in kinds)
    barrier = pltpu.get_barrier_semaphore()
    count = 0
    if wide:

        def greet(off, carry):
            t = lax.rem(me + off, GROUP)
            pl.semaphore_signal(
                barrier, inc=1, device_id=(tm, t // OBS_DEV, lax.rem(t, OBS_DEV)), device_id_type=MESH
            )
            return carry

        lax.fori_loop(1, GROUP, greet, 0)
        count += GROUP - 1
    if steps:
        for step in (1, TM_DEV - 1):
            pl.semaphore_signal(
                barrier, inc=1, device_id=(lax.rem(tm + step, TM_DEV), row, obs), device_id_type=MESH
            )
        count += 2
    for i, kind in enumerate(kinds):
        if kind == "gather":
            pltpu.make_async_copy(src[i], dst[i].at[me], own.at[i]).start()
        elif kind == "all":
            pltpu.make_async_copy(src[i].at[me], dst[i].at[me], own.at[i]).start()
        elif kind == "line":
            pltpu.make_async_copy(src[i], dst[i].at[obs], own.at[i]).start()
    pl.semaphore_wait(barrier, count)

    def shift(i, step):
        return pltpu.make_async_remote_copy(
            src_ref=src[i], dst_ref=dst[i], send_sem=send.at[i, 0], recv_sem=recv.at[i, 0],
            device_id=(lax.rem(tm + step + TM_DEV, TM_DEV), row, obs), device_id_type=MESH,
        )

    def line(i, off):
        return pltpu.make_async_remote_copy(
            src_ref=src[i], dst_ref=dst[i].at[obs], send_sem=send.at[i, off], recv_sem=recv.at[i, off],
            device_id=(tm, row, lax.rem(obs + off, OBS_DEV)), device_id_type=MESH,
        )

    def spread(i, off):
        t = lax.rem(me + off, GROUP)
        return pltpu.make_async_remote_copy(
            src_ref=src[i].at[t] if kinds[i] == "all" else src[i],
            dst_ref=dst[i].at[me], send_sem=send.at[i, off], recv_sem=recv.at[i, off],
            device_id=(tm, t // OBS_DEV, lax.rem(t, OBS_DEV)), device_id_type=MESH,
        )

    for i, kind in enumerate(kinds):
        if isinstance(kind, int):
            shift(i, kind).start()
        if kind == "line":
            for off in range(1, OBS_DEV):
                line(i, off).start()
    if wide:

        def begin(off, carry):
            for i, kind in enumerate(kinds):
                if kind in ("gather", "all"):
                    spread(i, off).start()
            return carry

        lax.fori_loop(1, GROUP, begin, 0)
    for i, kind in enumerate(kinds):
        if kind == "gather":
            pltpu.make_async_copy(src[i], dst[i].at[me], own.at[i]).wait()
        elif kind == "all":
            pltpu.make_async_copy(src[i].at[me], dst[i].at[me], own.at[i]).wait()
        elif kind == "line":
            pltpu.make_async_copy(src[i], dst[i].at[obs], own.at[i]).wait()
            for off in range(1, OBS_DEV):
                line(i, off).wait()
        else:
            shift(i, kind).wait()
    if wide:

        def finish(off, carry):
            for i, kind in enumerate(kinds):
                if kind in ("gather", "all"):
                    spread(i, off).wait()
            return carry

        lax.fori_loop(1, GROUP, finish, 0)


def exchange(ident, *moves):
    kinds = [kind for kind, _ in moves]
    arrays = [array for _, array in moves]
    lead = {"gather": (GROUP,), "line": (OBS_DEV,)}
    outs = [
        jax.ShapeDtypeStruct(lead.get(kind, ()) + array.shape, array.dtype) for kind, array in moves
    ]
    n = len(moves)
    return pl.pallas_call(
        functools.partial(exchange_body, kinds),
        out_shape=outs,
        in_specs=[ANY] * n,
        out_specs=[ANY] * n,
        scratch_shapes=[
            pltpu.SemaphoreType.DMA((n, GROUP)),
            pltpu.SemaphoreType.DMA((n, GROUP)),
            pltpu.SemaphoreType.DMA((n,)),
        ],
        compiler_params=pltpu.CompilerParams(collective_id=ident, has_side_effects=True),
    )(*arrays)


ST = NB * BW

factor_call = local(factor_body, [(2, BW, ST), (PAN, BW)])
first_system_call = local(
    first_system_body,
    [(BW, BW), (ST, BW), (PAN, ST), (8, ST), (8, BW)],
    [pltpu.VMEM((BW, BW), F32)],
    [SM] + [VM] * 5,
)
first_step_call = local(
    first_step_body,
    [(GROUP, 8, BW), (PAN, ST), (8, ST), (NB, BW, BW), (PAN, ST), (PAN, 2 * BW), (8, PAN)],
    [pltpu.VMEM((NB, BW, BW), F32), pltpu.VMEM((NB, 2 * PAN + 8, BW), F32), pltpu.VMEM((BW, BW), F32), pltpu.VMEM((NB, PAN, BW), F32)],
    [SM] * 2 + [VM] * 10,
)
first_cov_call = local(first_cov_body, [(PAN, ST)], [pltpu.VMEM((GROUP, PAN, PAN), F32)], [SM] + [VM] * 3)
second_gain_call = local(second_gain_body, [(PAN, 2 * BW)])
second_step_call = local(
    second_step_body,
    [(GROUP, 16, BW), (PAN, 2 * BW), (8, ST), (8, PAN)],
    [
        pltpu.VMEM((2 * BW, 2 * BW), F32),
        pltpu.VMEM((2 * BW, 2 * BW), F32),
        pltpu.VMEM((ST, 2 * BW), F32),
        pltpu.VMEM((NB, 2 * PAN + 8, BW), F32),
    ],
    [SM] * 2 + [VM] * 11,
)
second_cov_call = local(
    second_cov_body,
    [(PAN, ST), (PAN, ST)],
    [pltpu.VMEM((GROUP, PAN, PAN), F32), pltpu.VMEM((GROUP, PAN, PAN), F32)],
    [SM] + [VM] * 5,
)


def unpack_small(small):
    offs = jnp.swapaxes(small[:, 0:2, :PAN], 0, 1).reshape(2, ST)
    zeta = jnp.swapaxes(small[:OBS_DEV, 2:4, :PAN], 0, 1).reshape(2, BW)
    return offs, zeta


def per_device(dyn_pattern, dyn_values, offsets, covariance, obs_block, obs_matrix, obs_data):
    row, obs = lax.axis_index("row"), lax.axis_index("obs")
    me = jnp.stack([row, obs]).astype(jnp.int32)
    start = (row * OBS_DEV + obs) * PAN
    all_values = lax.all_gather(dyn_values, ("row", "obs"), axis=0, tiled=False)
    small = jnp.pad(jnp.concatenate([offsets, obs_data], axis=0), ((0, 4), (0, BW - PAN)))
    obs_rows, small = exchange(0, ("line", obs_matrix), ("gather", small))
    offs, zeta = unpack_small(small)
    phi, gain_pan = factor_call(obs_block[:, :, None], obs_rows, covariance)
    (gain,) = exchange(1, ("gather", gain_pan))
    linv, kal, p_pan, x_row, solved = first_system_call(me, phi, gain, covariance, offs, zeta)
    packed, lam_t, b_full, upper, lam_pan, fac_pan, info = first_step_call(
        me, dyn_pattern, all_values, dyn_values, phi, linv, kal, p_pan, x_row, solved, offs, zeta
    )
    received, lam_t_a, b_a = exchange(2, ("all", packed), (1, lam_t), (1, b_full))
    (cov_pan,) = first_cov_call(dyn_pattern, all_values, received, covariance)
    (cov_a,) = exchange(3, (1, cov_pan))
    (gain2_pan,) = second_gain_call(cov_a, upper, phi)
    (gain2,) = exchange(4, ("gather", gain2_pan))
    packed2, upper2, b2, info2 = second_step_call(
        me, dyn_pattern, all_values, gain2, upper, phi, kal, cov_a, lam_t_a, b_a, solved, zeta,
        b_full,
    )
    (received2,) = exchange(5, ("all", packed2))
    cov2, lam2 = second_cov_call(dyn_pattern, all_values, received2, upper, kal, cov_pan)
    top_cov, top_lam, top_up, top_b, top_info = exchange(
        6, (-1, cov2), (-1, lam2), (-1, upper2), (-1, b2), (-1, info2)
    )
    even = lax.axis_index("tm") % 2 == 0
    out_dyn = jnp.where(even, top_lam, lam_pan)
    out_cov = jnp.where(even, top_cov, cov_pan)
    out_off = lax.dynamic_slice_in_dim(jnp.where(even, top_b[0], b_full[0]), start, PAN, 0)
    zero = jnp.zeros_like(fac_pan)
    out_fac = jnp.where(
        even, jnp.concatenate([top_up, fac_pan], axis=1), jnp.concatenate([fac_pan, zero], axis=1)
    )
    out_info = jnp.where(even, info[0] + top_info[0], info[0])
    return (out_dyn[None], out_off[None], out_cov[None], out_fac[None], out_info[None])


def solution(mesh):
    placed = (
        P("tm", None, None),
        P("tm", ("row", "obs"), None),
        P("tm", ("row", "obs")),
        P("tm", ("row", "obs"), None),
        P("tm", None),
        P("tm", "obs", None),
        P("tm", "obs"),
    )
    return jax.shard_map(
        per_device,
        mesh=mesh,
        in_specs=placed,
        out_specs=(
            P("tm", ("row", "obs"), None),
            P("tm", ("row", "obs")),
            P("tm", ("row", "obs"), None),
            P("tm", ("row", "obs"), None),
            P("tm", ("row", "obs")),
        ),
        check_vma=False,
    )
```

```python
import functools

import jax
import jax.numpy as jnp
from jax import lax
from jax.experimental import pallas as pl
from jax.experimental.pallas import tpu as pltpu
from jax.sharding import PartitionSpec as P

F32 = jnp.float32
BF = jnp.bfloat16
NN = (((1,), (0,)), ((), ()))
NT = (((1,), (1,)), ((), ()))
TN = (((0,), (0,)), ((), ()))
MESH = pl.DeviceIdType.MESH
VM = pl.BlockSpec(memory_space=pltpu.VMEM)
SM = pl.BlockSpec(memory_space=pltpu.SMEM)
ANY = pl.BlockSpec(memory_space=pl.ANY)
NB = 8
BW = 128
GROUP = 32
OBS_DEV = 4
TM_DEV = 8
PAN = 32
INTERPRET = False


def halves(x):
    hi = x.astype(BF)
    return hi, (x - hi.astype(F32)).astype(BF)


def mm(a, b, dims):
    ah, al = a if isinstance(a, tuple) else halves(a)
    bh, bl = b if isinstance(b, tuple) else halves(b)
    d = functools.partial(lax.dot_general, dimension_numbers=dims, preferred_element_type=F32)
    return d(ah, bh) + (d(ah, bl) + d(al, bh))


def local(body, outs, scratch=(), specs=None, vmem=48 << 20):
    def call(*args):
        return pl.pallas_call(
            body,
            out_shape=[jax.ShapeDtypeStruct(s, F32) for s in outs],
            in_specs=specs if specs else [VM] * len(args),
            out_specs=[VM] * len(outs),
            scratch_shapes=list(scratch),
            compiler_params=pltpu.CompilerParams(vmem_limit_bytes=vmem),
            interpret=INTERPRET,
        )(*args)

    return call


def chol_inverse(s_ref, n_ref):
    n_ref[...] = eye(BW)
    sub = lax.broadcasted_iota(jnp.int32, (8, BW), 0)
    lane = lax.broadcasted_iota(jnp.int32, (32, BW), 1)

    def panel(b, carry):
        k0 = pl.multiple_of(b * 32, 32)
        r = [s_ref[pl.ds(k0 + 8 * t, 8), :] for t in range(4)]
        n = [n_ref[pl.ds(k0 + 8 * t, 8), :] for t in range(4)]
        a = [pltpu.roll(x, lax.rem(BW - k0, BW), 1) for x in r]
        for h in range(4):
            c = {t: [jnp.broadcast_to(a[t][:, 8 * h + j : 8 * h + j + 1], (8, BW)) for j in range(8)] for t in range(h, 4)}
            piv = jnp.ones((8, BW), F32)
            for j in range(8):
                p = jnp.broadcast_to(c[h][j][j : j + 1, :], (8, BW))
                inv = 1.0 / p
                piv = jnp.where(sub == j, p, piv)
                own = [c[h][m][j : j + 1, :] for m in range(8)]
                ra, rr, rn = a[h][j : j + 1, :], r[h][j : j + 1, :], n[h][j : j + 1, :]
                for t in range(h, 4):
                    f = c[t][j] * inv
                    if t == h:
                        f = jnp.where(sub > j, f, 0.0)
                    for m in range(j + 1, 8):
                        c[t][m] = c[t][m] - f * own[m]
                    if h < 3:
                        a[t] = a[t] - f * ra
                    r[t] = r[t] - f * rr
                    n[t] = n[t] - f * rn
            scale = lax.rsqrt(piv)
            scale = scale * (1.5 - 0.5 * piv * scale * scale)
            r[h] = r[h] * scale
            n[h] = n[h] * scale
        for t in range(4):
            n_ref[pl.ds(k0 + 8 * t, 8), :] = n[t]

        @pl.when(b < 3)
        def _():
            rows = jnp.concatenate(r, axis=0)
            later = jnp.where(lane >= k0 + 32, rows, 0.0)
            both = jnp.concatenate([rows, jnp.concatenate(n, axis=0)], axis=1)
            lh = later.astype(BF).astype(F32)
            bh = both.astype(BF).astype(F32)
            left = jnp.concatenate([lh, lh, later - lh], axis=0).astype(BF)
            right = jnp.concatenate([bh, both - bh, bh], axis=0).astype(BF)
            change = lax.dot_general(left, right, TN, preferred_element_type=F32)
            s_ref[...] = s_ref[...] - change[:, :BW]
            n_ref[...] = n_ref[...] - change[:, BW:]

        return carry

    lax.fori_loop(0, 4, panel, 0)

def chol_inverse_2(s_ref, linv_ref, t_ref, n_ref):
    t_ref[...] = s_ref[:BW, :BW]
    chol_inverse(t_ref, n_ref)
    n1 = n_ref[...]
    n1h = halves(n1)
    low = mm(s_ref[BW:, :BW], n1h, NT)
    lowh = halves(low)
    t_ref[...] = s_ref[BW:, BW:] - mm(lowh, lowh, NT)
    cross = mm(lowh, n1h, NN)
    chol_inverse(t_ref, n_ref)
    n2 = n_ref[...]
    linv_ref[:BW, :BW] = n1
    linv_ref[:BW, BW:] = jnp.zeros((BW, BW), F32)
    linv_ref[BW:, :BW] = -mm(n2, cross, NN)
    linv_ref[BW:, BW:] = n2


def eye(n):
    rows = lax.broadcasted_iota(jnp.int32, (n, n), 0)
    cols = lax.broadcasted_iota(jnp.int32, (n, n), 1)
    return jnp.where(rows == cols, 1.0, 0.0).astype(F32)


def block_row(v_ref, c, e):
    return v_ref[pl.ds(4 * c, 4), e].reshape(BW, 3 * BW)


def times_dyn_t(x_ref, pat, v_ref, e):
    out = []
    for c in range(NB):
        xs = jnp.concatenate([x_ref[pat[e, c, k]] for k in range(3)], axis=1)
        out.append(mm(xs, block_row(v_ref, c, e), NT))
    return out


def put_blocks(ref, x):
    for d in range(NB):
        ref[d] = x[:, d * BW : (d + 1) * BW]


def pack(y):
    return [
        jnp.concatenate([y[s * 8 : s * 8 + 8, q * PAN : q * PAN + PAN] for s in range(4)], axis=1)
        for q in range(GROUP)
    ]


def unpack(rec_ref, base, z_ref):
    for s in range(4):
        z_ref[:, s * 8 : s * 8 + 8, :] = rec_ref[:, base : base + 8, s * PAN : s * PAN + PAN]


def factor_body(blk_ref, obs_ref, cov_ref, phi_ref, g_ref):
    for e in range(2):
        mat = obs_ref[:, e].reshape(BW, 2 * BW)
        blk = blk_ref[e]
        nxt = lax.rem(blk + 1, NB)
        for d in range(NB):
            phi_ref[e, :, d * BW : (d + 1) * BW] = jnp.where(blk == d, mat[:, :BW], 0.0) + jnp.where(
                nxt == d, mat[:, BW:], 0.0
            )
    g_ref[...] = mm(cov_ref[0], phi_ref[1], NT)


def first_system_body(me, phi_ref, g_ref, cov_ref, offs_ref, zeta_ref, linv_ref, k_ref, p_ref, x_ref, solved_ref, s_ref):
    g = g_ref[...].reshape(NB * BW, BW)
    phi = phi_ref[1]
    s_ref[...] = eye(BW) + mm(phi, g, NN)
    chol_inverse(s_ref, linv_ref)
    linv = halves(linv_ref[...])
    k = mm(g, linv, NT)
    k_ref[...] = k
    kh = halves(k)
    row0 = pl.multiple_of((me[0] * OBS_DEV + me[1]) * PAN, PAN)
    p_ref[...] = cov_ref[0] - mm(k_ref[pl.ds(row0, PAN), :], kh, NT)
    b = jnp.broadcast_to(offs_ref[0:1, :], (8, NB * BW))
    z = jnp.broadcast_to(zeta_ref[1:2, :], (8, BW))
    solved = mm(z - mm(b, phi, NT), linv, NT)
    solved_ref[...] = solved
    x_ref[...] = b + mm(solved, kh, NT)


def first_step_body(
    me, pat, v_ref, vals_ref, phi_ref, linv_ref, k_ref, p_ref, x_ref, solved_ref, offs_ref, zeta_ref,
    pk_ref, lamt_ref, b_ref, u_ref, lam_ref, fac_ref, info_ref,
    o_ref, xt_ref, t_ref, acc_ref,
):
    row, col = me[0], me[1]
    lo = pl.multiple_of(col * PAN, PAN)
    o_ref[...] = jnp.zeros_like(o_ref)
    for c in range(NB):
        t = mm(phi_ref[1, :, c * BW : (c + 1) * BW], block_row(v_ref, c, 0), NN)
        for k in range(3):
            d = pat[0, c, k]
            o_ref[d] = o_ref[d] + t[:, k * BW : (k + 1) * BW]
    linv = halves(linv_ref[...])
    for d in range(NB):
        u_ref[d] = mm(linv, o_ref[d], NN)
    t_ref[...] = u_ref[row].T
    upper = t_ref[pl.ds(lo, PAN), :]
    kh = halves(k_ref[...])
    drop = mm(upper, kh, NT)
    p = p_ref[...]
    x = x_ref[...]
    for c in range(NB):
        blk = block_row(v_ref, c, 0)
        w = jnp.zeros((BW, BW), F32)
        for k in range(3):
            w = w + jnp.where(pat[0, c, k] == row, blk[:, k * BW : (k + 1) * BW], 0.0)
        t_ref[...] = w.T
        sl = slice(c * BW, (c + 1) * BW)
        xt_ref[c] = jnp.concatenate([p[:, sl], t_ref[pl.ds(lo, PAN), :] - drop[:, sl], x[:, sl]], axis=0)
    y = jnp.concatenate(times_dyn_t(xt_ref, pat, v_ref, 1), axis=1)
    lamt_ref[...] = y[PAN : 2 * PAN, :]
    b_ref[...] = y[2 * PAN :, :] + offs_ref[1:2, :]
    for q, blk in enumerate(pack(y[:PAN, :])):
        pk_ref[q] = blk
    acc_ref[...] = jnp.zeros_like(acc_ref)
    ak = jnp.zeros((PAN, BW), F32)
    for k in range(3):
        b = pat[1, row, k]
        mine = halves(vals_ref[1, :, k * BW : (k + 1) * BW])
        t = mm(mine, block_row(v_ref, b, 0), NN)
        for k2 in range(3):
            d = pat[0, b, k2]
            acc_ref[d] = acc_ref[d] + t[:, k2 * BW : (k2 + 1) * BW]
        ak = ak + mm(mine, k_ref[pl.ds(pl.multiple_of(b * BW, BW), BW), :], NN)
    akh = halves(ak)
    for d in range(NB):
        lam_ref[:, d * BW : (d + 1) * BW] = acc_ref[d] - mm(akh, u_ref[d], NN)
    o_ref[0] = phi_ref[0, :, 0:BW]
    for d in range(NB):
        o_ref[d] = phi_ref[0, :, d * BW : (d + 1) * BW]
    t_ref[...] = o_ref[row].T
    prior = t_ref[pl.ds(lo, PAN), :]
    fac_ref[:, :BW] = upper
    fac_ref[:, BW:] = prior
    zeta = jnp.broadcast_to(zeta_ref[0:1, :], (8, BW))
    info_ref[...] = mm(solved_ref[...], upper, NT) + mm(zeta, prior, NT)


def dyn_times(z_ref, pat, v_ref, e, c):
    zs = jnp.concatenate([z_ref[pl.ds(4 * pat[e, c, k], 4)].reshape(BW, PAN) for k in range(3)], axis=0)
    return mm(block_row(v_ref, c, e), zs, NN)


def first_cov_body(pat, v_ref, rec_ref, cov_ref, c_ref, z_ref):
    unpack(rec_ref, 0, z_ref)
    for c in range(NB):
        sl = slice(c * BW, (c + 1) * BW)
        c_ref[:, sl] = dyn_times(z_ref, pat, v_ref, 1, c).T + cov_ref[1, :, sl]


def both_factors(u_ref, phi_ref):
    u = jnp.concatenate([u_ref[d] for d in range(NB)], axis=1)
    return jnp.concatenate([u, phi_ref[0]], axis=0)


def second_gain_body(ca_ref, u_ref, phi_ref, g_ref):
    g_ref[...] = mm(ca_ref[...], both_factors(u_ref, phi_ref), NT)


def second_step_body(
    me, pat, v_ref, g_ref, u_ref, phi_ref, k_ref, ca_ref, lamta_ref, ba_ref, solved_ref, zeta_ref, bb_ref,
    pk_ref, up_ref, b_ref, info_ref,
    s_ref, linv_ref, k2_ref, xt_ref, t_ref, n_ref,
):
    g = g_ref[...].reshape(NB * BW, 2 * BW)
    phi = halves(both_factors(u_ref, phi_ref))
    s_ref[...] = eye(2 * BW) + mm(phi, g, NN)
    chol_inverse_2(s_ref, linv_ref, t_ref, n_ref)
    linv = halves(linv_ref[...])
    k2 = mm(g, linv, NT)
    k2_ref[...] = k2
    k2h = halves(k2)
    row0 = pl.multiple_of((me[0] * OBS_DEV + me[1]) * PAN, PAN)
    ca = ca_ref[...]
    p = ca - mm(k2_ref[pl.ds(row0, PAN), :], k2h, NT)
    lamta = lamta_ref[...]
    upper = mm(mm(lamta, phi, NT), linv, NT)
    up_ref[...] = upper
    mt = lamta - mm(upper, k2h, NT)
    zeta = jnp.concatenate([solved_ref[...], jnp.broadcast_to(zeta_ref[0:1, :], (8, BW))], axis=1)
    ba = ba_ref[...]
    solved = mm(zeta - mm(ba, phi, NT), linv, NT)
    info_ref[...] = mm(solved, upper, NT)
    xt = jnp.concatenate([p, mt, ba + mm(solved, k2h, NT)], axis=0)
    put_blocks(xt_ref, xt)
    u = jnp.concatenate([u_ref[d] for d in range(NB)], axis=1)
    h = jnp.concatenate(times_dyn_t(xt_ref, pat, v_ref, 0), axis=1)
    put_blocks(xt_ref, h - mm(mm(xt, u, NT), k_ref[...], NT))
    y = jnp.concatenate(times_dyn_t(xt_ref, pat, v_ref, 1), axis=1)
    b_ref[...] = y[2 * PAN :, :] + bb_ref[1:2, :]
    for q, blk in enumerate(pack(y[:PAN, :])):
        pk_ref[q, 0:8] = blk
    for q, blk in enumerate(pack(y[PAN : 2 * PAN, :])):
        pk_ref[q, 8:16] = blk


def second_cov_body(pat, v_ref, rec_ref, u_ref, k_ref, cb_ref, c_ref, lam_ref, z_ref, z2_ref):
    unpack(rec_ref, 8, z_ref)
    for c in range(NB):
        lam_ref[:, c * BW : (c + 1) * BW] = z_ref[4 * c : 4 * c + 4].reshape(BW, PAN).T
    unpack(rec_ref, 0, z_ref)
    uz = jnp.zeros((BW, PAN), F32)
    for d in range(NB):
        uz = uz + mm(u_ref[d], z_ref[4 * d : 4 * d + 4].reshape(BW, PAN), NN)
    kz = mm(k_ref[...], uz, NN)
    for c in range(NB):
        part = dyn_times(z_ref, pat, v_ref, 0, c) - kz[c * BW : (c + 1) * BW, :]
        z2_ref[4 * c : 4 * c + 4] = part.reshape(4, PAN, PAN)
    for c in range(NB):
        sl = slice(c * BW, (c + 1) * BW)
        c_ref[:, sl] = dyn_times(z2_ref, pat, v_ref, 1, c).T + cb_ref[:, sl]


def exchange_body(kinds, *refs):
    n = len(kinds)
    src, dst = refs[:n], refs[n : 2 * n]
    send, recv, own = refs[2 * n :]
    tm, row, obs = lax.axis_index("tm"), lax.axis_index("row"), lax.axis_index("obs")
    me = row * OBS_DEV + obs
    steps = [kind for kind in kinds if isinstance(kind, int)]
    wide = any(kind in ("gather", "all") for kind in kinds)
    barrier = pltpu.get_barrier_semaphore()
    count = 0
    if wide:

        def greet(off, carry):
            t = lax.rem(me + off, GROUP)
            pl.semaphore_signal(
                barrier, inc=1, device_id=(tm, t // OBS_DEV, lax.rem(t, OBS_DEV)), device_id_type=MESH
            )
            return carry

        lax.fori_loop(1, GROUP, greet, 0)
        count += GROUP - 1
    if steps:
        for step in (1, TM_DEV - 1):
            pl.semaphore_signal(
                barrier, inc=1, device_id=(lax.rem(tm + step, TM_DEV), row, obs), device_id_type=MESH
            )
        count += 2
    for i, kind in enumerate(kinds):
        if kind == "gather":
            pltpu.make_async_copy(src[i], dst[i].at[me], own.at[i]).start()
        elif kind == "all":
            pltpu.make_async_copy(src[i].at[me], dst[i].at[me], own.at[i]).start()
        elif kind == "line":
            pltpu.make_async_copy(src[i], dst[i].at[obs], own.at[i]).start()
    pl.semaphore_wait(barrier, count)

    def shift(i, step):
        return pltpu.make_async_remote_copy(
            src_ref=src[i], dst_ref=dst[i], send_sem=send.at[i, 0], recv_sem=recv.at[i, 0],
            device_id=(lax.rem(tm + step + TM_DEV, TM_DEV), row, obs), device_id_type=MESH,
        )

    def line(i, off):
        return pltpu.make_async_remote_copy(
            src_ref=src[i], dst_ref=dst[i].at[obs], send_sem=send.at[i, off], recv_sem=recv.at[i, off],
            device_id=(tm, row, lax.rem(obs + off, OBS_DEV)), device_id_type=MESH,
        )

    def spread(i, off):
        t = lax.rem(me + off, GROUP)
        return pltpu.make_async_remote_copy(
            src_ref=src[i].at[t] if kinds[i] == "all" else src[i],
            dst_ref=dst[i].at[me], send_sem=send.at[i, off], recv_sem=recv.at[i, off],
            device_id=(tm, t // OBS_DEV, lax.rem(t, OBS_DEV)), device_id_type=MESH,
        )

    for i, kind in enumerate(kinds):
        if isinstance(kind, int):
            shift(i, kind).start()
        if kind == "line":
            for off in range(1, OBS_DEV):
                line(i, off).start()
    if wide:

        def begin(off, carry):
            for i, kind in enumerate(kinds):
                if kind in ("gather", "all"):
                    spread(i, off).start()
            return carry

        lax.fori_loop(1, GROUP, begin, 0)
    for i, kind in enumerate(kinds):
        if kind == "gather":
            pltpu.make_async_copy(src[i], dst[i].at[me], own.at[i]).wait()
        elif kind == "all":
            pltpu.make_async_copy(src[i].at[me], dst[i].at[me], own.at[i]).wait()
        elif kind == "line":
            pltpu.make_async_copy(src[i], dst[i].at[obs], own.at[i]).wait()
            for off in range(1, OBS_DEV):
                line(i, off).wait()
        else:
            shift(i, kind).wait()
    if wide:

        def finish(off, carry):
            for i, kind in enumerate(kinds):
                if kind in ("gather", "all"):
                    spread(i, off).wait()
            return carry

        lax.fori_loop(1, GROUP, finish, 0)


def exchange(ident, *moves):
    kinds = [kind for kind, _ in moves]
    arrays = [array for _, array in moves]
    lead = {"gather": (GROUP,), "line": (OBS_DEV,)}
    outs = [
        jax.ShapeDtypeStruct(lead.get(kind, ()) + array.shape, array.dtype) for kind, array in moves
    ]
    n = len(moves)
    return pl.pallas_call(
        functools.partial(exchange_body, kinds),
        out_shape=outs,
        in_specs=[ANY] * n,
        out_specs=[ANY] * n,
        scratch_shapes=[
            pltpu.SemaphoreType.DMA((n, GROUP)),
            pltpu.SemaphoreType.DMA((n, GROUP)),
            pltpu.SemaphoreType.DMA((n,)),
        ],
        compiler_params=pltpu.CompilerParams(collective_id=ident, has_side_effects=True),
    )(*arrays)


ST = NB * BW

factor_call = local(factor_body, [(2, BW, ST), (PAN, BW)])
first_system_call = local(
    first_system_body,
    [(BW, BW), (ST, BW), (PAN, ST), (8, ST), (8, BW)],
    [pltpu.VMEM((BW, BW), F32)],
    [SM] + [VM] * 5,
)
first_step_call = local(
    first_step_body,
    [(GROUP, 8, BW), (PAN, ST), (8, ST), (NB, BW, BW), (PAN, ST), (PAN, 2 * BW), (8, PAN)],
    [pltpu.VMEM((NB, BW, BW), F32), pltpu.VMEM((NB, 2 * PAN + 8, BW), F32), pltpu.VMEM((BW, BW), F32), pltpu.VMEM((NB, PAN, BW), F32)],
    [SM] * 2 + [VM] * 10,
)
first_cov_call = local(first_cov_body, [(PAN, ST)], [pltpu.VMEM((GROUP, PAN, PAN), F32)], [SM] + [VM] * 3)
second_gain_call = local(second_gain_body, [(PAN, 2 * BW)])
second_step_call = local(
    second_step_body,
    [(GROUP, 16, BW), (PAN, 2 * BW), (8, ST), (8, PAN)],
    [
        pltpu.VMEM((2 * BW, 2 * BW), F32),
        pltpu.VMEM((2 * BW, 2 * BW), F32),
        pltpu.VMEM((ST, 2 * BW), F32),
        pltpu.VMEM((NB, 2 * PAN + 8, BW), F32),
        pltpu.VMEM((BW, BW), F32),
        pltpu.VMEM((BW, BW), F32),
    ],
    [SM] * 2 + [VM] * 11,
)
second_cov_call = local(
    second_cov_body,
    [(PAN, ST), (PAN, ST)],
    [pltpu.VMEM((GROUP, PAN, PAN), F32), pltpu.VMEM((GROUP, PAN, PAN), F32)],
    [SM] + [VM] * 5,
)


def unpack_small(small):
    offs = jnp.swapaxes(small[:, 0:2, :PAN], 0, 1).reshape(2, ST)
    zeta = jnp.swapaxes(small[:OBS_DEV, 2:4, :PAN], 0, 1).reshape(2, BW)
    return offs, zeta


def per_device(dyn_pattern, dyn_values, offsets, covariance, obs_block, obs_matrix, obs_data):
    row, obs = lax.axis_index("row"), lax.axis_index("obs")
    me = jnp.stack([row, obs]).astype(jnp.int32)
    start = (row * OBS_DEV + obs) * PAN
    all_values = lax.all_gather(dyn_values, ("row", "obs"), axis=0, tiled=False)
    small = jnp.pad(jnp.concatenate([offsets, obs_data], axis=0), ((0, 4), (0, BW - PAN)))
    obs_rows, small = exchange(0, ("line", obs_matrix), ("gather", small))
    offs, zeta = unpack_small(small)
    phi, gain_pan = factor_call(obs_block[:, :, None], obs_rows, covariance)
    (gain,) = exchange(1, ("gather", gain_pan))
    linv, kal, p_pan, x_row, solved = first_system_call(me, phi, gain, covariance, offs, zeta)
    packed, lam_t, b_full, upper, lam_pan, fac_pan, info = first_step_call(
        me, dyn_pattern, all_values, dyn_values, phi, linv, kal, p_pan, x_row, solved, offs, zeta
    )
    received, lam_t_a, b_a = exchange(2, ("all", packed), (1, lam_t), (1, b_full))
    (cov_pan,) = first_cov_call(dyn_pattern, all_values, received, covariance)
    (cov_a,) = exchange(3, (1, cov_pan))
    (gain2_pan,) = second_gain_call(cov_a, upper, phi)
    (gain2,) = exchange(4, ("gather", gain2_pan))
    packed2, upper2, b2, info2 = second_step_call(
        me, dyn_pattern, all_values, gain2, upper, phi, kal, cov_a, lam_t_a, b_a, solved, zeta,
        b_full,
    )
    (received2,) = exchange(5, ("all", packed2))
    cov2, lam2 = second_cov_call(dyn_pattern, all_values, received2, upper, kal, cov_pan)
    top_cov, top_lam, top_up, top_b, top_info = exchange(
        6, (-1, cov2), (-1, lam2), (-1, upper2), (-1, b2), (-1, info2)
    )
    even = lax.axis_index("tm") % 2 == 0
    out_dyn = jnp.where(even, top_lam, lam_pan)
    out_cov = jnp.where(even, top_cov, cov_pan)
    out_off = lax.dynamic_slice_in_dim(jnp.where(even, top_b[0], b_full[0]), start, PAN, 0)
    zero = jnp.zeros_like(fac_pan)
    out_fac = jnp.where(
        even, jnp.concatenate([top_up, fac_pan], axis=1), jnp.concatenate([fac_pan, zero], axis=1)
    )
    out_info = jnp.where(even, info[0] + top_info[0], info[0])
    return (out_dyn[None], out_off[None], out_cov[None], out_fac[None], out_info[None])


def solution(mesh):
    placed = (
        P("tm", None, None),
        P("tm", ("row", "obs"), None),
        P("tm", ("row", "obs")),
        P("tm", ("row", "obs"), None),
        P("tm", None),
        P("tm", "obs", None),
        P("tm", "obs"),
    )
    return jax.shard_map(
        per_device,
        mesh=mesh,
        in_specs=placed,
        out_specs=(
            P("tm", ("row", "obs"), None),
            P("tm", ("row", "obs")),
            P("tm", ("row", "obs"), None),
            P("tm", ("row", "obs"), None),
            P("tm", ("row", "obs")),
        ),
        check_vma=False,
    )
```

```python
import functools

import jax
import jax.numpy as jnp
from jax import lax
from jax.experimental import pallas as pl
from jax.experimental.pallas import tpu as pltpu
from jax.sharding import PartitionSpec as P

F32 = jnp.float32
BF = jnp.bfloat16
NN = (((1,), (0,)), ((), ()))
NT = (((1,), (1,)), ((), ()))
TN = (((0,), (0,)), ((), ()))
MESH = pl.DeviceIdType.MESH
VM = pl.BlockSpec(memory_space=pltpu.VMEM)
SM = pl.BlockSpec(memory_space=pltpu.SMEM)
ANY = pl.BlockSpec(memory_space=pl.ANY)
NB = 8
BW = 128
ST = NB * BW
GROUP = 32
SIDE = 4
TM_DEV = 8
PAN = 32


def halves(x):
    hi = x.astype(BF)
    return hi, (x - hi.astype(F32)).astype(BF)
def mm(a, b, dims):
    ah, al = a if isinstance(a, tuple) else halves(a)
    bh, bl = b if isinstance(b, tuple) else halves(b)
    d = functools.partial(lax.dot_general, dimension_numbers=dims, preferred_element_type=F32)
    return d(ah, bh) + (d(ah, bl) + d(al, bh))
def eye(n):
    rows = lax.broadcasted_iota(jnp.int32, (n, n), 0)
    cols = lax.broadcasted_iota(jnp.int32, (n, n), 1)
    return jnp.where(rows == cols, 1.0, 0.0).astype(F32)


def chol_inverse(s_ref, n_ref):
    n_ref[...] = eye(BW)
    sub = lax.broadcasted_iota(jnp.int32, (8, BW), 0)
    lane = lax.broadcasted_iota(jnp.int32, (32, BW), 1)

    def panel(b, carry):
        k0 = pl.multiple_of(b * 32, 32)
        r = [s_ref[pl.ds(k0 + 8 * t, 8), :] for t in range(4)]
        n = [n_ref[pl.ds(k0 + 8 * t, 8), :] for t in range(4)]
        a = [pltpu.roll(x, lax.rem(BW - k0, BW), 1) for x in r]
        for h in range(4):
            c = {t: [jnp.broadcast_to(a[t][:, 8 * h + j : 8 * h + j + 1], (8, BW)) for j in range(8)] for t in range(h, 4)}
            piv = jnp.ones((8, BW), F32)
            for j in range(8):
                p = jnp.broadcast_to(c[h][j][j : j + 1, :], (8, BW))
                inv = 1.0 / p
                piv = jnp.where(sub == j, p, piv)
                own = [c[h][m][j : j + 1, :] for m in range(8)]
                ra, rr, rn = a[h][j : j + 1, :], r[h][j : j + 1, :], n[h][j : j + 1, :]
                for t in range(h, 4):
                    f = c[t][j] * inv
                    if t == h:
                        f = jnp.where(sub > j, f, 0.0)
                    for m in range(j + 1, 8):
                        c[t][m] = c[t][m] - f * own[m]
                    if h < 3:
                        a[t] = a[t] - f * ra
                    r[t] = r[t] - f * rr
                    n[t] = n[t] - f * rn
            scale = lax.rsqrt(piv)
            scale = scale * (1.5 - 0.5 * piv * scale * scale)
            r[h] = r[h] * scale
            n[h] = n[h] * scale
        for t in range(4):
            n_ref[pl.ds(k0 + 8 * t, 8), :] = n[t]

        @pl.when(b < 3)
        def _():
            rows = jnp.concatenate(r, axis=0)
            later = jnp.where(lane >= k0 + 32, rows, 0.0)
            both = jnp.concatenate([rows, jnp.concatenate(n, axis=0)], axis=1)
            lh = later.astype(BF).astype(F32)
            bh = both.astype(BF).astype(F32)
            left = jnp.concatenate([lh, lh, later - lh], axis=0).astype(BF)
            right = jnp.concatenate([bh, both - bh, bh], axis=0).astype(BF)
            change = lax.dot_general(left, right, TN, preferred_element_type=F32)
            s_ref[...] = s_ref[...] - change[:, :BW]
            n_ref[...] = n_ref[...] - change[:, BW:]

        return carry

    lax.fori_loop(0, 4, panel, 0)

def chol_inverse_2(s_ref, linv_ref, t_ref, n_ref):
    t_ref[...] = s_ref[:BW, :BW]
    chol_inverse(t_ref, n_ref)
    n1 = n_ref[...]
    n1h = halves(n1)
    low = mm(s_ref[BW:, :BW], n1h, NT)
    lowh = halves(low)
    t_ref[...] = s_ref[BW:, BW:] - mm(lowh, lowh, NT)
    cross = mm(lowh, n1h, NN)
    chol_inverse(t_ref, n_ref)
    n2 = n_ref[...]
    linv_ref[:BW, :BW] = n1
    linv_ref[:BW, BW:] = jnp.zeros((BW, BW), F32)
    linv_ref[BW:, :BW] = -mm(n2, cross, NN)
    linv_ref[BW:, BW:] = n2


def times_dyn_t(x_ref, pat, rows, e):
    out = []
    for c in range(NB):
        xs = jnp.concatenate([x_ref[pat[e, c, k]] for k in range(3)], axis=1)
        out.append(mm(xs, rows(c), NT))
    return out


def dyn_times(z_ref, pat, rows, e, c):
    zs = jnp.concatenate([z_ref[pat[e, c, k]].reshape(BW, PAN) for k in range(3)], axis=0)
    return mm(rows(c), zs, NN)


def is_block(found, block):
    return (found == block).astype(F32)


def put_blocks(ref, x):
    for d in range(NB):
        ref[d] = x[:, d * BW : (d + 1) * BW]


def pack(y):
    return [
        jnp.concatenate([y[s * 8 : s * 8 + 8, q * PAN : q * PAN + PAN] for s in range(4)], axis=1)
        for q in range(GROUP)
    ]


def unpack(rec_ref, base, z_ref):
    for s in range(4):
        part = rec_ref[:, base : base + 8, s * PAN : s * PAN + PAN]
        z_ref[:, :, s * 8 : s * 8 + 8, :] = part.reshape(NB, 4, 8, PAN)


def factor_rows(blk, mat):
    at = jnp.broadcast_to(blk.astype(F32), (BW, BW)).T
    out = []
    for d in range(NB):
        before = (d + NB - 1) % NB
        out.append(jnp.where(at == d, mat[:, :BW], 0.0) + jnp.where(at == before, mat[:, BW:], 0.0))
    return out


class Gather:
    def __init__(self, place, src, buf, send, recv, swapped):
        tm, row, obs = place
        x, core = row // 2, lax.rem(row, 2)
        self.core, self.buf, self.src = core, buf, src
        self.i, self.j = (obs, x) if swapped else (x, obs)
        self.send, self.recv = send, recv

        def device(i, j, c):
            xx, yy = (j, i) if swapped else (i, j)
            return (tm, 2 * xx + c, yy)

        self.device = device

    def copy(self, src, dst, n, device):
        return pltpu.make_async_remote_copy(
            src_ref=src, dst_ref=dst, send_sem=self.send.at[n], recv_sem=self.recv.at[n],
            device_id=device, device_id_type=MESH,
        )

    def first(self, d):
        piece = self.buf.at[self.core, self.i, self.j]
        j = lax.rem(self.j + d, SIDE)
        return self.copy(self.src if self.src is not None else piece, piece, d - 1, self.device(self.i, j, self.core))

    def second(self, d):
        block = self.buf.at[self.core, self.i]
        i = lax.rem(self.i + d, SIDE)
        return self.copy(block, block, 2 + d, self.device(i, self.j, self.core))

    def across(self, d):
        block = self.buf.at[self.core, lax.rem(self.i + SIDE - d, SIDE)]
        return self.copy(block, block, 6 + d, self.device(self.i, self.j, 1 - self.core))

    def phase1(self):
        for d in range(1, SIDE):
            self.first(d).start()

    def phase2(self):
        for d in range(1, SIDE):
            self.first(d).wait_recv()
        for d in range(1, SIDE):
            self.second(d).start()
        self.across(0).start()

    def phase3(self):
        for d in range(1, SIDE):
            self.second(d).wait_recv()
            self.across(d).start()

    def finish(self):
        for d in range(SIDE):
            self.across(d).wait_recv()

    def drain(self):
        for d in range(1, SIDE):
            self.first(d).wait_send()
            self.second(d).wait_send()
        for d in range(SIDE):
            self.across(d).wait_send()


class Swap:
    def __init__(self, place, src, dst, send, recv, own):
        self.tm, row, obs = place
        self.me = row * SIDE + obs
        self.src, self.dst, self.send, self.recv, self.own = src, dst, send, recv, own

    def copy(self, off):
        t = lax.rem(self.me + off, GROUP)
        return pltpu.make_async_remote_copy(
            src_ref=self.src.at[t], dst_ref=self.dst.at[self.me],
            send_sem=self.send.at[off], recv_sem=self.recv.at[off],
            device_id=(self.tm, t // SIDE, lax.rem(t, SIDE)), device_id_type=MESH,
        )

    def mine(self):
        return pltpu.make_async_copy(self.src.at[self.me], self.dst.at[self.me], self.own)

    def start(self):
        def begin(off, carry):
            self.copy(off).start()
            return carry

        lax.fori_loop(1, GROUP, begin, 0)
        self.mine().start()

    def finish(self):
        def end(off, carry):
            self.copy(off).wait_recv()
            return carry

        self.mine().wait()
        lax.fori_loop(1, GROUP, end, 0)

    def drain(self):
        def end(off, carry):
            self.copy(off).wait_send()
            return carry

        lax.fori_loop(1, GROUP, end, 0)


def kernel(
    pat, vals, offs, cov, blk, omat, odat,
    out_dyn, out_off, out_cov, out_fac, out_info,
    cov_v, obs_v, vi, vj, ga, gb, phi, s1, t1, n1, linv_v, s2, linv2_v,
    g_v, k_v, u_v, o_v, xt, pk, rec, lamt, lamt_a, bz, ba, c_pan, ca, g2a, g2b, g2_v, k2_v,
    pk2, rec2, fac2, c2, lam2, vec, vec_in, lam, fac, z1, z2, kb_v,
    obs_s, obs_r, gat_s, gat_r, swap_s, swap_r, z_s, z_r, own,
):
    tm, row, obs = lax.axis_index("tm"), lax.axis_index("row"), lax.axis_index("obs")
    place = (tm, row, obs)
    x, core = row // 2, lax.rem(row, 2)
    me = row * SIDE + obs
    row0 = pl.multiple_of(me * PAN, PAN)
    lo = pl.multiple_of(obs * PAN, PAN)
    odd = lax.rem(tm, 2) == 1
    up = (lax.rem(tm + 1, TM_DEV), row, obs)
    down = (lax.rem(tm + TM_DEV - 1, TM_DEV), row, obs)

    def rows_i(c):
        return vi[c % 2, c // 2].reshape(BW, 3 * BW)

    def rows_j(c):
        return vj[c % 2, :, c // 2].reshape(BW, 3 * BW)

    def obs_copy(e, d):
        return pltpu.make_async_remote_copy(
            src_ref=omat.at[e], dst_ref=obs_v.at[e, obs], send_sem=obs_s.at[e, d - 1], recv_sem=obs_r.at[e, d - 1],
            device_id=(tm, row, lax.rem(obs + d, SIDE)), device_id_type=MESH,
        )

    def z_copy(n, src, dst, device):
        return pltpu.make_async_remote_copy(
            src_ref=src, dst_ref=dst, send_sem=z_s.at[n], recv_sem=z_r.at[n], device_id=device, device_id_type=MESH
        )

    gather_i = Gather(place, vals.at[0], vi, gat_s.at[0], gat_r.at[0], False)
    gather_j = Gather(place, vals.at[1], vj, gat_s.at[1], gat_r.at[1], True)
    gather_ga = Gather(place, None, ga, gat_s.at[2], gat_r.at[2], False)
    gather_gb = Gather(place, None, gb, gat_s.at[3], gat_r.at[3], True)
    gather_2a = Gather(place, None, g2a, gat_s.at[4], gat_r.at[4], False)
    gather_2b = Gather(place, None, g2b, gat_s.at[5], gat_r.at[5], True)
    swap1 = Swap(place, pk, rec, swap_s.at[0], swap_r.at[0], own.at[4])
    swap2 = Swap(place, pk2, rec2, swap_s.at[1], swap_r.at[1], own.at[5])
    up_lam = z_copy(0, lamt, lamt_a, up)
    up_b = z_copy(1, bz, ba, up)
    up_cov = z_copy(2, c_pan, ca, up)
    down_dyn = z_copy(3, lam2, out_dyn.at[0], down)
    down_cov = z_copy(4, c2, out_cov.at[0], down)
    down_fac = z_copy(5, fac2, out_fac.at[0, :, 0 : 2 * BW], down)
    down_vec = z_copy(6, vec, vec_in, down)

    local_cov = pltpu.make_async_copy(cov, cov_v, own.at[0])
    local_i = pltpu.make_async_copy(vals.at[0], vi.at[core, x, obs], own.at[1])
    local_j = pltpu.make_async_copy(vals.at[1], vj.at[core, obs, x], own.at[2])
    local_obs = pltpu.make_async_copy(omat, obs_v.at[:, obs], own.at[3])
    local_obs.start()
    local_cov.start()
    local_i.start()
    local_j.start()

    barrier = pltpu.get_barrier_semaphore()

    def greet(off, carry):
        t = lax.rem(me + off, GROUP)
        pl.semaphore_signal(barrier, inc=1, device_id=(tm, t // SIDE, lax.rem(t, SIDE)), device_id_type=MESH)
        return carry

    lax.fori_loop(1, GROUP, greet, 0)
    pl.semaphore_signal(barrier, inc=1, device_id=up, device_id_type=MESH)
    pl.semaphore_signal(barrier, inc=1, device_id=down, device_id_type=MESH)
    pl.semaphore_wait(barrier, GROUP + 1)

    for d in range(1, SIDE):
        obs_copy(1, d).start()
    for d in range(1, SIDE):
        obs_copy(0, d).start()
    gather_i.phase1()
    gather_j.phase1()

    local_obs.wait()
    for d in range(1, SIDE):
        obs_copy(1, d).wait_recv()
    for d, part in enumerate(factor_rows(blk[1:2, :], obs_v[1].reshape(BW, 2 * BW))):
        phi[1, :, d * BW : (d + 1) * BW] = part
    local_cov.wait()
    gain = mm(cov_v[0], phi[1], NT)
    ga[core, x, obs] = gain[0:16]
    small = jnp.concatenate([offs[...], odat[...]], axis=0)
    gb[core, obs, x, 0:16] = gain[16:32]
    gb[core, obs, x, 16:24] = jnp.zeros((8, BW), F32)
    gb[core, obs, x, 16:20, 0:PAN] = small
    gather_ga.phase1()
    gather_gb.phase1()
    gather_ga.phase2()
    gather_gb.phase2()
    local_i.wait()
    local_j.wait()
    gather_i.phase2()
    gather_j.phase2()
    gather_ga.phase3()
    gather_gb.phase3()
    for d in range(1, SIDE):
        obs_copy(0, d).wait_recv()
    for d, part in enumerate(factor_rows(blk[0:1, :], obs_v[0].reshape(BW, 2 * BW))):
        phi[0, :, d * BW : (d + 1) * BW] = part
    gather_ga.finish()
    gather_gb.finish()

    vecs = []
    for c in range(NB):
        both = jnp.concatenate([ga[c % 2, c // 2], gb[c % 2, :, c // 2, 0:16]], axis=1)
        g_v[c * BW : (c + 1) * BW, :] = both.reshape(BW, BW)
        vecs.append(jnp.concatenate([gb[c % 2, o, c // 2, 16:24, 0:PAN] for o in range(SIDE)], axis=1))
    zeta_i = jnp.broadcast_to(vecs[0][2:3, :], (8, BW))
    zeta_j = jnp.broadcast_to(vecs[0][3:4, :], (8, BW))
    b_i = jnp.concatenate([jnp.broadcast_to(v[0:1, :], (8, BW)) for v in vecs], axis=1)
    b_j = jnp.concatenate([jnp.broadcast_to(v[1:2, :], (8, BW)) for v in vecs], axis=1)
    g = halves(g_v[...])
    phi_j = halves(phi[1])
    s1[...] = eye(BW) + mm(phi_j, g, NN)
    chol_inverse(s1, linv_v)
    linv = halves(linv_v[...])
    k = mm(g, linv, NT)
    k_v[...] = k
    for c in range(NB):
        kb_v[c] = k[c * BW : (c + 1) * BW, :]
    kh = halves(k)
    p = cov_v[0] - mm(k_v[pl.ds(row0, PAN), :], kh, NT)
    solved = mm(zeta_j - mm(b_i, phi_j, NT), linv, NT)
    xrow = b_i + mm(solved, kh, NT)
    gather_i.phase3()
    gather_j.phase3()
    gather_i.finish()

    for c in range(NB):
        t = mm(phi[1, :, c * BW : (c + 1) * BW], rows_i(c), NN)
        for d in range(NB):
            part = jnp.zeros((BW, BW), F32) if c == 0 else o_v[d]
            for n in range(3):
                part = part + is_block(pat[0, c, n], d) * t[:, n * BW : (n + 1) * BW]
            o_v[d] = part
    for d in range(NB):
        u_v[d] = mm(linv, o_v[d], NN)
    t1[...] = u_v[row].T
    upper = t1[pl.ds(lo, PAN), :]
    drop = mm(upper, kh, NT)
    for c in range(NB):
        rows = rows_i(c)
        w = jnp.zeros((BW, BW), F32)
        for n in range(3):
            w = w + is_block(pat[0, c, n], row) * rows[:, n * BW : (n + 1) * BW]
        t1[...] = w.T
        sl = slice(c * BW, (c + 1) * BW)
        xt[c] = jnp.concatenate([p[:, sl], t1[pl.ds(lo, PAN), :] - drop[:, sl], xrow[:, sl]], axis=0)
    gather_j.finish()
    y = jnp.concatenate(times_dyn_t(xt, pat, rows_j, 1), axis=1)
    for q, part in enumerate(pack(y[:PAN, :])):
        pk[q] = part
    swap1.start()
    lamt[...] = y[PAN : 2 * PAN, :]
    b_own = y[2 * PAN :, :] + b_j
    bz[...] = b_own

    @pl.when(jnp.logical_not(odd))
    def _():
        up_lam.start()
        up_b.start()

    for d in range(NB):
        o_v[d] = phi[0, :, d * BW : (d + 1) * BW]
    t1[...] = o_v[row].T
    prior = t1[pl.ds(lo, PAN), :]
    fac[:, :BW] = upper
    fac[:, BW : 2 * BW] = prior
    fac[:, 2 * BW :] = jnp.zeros((PAN, 2 * BW), F32)
    info = mm(solved, upper, NT) + mm(zeta_i, prior, NT)
    swap1.finish()

    unpack(rec, 0, z1)
    for c in range(NB):
        sl = slice(c * BW, (c + 1) * BW)
        c_pan[:, sl] = dyn_times(z1, pat, rows_j, 1, c).T + cov_v[1, :, sl]

    def my_panel(full):
        put_blocks(o_v.at[:, 0:8, :], full)
        block = o_v[row, 0:8, :]
        return pltpu.roll(block, lax.rem(BW - lo, BW), 1)[0:1, 0:PAN]

    @pl.when(jnp.logical_not(odd))
    def _():
        up_cov.start()
        pieces = pltpu.make_async_copy(fac.at[:, 0 : 2 * BW], out_fac.at[0, :, 2 * BW :], own.at[6])
        pieces.start()
        pieces.wait()
        down_vec.wait_recv()
        out_off[...] = vec_in[0:1, 0:PAN]
        out_info[...] = info[0:1, :] + vec_in[1:2, 0:PAN]
        down_dyn.wait_recv()
        down_cov.wait_recv()
        down_fac.wait_recv()
        up_lam.wait_send()
        up_b.wait_send()
        up_cov.wait_send()

    @pl.when(odd)
    def _():
        out_off[...] = my_panel(b_own)
        out_info[...] = info[0:1, :]
        ones = [
            pltpu.make_async_copy(c_pan, out_cov.at[0], own.at[6]),
            pltpu.make_async_copy(fac, out_fac.at[0], own.at[7]),
        ]
        for one in ones:
            one.start()
        up_lam.wait_recv()
        up_b.wait_recv()
        lam_parts = [jnp.zeros((PAN, BW), F32) for _ in range(NB)]
        ak = jnp.zeros((PAN, BW), F32)
        for n in range(3):
            b = pat[1, row, n]
            block = vj[core, obs, x, :, n * BW : (n + 1) * BW]
            mine = halves(block)
            t = mm(mine, vi[lax.rem(b, 2), lax.div(b, 2)].reshape(BW, 3 * BW), NN)
            for m in range(3):
                at = pat[0, b, m]
                for d in range(NB):
                    lam_parts[d] = lam_parts[d] + is_block(at, d) * t[:, m * BW : (m + 1) * BW]
            ak = ak + mm(mine, kb_v[b], NN)
        akh = halves(ak)
        for d in range(NB):
            lam[:, d * BW : (d + 1) * BW] = lam_parts[d] - mm(akh, u_v[d], NN)
        dyn_out = pltpu.make_async_copy(lam, out_dyn.at[0], own.at[8])
        dyn_out.start()

        up_cov.wait_recv()
        u = jnp.concatenate([u_v[d] for d in range(NB)], axis=1)
        phi_b = halves(jnp.concatenate([u, phi[0]], axis=0))
        gain2 = mm(ca[...], phi_b, NT)
        g2a[core, x, obs] = gain2[:, :BW]
        g2b[core, obs, x] = gain2[:, BW:]
        gather_2a.phase1()
        gather_2b.phase1()
        gather_2a.phase2()
        gather_2b.phase2()
        gather_2a.phase3()
        gather_2b.phase3()
        gather_2a.finish()
        gather_2b.finish()
        for c in range(NB):
            g2_v[c * BW : (c + 1) * BW, :BW] = g2a[c % 2, c // 2].reshape(BW, BW)
            g2_v[c * BW : (c + 1) * BW, BW:] = g2b[c % 2, :, c // 2].reshape(BW, BW)
        g2 = halves(g2_v[...])
        s2[...] = eye(2 * BW) + mm(phi_b, g2, NN)
        chol_inverse_2(s2, linv2_v, t1, n1)
        linv2 = halves(linv2_v[...])
        k2 = mm(g2, linv2, NT)
        k2_v[...] = k2
        k2h = halves(k2)
        p2 = ca[...] - mm(k2_v[pl.ds(row0, PAN), :], k2h, NT)
        la = lamt_a[...]
        upper2 = mm(mm(la, phi_b, NT), linv2, NT)
        fac2[...] = upper2
        down_fac.start()
        mt = la - mm(upper2, k2h, NT)
        zeta = jnp.concatenate([solved, zeta_i], axis=1)
        bp = ba[...]
        solved2 = mm(zeta - mm(bp, phi_b, NT), linv2, NT)
        xs = jnp.concatenate([p2, mt, bp + mm(solved2, k2h, NT)], axis=0)
        put_blocks(xt, xs)
        h = jnp.concatenate(times_dyn_t(xt, pat, rows_i, 0), axis=1)
        put_blocks(xt, h - mm(mm(xs, u, NT), k_v[...], NT))
        y2 = jnp.concatenate(times_dyn_t(xt, pat, rows_j, 1), axis=1)
        for q, part in enumerate(pack(y2[:PAN, :])):
            pk2[q, 0:8] = part
        for q, part in enumerate(pack(y2[PAN : 2 * PAN, :])):
            pk2[q, 8:16] = part
        swap2.start()
        vec[...] = jnp.zeros((8, BW), F32)
        vec[0:1, 0:PAN] = my_panel(y2[2 * PAN :, :] + b_own)
        vec[1:2, 0:PAN] = mm(solved2, upper2, NT)[0:1, :]
        down_vec.start()
        swap2.finish()
        unpack(rec2, 8, z1)
        for c in range(NB):
            lam2[:, c * BW : (c + 1) * BW] = z1[c].reshape(BW, PAN).T
        down_dyn.start()
        unpack(rec2, 0, z1)
        uz = jnp.zeros((BW, PAN), F32)
        for d in range(NB):
            uz = uz + mm(u_v[d], z1[d].reshape(BW, PAN), NN)
        kz = mm(k_v[...], uz, NN)
        for c in range(NB):
            part = dyn_times(z1, pat, rows_i, 0, c) - kz[c * BW : (c + 1) * BW, :]
            z2[c] = part.reshape(4, PAN, PAN)
        for c in range(NB):
            sl = slice(c * BW, (c + 1) * BW)
            c2[:, sl] = dyn_times(z2, pat, rows_j, 1, c).T + c_pan[:, sl]
        down_cov.start()
        for one in ones:
            one.wait()
        dyn_out.wait()
        gather_2a.drain()
        gather_2b.drain()
        swap2.drain()
        for one in (down_fac, down_vec, down_dyn, down_cov):
            one.wait_send()

    for e in range(2):
        for d in range(1, SIDE):
            obs_copy(e, d).wait_send()
    for one in (gather_i, gather_j, gather_ga, gather_gb):
        one.drain()
    swap1.drain()


def vmem(*shape):
    return pltpu.VMEM(shape, F32)


def dma(*shape):
    return pltpu.SemaphoreType.DMA(shape)


SCRATCH = [
    vmem(2, PAN, ST), vmem(2, SIDE, PAN, 2 * BW),
    vmem(2, SIDE, SIDE, PAN, 3 * BW), vmem(2, SIDE, SIDE, PAN, 3 * BW),
    vmem(2, SIDE, SIDE, 16, BW), vmem(2, SIDE, SIDE, 24, BW),
    vmem(2, BW, ST),
    vmem(BW, BW), vmem(BW, BW), vmem(BW, BW), vmem(BW, BW),
    vmem(2 * BW, 2 * BW), vmem(2 * BW, 2 * BW),
    vmem(ST, BW), vmem(ST, BW), vmem(NB, BW, BW), vmem(NB, BW, BW), vmem(NB, 2 * PAN + 8, BW),
    vmem(GROUP, 8, BW), vmem(GROUP, 8, BW),
    vmem(PAN, ST), vmem(PAN, ST), vmem(8, ST), vmem(8, ST), vmem(PAN, ST), vmem(PAN, ST),
    vmem(2, SIDE, SIDE, PAN, BW), vmem(2, SIDE, SIDE, PAN, BW),
    vmem(ST, 2 * BW), vmem(ST, 2 * BW),
    vmem(GROUP, 16, BW), vmem(GROUP, 16, BW),
    vmem(PAN, 2 * BW), vmem(PAN, ST), vmem(PAN, ST), vmem(8, BW), vmem(8, BW),
    vmem(PAN, ST), vmem(PAN, 4 * BW),
    vmem(NB, 4, PAN, PAN), vmem(NB, 4, PAN, PAN), vmem(NB, BW, BW),
    dma(2, 3), dma(2, 3), dma(6, 10), dma(6, 10), dma(2, GROUP), dma(2, GROUP), dma(7), dma(7), dma(9),
]


def per_device(*args):
    outs = [(1, PAN, ST), (1, PAN), (1, PAN, ST), (1, PAN, 4 * BW), (1, PAN)]
    return pl.pallas_call(
        kernel,
        out_shape=[jax.ShapeDtypeStruct(s, F32) for s in outs],
        in_specs=[SM, ANY, VM, ANY, VM, ANY, VM],
        out_specs=[ANY, VM, ANY, ANY, VM],
        scratch_shapes=SCRATCH,
        compiler_params=pltpu.CompilerParams(
            collective_id=0, has_side_effects=True, vmem_limit_bytes=50 << 20
        ),
    )(*args)


def solution(mesh):
    placed = (
        P("tm", None, None),
        P("tm", ("row", "obs"), None),
        P("tm", ("row", "obs")),
        P("tm", ("row", "obs"), None),
        P("tm", None),
        P("tm", "obs", None),
        P("tm", "obs"),
    )
    return jax.shard_map(
        per_device,
        mesh=mesh,
        in_specs=placed,
        out_specs=(
            P("tm", ("row", "obs"), None),
            P("tm", ("row", "obs")),
            P("tm", ("row", "obs"), None),
            P("tm", ("row", "obs"), None),
            P("tm", ("row", "obs")),
        ),
        check_vma=False,
    )
```

```python
import functools

import jax
import jax.numpy as jnp
from jax import lax
from jax.experimental import pallas as pl
from jax.experimental.pallas import tpu as pltpu
from jax.sharding import PartitionSpec as P

F32 = jnp.float32
BF = jnp.bfloat16
NN = (((1,), (0,)), ((), ()))
NT = (((1,), (1,)), ((), ()))
TN = (((0,), (0,)), ((), ()))
MESH = pl.DeviceIdType.MESH
VM = pl.BlockSpec(memory_space=pltpu.VMEM)
SM = pl.BlockSpec(memory_space=pltpu.SMEM)
ANY = pl.BlockSpec(memory_space=pl.ANY)
NB = 8
BW = 128
ST = NB * BW
GROUP = 32
SIDE = 4
TM_DEV = 8
PAN = 32
CHUNK = 256


def halves(x):
    hi = x.astype(BF)
    return hi, (x - hi.astype(F32)).astype(BF)
def mm(a, b, dims):
    ah, al = a if isinstance(a, tuple) else halves(a)
    bh, bl = b if isinstance(b, tuple) else halves(b)
    d = functools.partial(lax.dot_general, dimension_numbers=dims, preferred_element_type=F32)
    return d(ah, bh) + (d(ah, bl) + d(al, bh))
def eye(n):
    rows = lax.broadcasted_iota(jnp.int32, (n, n), 0)
    cols = lax.broadcasted_iota(jnp.int32, (n, n), 1)
    return jnp.where(rows == cols, 1.0, 0.0).astype(F32)


def chol_inverse(s_ref, n_ref):
    n_ref[...] = eye(BW)
    sub = lax.broadcasted_iota(jnp.int32, (8, BW), 0)
    lane = lax.broadcasted_iota(jnp.int32, (32, BW), 1)

    def panel(b, carry):
        k0 = pl.multiple_of(b * 32, 32)
        r = [s_ref[pl.ds(k0 + 8 * t, 8), :] for t in range(4)]
        n = [n_ref[pl.ds(k0 + 8 * t, 8), :] for t in range(4)]
        a = [pltpu.roll(x, lax.rem(BW - k0, BW), 1) for x in r]
        for h in range(4):
            c = {t: [jnp.broadcast_to(a[t][:, 8 * h + j : 8 * h + j + 1], (8, BW)) for j in range(8)] for t in range(h, 4)}
            piv = jnp.ones((8, BW), F32)
            for j in range(8):
                p = jnp.broadcast_to(c[h][j][j : j + 1, :], (8, BW))
                inv = 1.0 / p
                piv = jnp.where(sub == j, p, piv)
                own = [c[h][m][j : j + 1, :] for m in range(8)]
                ra, rr, rn = a[h][j : j + 1, :], r[h][j : j + 1, :], n[h][j : j + 1, :]
                for t in range(h, 4):
                    f = c[t][j] * inv
                    if t == h:
                        f = jnp.where(sub > j, f, 0.0)
                    for m in range(j + 1, 8):
                        c[t][m] = c[t][m] - f * own[m]
                    if h < 3:
                        a[t] = a[t] - f * ra
                    r[t] = r[t] - f * rr
                    n[t] = n[t] - f * rn
            scale = lax.rsqrt(piv)
            scale = scale * (1.5 - 0.5 * piv * scale * scale)
            r[h] = r[h] * scale
            n[h] = n[h] * scale
        for t in range(4):
            n_ref[pl.ds(k0 + 8 * t, 8), :] = n[t]

        @pl.when(b < 3)
        def _():
            rows = jnp.concatenate(r, axis=0)
            later = jnp.where(lane >= k0 + 32, rows, 0.0)
            both = jnp.concatenate([rows, jnp.concatenate(n, axis=0)], axis=1)
            lh = later.astype(BF).astype(F32)
            bh = both.astype(BF).astype(F32)
            left = jnp.concatenate([lh, lh, later - lh], axis=0).astype(BF)
            right = jnp.concatenate([bh, both - bh, bh], axis=0).astype(BF)
            change = lax.dot_general(left, right, TN, preferred_element_type=F32)
            s_ref[...] = s_ref[...] - change[:, :BW]
            n_ref[...] = n_ref[...] - change[:, BW:]

        return carry

    lax.fori_loop(0, 4, panel, 0)

def chol_inverse_2(s_ref, linv_ref, t_ref, n_ref):
    t_ref[...] = s_ref[:BW, :BW]
    chol_inverse(t_ref, n_ref)
    n1 = n_ref[...]
    n1h = halves(n1)
    low = mm(s_ref[BW:, :BW], n1h, NT)
    lowh = halves(low)
    t_ref[...] = s_ref[BW:, BW:] - mm(lowh, lowh, NT)
    cross = mm(lowh, n1h, NN)
    chol_inverse(t_ref, n_ref)
    n2 = n_ref[...]
    linv_ref[:BW, :BW] = n1
    linv_ref[:BW, BW:] = jnp.zeros((BW, BW), F32)
    linv_ref[BW:, :BW] = -mm(n2, cross, NN)
    linv_ref[BW:, BW:] = n2


def times_dyn_t(x_ref, pat, rows, e):
    out = []
    for c in range(NB):
        xs = jnp.concatenate([x_ref[pat[k, e, c]] for k in range(3)], axis=1)
        out.append(mm(xs, rows(c), NT))
    return out


def dyn_times(z_ref, pat, rows, e, c):
    zs = jnp.concatenate([z_ref[pat[k, e, c]].reshape(BW, PAN) for k in range(3)], axis=0)
    return mm(rows(c), zs, NN)


def is_block(found, block):
    return (found == block).astype(F32)


def put_blocks(ref, x):
    for d in range(NB):
        ref[d] = x[:, d * BW : (d + 1) * BW]


def pack(y):
    return [
        jnp.concatenate([y[s * 8 : s * 8 + 8, q * PAN : q * PAN + PAN] for s in range(4)], axis=1)
        for q in range(GROUP)
    ]


def unpack(rec_ref, z_ref):
    for s in range(4):
        part = rec_ref[:, :, s * PAN : s * PAN + PAN]
        z_ref[:, :, s * 8 : s * 8 + 8, :] = part.reshape(NB, 4, 8, PAN)


def factor_rows(blk, mat):
    at = jnp.broadcast_to(blk.astype(F32), (BW, BW)).T
    out = []
    for d in range(NB):
        before = (d + NB - 1) % NB
        out.append(jnp.where(at == d, mat[:, :BW], 0.0) + jnp.where(at == before, mat[:, BW:], 0.0))
    return out


class Gather:
    def __init__(self, place, src, buf, send, recv, swapped):
        tm, row, obs = place
        x, core = row // 2, lax.rem(row, 2)
        self.core, self.buf, self.src = core, buf, src
        self.i, self.j = (obs, x) if swapped else (x, obs)
        self.send, self.recv = send, recv

        def device(i, j, c):
            xx, yy = (j, i) if swapped else (i, j)
            return (tm, 2 * xx + c, yy)

        self.device = device

    def copy(self, src, dst, n, device):
        return pltpu.make_async_remote_copy(
            src_ref=src, dst_ref=dst, send_sem=self.send.at[n], recv_sem=self.recv.at[n],
            device_id=device, device_id_type=MESH,
        )

    def first(self, d):
        piece = self.buf.at[self.core, self.i, self.j]
        j = lax.rem(self.j + d, SIDE)
        return self.copy(self.src if self.src is not None else piece, piece, d - 1, self.device(self.i, j, self.core))

    def second(self, d):
        block = self.buf.at[self.core, self.i]
        i = lax.rem(self.i + d, SIDE)
        return self.copy(block, block, 2 + d, self.device(i, self.j, self.core))

    def across(self, d):
        block = self.buf.at[self.core, lax.rem(self.i + SIDE - d, SIDE)]
        return self.copy(block, block, 6 + d, self.device(self.i, self.j, 1 - self.core))

    def phase1(self):
        for d in range(1, SIDE):
            self.first(d).start()

    def phase2(self):
        for d in range(1, SIDE):
            self.first(d).wait_recv()
        for d in range(1, SIDE):
            self.second(d).start()
        self.across(0).start()

    def phase3(self):
        for d in range(1, SIDE):
            self.second(d).wait_recv()
            self.across(d).start()

    def finish(self):
        for d in range(SIDE):
            self.across(d).wait_recv()

    def drain(self):
        for d in range(1, SIDE):
            self.first(d).wait_send()
            self.second(d).wait_send()
        for d in range(SIDE):
            self.across(d).wait_send()


class Swap:
    def __init__(self, place, src, dst, send, recv, own):
        self.tm, row, obs = place
        self.me = row * SIDE + obs
        self.src, self.dst, self.send, self.recv, self.own = src, dst, send, recv, own
        self.low = 0 if own is None else 1

    def copy(self, off):
        t = lax.rem(self.me + off, GROUP)
        return pltpu.make_async_remote_copy(
            src_ref=self.src.at[t], dst_ref=self.dst.at[self.me],
            send_sem=self.send.at[off], recv_sem=self.recv.at[off],
            device_id=(self.tm, t // SIDE, lax.rem(t, SIDE)), device_id_type=MESH,
        )

    def mine(self):
        return pltpu.make_async_copy(self.src.at[self.me], self.dst.at[self.me], self.own)

    def start(self):
        def begin(off, carry):
            self.copy(off).start()
            return carry

        lax.fori_loop(self.low, GROUP, begin, 0)
        if self.low:
            self.mine().start()

    def finish(self):
        def end(off, carry):
            self.copy(off).wait_recv()
            return carry

        if self.low:
            self.mine().wait()
        lax.fori_loop(self.low, GROUP, end, 0)

    def drain(self):
        def end(off, carry):
            self.copy(off).wait_send()
            return carry

        lax.fori_loop(self.low, GROUP, end, 0)


def kernel(
    pat, vals, offs_h, cov, blk_h, omat, odat_h,
    out_dyn, out_off, out_cov, out_fac, out_info,
    cov_v, obs_v, vi, vj, ga, gb, phi, s1, t1, n1, linv_v, s2, linv2_v,
    g_v, k_v, u_v, o_v, xt, pk, rec, lamt, lamt_a, bz, ba, c_pan, ca, g2a, g2b, g2_v,
    pk2, rec2, pkl, recl, fac2, c2, vec, vec_in, lam, fac, z1, z2, kb_v, offs, blk, odat,
    obs_s, obs_r, gat_s, gat_r, swap_s, swap_r, z_s, z_r, own,
):
    tm, row, obs = lax.axis_index("tm"), lax.axis_index("row"), lax.axis_index("obs")
    place = (tm, row, obs)
    x, core = row // 2, lax.rem(row, 2)
    me = row * SIDE + obs
    row0 = pl.multiple_of(me * PAN, PAN)
    lo = pl.multiple_of(obs * PAN, PAN)
    odd = lax.rem(tm, 2) == 1
    up = (lax.rem(tm + 1, TM_DEV), row, obs)
    down = (lax.rem(tm + TM_DEV - 1, TM_DEV), row, obs)

    def rows_i(c):
        return vi[c % 2, c // 2].reshape(BW, 3 * BW)

    def rows_j(c):
        return vj[c % 2, :, c // 2].reshape(BW, 3 * BW)

    def obs_copy(e, d):
        return pltpu.make_async_remote_copy(
            src_ref=omat.at[e], dst_ref=obs_v.at[e, obs], send_sem=obs_s.at[e, d - 1], recv_sem=obs_r.at[e, d - 1],
            device_id=(tm, row, lax.rem(obs + d, SIDE)), device_id_type=MESH,
        )

    def z_copy(n, src, dst, device):
        return pltpu.make_async_remote_copy(
            src_ref=src, dst_ref=dst, send_sem=z_s.at[n], recv_sem=z_r.at[n], device_id=device, device_id_type=MESH
        )

    gather_i = Gather(place, vals.at[0], vi, gat_s.at[0], gat_r.at[0], False)
    gather_j = Gather(place, vals.at[1], vj, gat_s.at[1], gat_r.at[1], True)
    gather_ga = Gather(place, None, ga, gat_s.at[2], gat_r.at[2], False)
    gather_gb = Gather(place, None, gb, gat_s.at[3], gat_r.at[3], True)
    gather_2a = Gather(place, None, g2a, gat_s.at[4], gat_r.at[4], False)
    gather_2b = Gather(place, None, g2b, gat_s.at[5], gat_r.at[5], True)
    swap1 = Swap(place, pk, rec, swap_s.at[0], swap_r.at[0], own.at[4])
    swap2 = Swap(place, pk2, rec2, swap_s.at[1], swap_r.at[1], own.at[5])
    swap3 = Swap(down, pkl, recl, swap_s.at[2], swap_r.at[2], None)
    up_lam = z_copy(0, lamt, lamt_a, up)
    up_b = z_copy(1, bz, ba, up)
    def chunk(n):
        return pl.ds(n * CHUNK, CHUNK)

    up_cov = [z_copy(8 + n, c_pan.at[:, chunk(n)], ca.at[:, chunk(n)], up) for n in range(ST // CHUNK)]
    down_cov = [
        z_copy(4 + n, c2.at[:, chunk(n)], out_cov.at[0, :, chunk(n)], down) for n in range(ST // CHUNK)
    ]
    down_fac = z_copy(2, fac2, out_fac.at[0, :, 0 : 2 * BW], down)
    down_vec = z_copy(3, vec, vec_in, down)

    local_cov = pltpu.make_async_copy(cov, cov_v, own.at[0])
    local_i = pltpu.make_async_copy(vals.at[0], vi.at[core, x, obs], own.at[1])
    local_j = pltpu.make_async_copy(vals.at[1], vj.at[core, obs, x], own.at[2])
    local_obs = pltpu.make_async_copy(omat, obs_v.at[:, obs], own.at[3])
    tiny = [
        pltpu.make_async_copy(a, b, own.at[9 + n])
        for n, (a, b) in enumerate([(offs_h, offs), (odat_h, odat), (blk_h, blk)])
    ]
    local_obs.start()
    for one in tiny:
        one.start()
    local_cov.start()
    local_i.start()
    local_j.start()

    barrier = pltpu.get_barrier_semaphore()

    partners = [(tm, row, lax.rem(obs + d, SIDE)) for d in range(1, SIDE)]
    partners += [(tm, 2 * lax.rem(x + d, SIDE) + core, obs) for d in range(1, SIDE)]
    partners += [(tm, 2 * x + 1 - core, obs), up, down]
    for partner in partners:
        pl.semaphore_signal(barrier, inc=1, device_id=partner, device_id_type=MESH)
    pl.semaphore_wait(barrier, len(partners))

    for d in range(1, SIDE):
        obs_copy(1, d).start()
    for d in range(1, SIDE):
        obs_copy(0, d).start()
    gather_i.phase1()
    gather_j.phase1()

    local_obs.wait()
    for one in tiny:
        one.wait()
    for d in range(1, SIDE):
        obs_copy(1, d).wait_recv()
    for d, part in enumerate(factor_rows(blk[1:2, :], obs_v[1].reshape(BW, 2 * BW))):
        phi[1, :, d * BW : (d + 1) * BW] = part
    local_cov.wait()
    gain = mm(cov_v[0], phi[1], NT)
    ga[core, x, obs] = gain[0:16]
    small = jnp.concatenate([offs[...], odat[...]], axis=0)
    gb[core, obs, x, 0:16] = gain[16:32]
    gb[core, obs, x, 16:24] = jnp.zeros((8, BW), F32)
    gb[core, obs, x, 16:20, 0:PAN] = small
    gather_ga.phase1()
    gather_gb.phase1()
    gather_ga.phase2()
    gather_gb.phase2()
    local_i.wait()
    local_j.wait()
    gather_i.phase2()
    gather_j.phase2()
    gather_ga.phase3()
    gather_gb.phase3()
    for d in range(1, SIDE):
        obs_copy(0, d).wait_recv()
    for d, part in enumerate(factor_rows(blk[0:1, :], obs_v[0].reshape(BW, 2 * BW))):
        phi[0, :, d * BW : (d + 1) * BW] = part
    gather_ga.finish()
    gather_gb.finish()

    vecs = []
    for c in range(NB):
        both = jnp.concatenate([ga[c % 2, c // 2], gb[c % 2, :, c // 2, 0:16]], axis=1)
        g_v[c * BW : (c + 1) * BW, :] = both.reshape(BW, BW)
        vecs.append(jnp.concatenate([gb[c % 2, o, c // 2, 16:24, 0:PAN] for o in range(SIDE)], axis=1))
    zeta_i = jnp.broadcast_to(vecs[0][2:3, :], (8, BW))
    zeta_j = jnp.broadcast_to(vecs[0][3:4, :], (8, BW))
    b_i = jnp.concatenate([jnp.broadcast_to(v[0:1, :], (8, BW)) for v in vecs], axis=1)
    b_j = jnp.concatenate([jnp.broadcast_to(v[1:2, :], (8, BW)) for v in vecs], axis=1)
    g = halves(g_v[...])
    phi_j = halves(phi[1])
    s1[...] = eye(BW) + mm(phi_j, g, NN)
    chol_inverse(s1, linv_v)
    linv = halves(linv_v[...])
    k = mm(g, linv, NT)
    k_v[...] = k
    for c in range(NB):
        kb_v[c] = k[c * BW : (c + 1) * BW, :]
    kh = halves(k)
    p = cov_v[0] - mm(k_v[pl.ds(row0, PAN), :], kh, NT)
    solved = mm(zeta_j - mm(b_i, phi_j, NT), linv, NT)
    xrow = b_i + mm(solved, kh, NT)
    gather_i.phase3()
    gather_j.phase3()
    gather_i.finish()

    for c in range(NB):
        t = mm(phi[1, :, c * BW : (c + 1) * BW], rows_i(c), NN)
        for d in range(NB):
            part = jnp.zeros((BW, BW), F32) if c == 0 else o_v[d]
            for n in range(3):
                part = part + is_block(pat[n, 0, c], d) * t[:, n * BW : (n + 1) * BW]
            o_v[d] = part
    for d in range(NB):
        u_v[d] = mm(linv, o_v[d], NN)
    t1[...] = u_v[row].T
    upper = t1[pl.ds(lo, PAN), :]
    drop = mm(upper, kh, NT)
    for c in range(NB):
        rows = rows_i(c)
        w = jnp.zeros((BW, BW), F32)
        for n in range(3):
            w = w + is_block(pat[n, 0, c], row) * rows[:, n * BW : (n + 1) * BW]
        t1[...] = w.T
        sl = slice(c * BW, (c + 1) * BW)
        xt[c] = jnp.concatenate([p[:, sl], t1[pl.ds(lo, PAN), :] - drop[:, sl], xrow[:, sl]], axis=0)
    gather_j.finish()
    y = jnp.concatenate(times_dyn_t(xt, pat, rows_j, 1), axis=1)
    for q, part in enumerate(pack(y[:PAN, :])):
        pk[q] = part
    swap1.start()
    lamt[...] = y[PAN : 2 * PAN, :]
    b_own = y[2 * PAN :, :] + b_j
    bz[...] = b_own

    @pl.when(jnp.logical_not(odd))
    def _():
        up_lam.start()
        up_b.start()

    for d in range(NB):
        o_v[d] = phi[0, :, d * BW : (d + 1) * BW]
    t1[...] = o_v[row].T
    prior = t1[pl.ds(lo, PAN), :]
    fac[:, :BW] = upper
    fac[:, BW : 2 * BW] = prior
    fac[:, 2 * BW :] = jnp.zeros((PAN, 2 * BW), F32)
    info = mm(solved, upper, NT) + mm(zeta_i, prior, NT)
    swap1.finish()

    def send_up(n):
        @pl.when(jnp.logical_not(odd))
        def _():
            up_cov[n].start()

    unpack(rec, z1)
    for c in range(NB):
        sl = slice(c * BW, (c + 1) * BW)
        c_pan[:, sl] = dyn_times(z1, pat, rows_j, 1, c).T + cov_v[1, :, sl]
        if c % 2 == 1:
            send_up(c // 2)

    def my_panel(full):
        put_blocks(o_v.at[:, 0:8, :], full)
        block = o_v[row, 0:8, :]
        return pltpu.roll(block, lax.rem(BW - lo, BW), 1)[0:1, 0:PAN]

    @pl.when(jnp.logical_not(odd))
    def _():
        pieces = pltpu.make_async_copy(fac.at[:, 0 : 2 * BW], out_fac.at[0, :, 2 * BW :], own.at[6])
        pieces.start()
        pieces.wait()
        down_vec.wait_recv()
        out_off[...] = vec_in[0:1, 0:PAN]
        out_info[...] = info[0:1, :] + vec_in[1:2, 0:PAN]
        swap3.finish()
        unpack(recl, z1)
        for c in range(NB):
            lam[:, c * BW : (c + 1) * BW] = z1[c].reshape(BW, PAN).T
        dyn_out = pltpu.make_async_copy(lam, out_dyn.at[0], own.at[8])
        dyn_out.start()
        dyn_out.wait()
        for one in down_cov:
            one.wait_recv()
        down_fac.wait_recv()
        up_lam.wait_send()
        up_b.wait_send()
        for one in up_cov:
            one.wait_send()

    @pl.when(odd)
    def _():
        out_off[...] = my_panel(b_own)
        out_info[...] = info[0:1, :]
        ones = [
            pltpu.make_async_copy(c_pan, out_cov.at[0], own.at[6]),
            pltpu.make_async_copy(fac, out_fac.at[0], own.at[7]),
        ]
        for one in ones:
            one.start()
        up_lam.wait_recv()
        up_b.wait_recv()
        lam_parts = [jnp.zeros((PAN, BW), F32) for _ in range(NB)]
        ak = jnp.zeros((PAN, BW), F32)
        for n in range(3):
            b = pat[n, 1, row]
            block = vj[core, obs, x, :, n * BW : (n + 1) * BW]
            mine = halves(block)
            t = mm(mine, vi[lax.rem(b, 2), lax.div(b, 2)].reshape(BW, 3 * BW), NN)
            for m in range(3):
                at = pat[m, 0, b]
                for d in range(NB):
                    lam_parts[d] = lam_parts[d] + is_block(at, d) * t[:, m * BW : (m + 1) * BW]
            ak = ak + mm(mine, kb_v[b], NN)
        akh = halves(ak)
        for d in range(NB):
            lam[:, d * BW : (d + 1) * BW] = lam_parts[d] - mm(akh, u_v[d], NN)
        dyn_out = pltpu.make_async_copy(lam, out_dyn.at[0], own.at[8])
        dyn_out.start()

        u = jnp.concatenate([u_v[d] for d in range(NB)], axis=1)
        phi_b = halves(jnp.concatenate([u, phi[0]], axis=0))
        gain2 = jnp.zeros((PAN, 2 * BW), F32)
        for n in range(ST // CHUNK):
            up_cov[n].wait_recv()
            part = tuple(h[:, n * CHUNK : (n + 1) * CHUNK] for h in phi_b)
            gain2 = gain2 + mm(ca[:, chunk(n)], part, NT)
        g2a[core, x, obs] = gain2[:, :BW]
        g2b[core, obs, x] = gain2[:, BW:]
        gather_2a.phase1()
        gather_2b.phase1()
        la, bp = lamt_a[...], ba[...]
        start = jnp.concatenate([ca[...], la, bp], axis=0)
        across = mm(start[PAN:], phi_b, NT)
        seen = across[:PAN]
        resid = jnp.concatenate([solved, zeta_i], axis=1) - across[PAN:]
        gather_2a.phase2()
        gather_2b.phase2()
        gather_2a.phase3()
        gather_2b.phase3()
        gather_2a.finish()
        gather_2b.finish()
        for c in range(NB):
            g2_v[c * BW : (c + 1) * BW, :BW] = g2a[c % 2, c // 2].reshape(BW, BW)
            g2_v[c * BW : (c + 1) * BW, BW:] = g2b[c % 2, :, c // 2].reshape(BW, BW)
        g2 = halves(g2_v[...])
        s2[...] = eye(2 * BW) + mm(phi_b, g2, NN)
        chol_inverse_2(s2, linv2_v, t1, n1)
        linv2 = halves(linv2_v[...])
        ahead = mm(jnp.concatenate([g2_v[pl.ds(row0, PAN), :], seen, resid], axis=0), linv2, NT)
        fac2[...] = ahead[PAN : 2 * PAN]
        down_fac.start()
        solved2 = ahead[2 * PAN :]
        sign = jnp.where(lax.broadcasted_iota(jnp.int32, (2 * PAN + 8, 1), 0) < 2 * PAN, -1.0, 1.0)
        xs = start + mm(sign * mm(ahead, linv2, NN), g2, NT)
        put_blocks(xt, xs)
        h = jnp.concatenate(times_dyn_t(xt, pat, rows_i, 0), axis=1)
        put_blocks(xt, h - mm(mm(xs, u, NT), k_v[...], NT))
        y2 = jnp.concatenate(times_dyn_t(xt, pat, rows_j, 1), axis=1)
        for q, part in enumerate(pack(y2[:PAN, :])):
            pk2[q] = part
        swap2.start()
        for q, part in enumerate(pack(y2[PAN : 2 * PAN, :])):
            pkl[q] = part
        swap3.start()
        vec[...] = jnp.zeros((8, BW), F32)
        vec[0:1, 0:PAN] = my_panel(y2[2 * PAN :, :] + b_own)
        vec[1:2, 0:PAN] = mm(solved2, fac2[...], NT)[0:1, :]
        down_vec.start()
        swap2.finish()
        unpack(rec2, z1)
        uz = jnp.zeros((BW, PAN), F32)
        for d in range(NB):
            uz = uz + mm(u_v[d], z1[d].reshape(BW, PAN), NN)
        kz = mm(k_v[...], uz, NN)
        for c in range(NB):
            part = dyn_times(z1, pat, rows_i, 0, c) - kz[c * BW : (c + 1) * BW, :]
            z2[c] = part.reshape(4, PAN, PAN)
        for c in range(NB):
            sl = slice(c * BW, (c + 1) * BW)
            c2[:, sl] = dyn_times(z2, pat, rows_j, 1, c).T + c_pan[:, sl]
            if c % 2 == 1:
                down_cov[c // 2].start()
        for one in ones:
            one.wait()
        dyn_out.wait()
        gather_2a.drain()
        gather_2b.drain()
        swap2.drain()
        swap3.drain()
        for one in [down_fac, down_vec] + down_cov:
            one.wait_send()

    for e in range(2):
        for d in range(1, SIDE):
            obs_copy(e, d).wait_send()
    for one in (gather_i, gather_j, gather_ga, gather_gb):
        one.drain()
    swap1.drain()


def vmem(*shape):
    return pltpu.VMEM(shape, F32)


def dma(*shape):
    return pltpu.SemaphoreType.DMA(shape)


SCRATCH = [
    vmem(2, PAN, ST), vmem(2, SIDE, PAN, 2 * BW),
    vmem(2, SIDE, SIDE, PAN, 3 * BW), vmem(2, SIDE, SIDE, PAN, 3 * BW),
    vmem(2, SIDE, SIDE, 16, BW), vmem(2, SIDE, SIDE, 24, BW),
    vmem(2, BW, ST),
    vmem(BW, BW), vmem(BW, BW), vmem(BW, BW), vmem(BW, BW),
    vmem(2 * BW, 2 * BW), vmem(2 * BW, 2 * BW),
    vmem(ST, BW), vmem(ST, BW), vmem(NB, BW, BW), vmem(NB, BW, BW), vmem(NB, 2 * PAN + 8, BW),
    vmem(GROUP, 8, BW), vmem(GROUP, 8, BW),
    vmem(PAN, ST), vmem(PAN, ST), vmem(8, ST), vmem(8, ST), vmem(PAN, ST), vmem(PAN, ST),
    vmem(2, SIDE, SIDE, PAN, BW), vmem(2, SIDE, SIDE, PAN, BW),
    vmem(ST, 2 * BW),
    vmem(GROUP, 8, BW), vmem(GROUP, 8, BW), vmem(GROUP, 8, BW), vmem(GROUP, 8, BW),
    vmem(PAN, 2 * BW), vmem(PAN, ST), vmem(8, BW), vmem(8, BW),
    vmem(PAN, ST), vmem(PAN, 4 * BW),
    vmem(NB, 4, PAN, PAN), vmem(NB, 4, PAN, PAN), vmem(NB, BW, BW),
    vmem(2, PAN), pltpu.VMEM((2, BW), jnp.int32), vmem(2, PAN),
    dma(2, 3), dma(2, 3), dma(6, 10), dma(6, 10), dma(3, GROUP), dma(3, GROUP), dma(12), dma(12), dma(12),
]


def place_body(*refs):
    n = len(refs) // 2
    sems = refs[-1]
    copies = [pltpu.make_async_copy(refs[i], refs[n + i], sems.at[i]) for i in range(n)]
    for one in copies:
        one.start()
    for one in copies:
        one.wait()


def per_device(dyn_pattern, *rest):
    outs = [(1, PAN, ST), (1, PAN), (1, PAN, ST), (1, PAN, 4 * BW), (1, PAN)]
    found = pl.pallas_call(
        kernel,
        out_shape=[jax.ShapeDtypeStruct(s, F32) for s in outs],
        in_specs=[SM] + [ANY] * 6,
        out_specs=[ANY, VM, ANY, ANY, VM],
        scratch_shapes=SCRATCH,
        compiler_params=pltpu.CompilerParams(
            collective_id=0, has_side_effects=True, vmem_limit_bytes=60 << 20
        ),
    )(jnp.transpose(dyn_pattern, (2, 0, 1)), *rest)
    return pl.pallas_call(
        place_body,
        out_shape=[jax.ShapeDtypeStruct(s, F32) for s in outs],
        in_specs=[VM] * len(outs),
        out_specs=[ANY] * len(outs),
        scratch_shapes=[dma(len(outs))],
    )(*found)


def solution(mesh):
    placed = (
        P("tm", None, None),
        P("tm", ("row", "obs"), None),
        P("tm", ("row", "obs")),
        P("tm", ("row", "obs"), None),
        P("tm", None),
        P("tm", "obs", None),
        P("tm", "obs"),
    )
    return jax.shard_map(
        per_device,
        mesh=mesh,
        in_specs=placed,
        out_specs=(
            P("tm", ("row", "obs"), None),
            P("tm", ("row", "obs")),
            P("tm", ("row", "obs"), None),
            P("tm", ("row", "obs"), None),
            P("tm", ("row", "obs")),
        ),
        check_vma=False,
    )
```

```python
import functools

import jax
import jax.numpy as jnp
from jax import lax
from jax.experimental import pallas as pl
from jax.experimental.pallas import tpu as pltpu
from jax.sharding import PartitionSpec as P

F32 = jnp.float32
BF = jnp.bfloat16
NN = (((1,), (0,)), ((), ()))
NT = (((1,), (1,)), ((), ()))
TN = (((0,), (0,)), ((), ()))
MESH = pl.DeviceIdType.MESH
VM = pl.BlockSpec(memory_space=pltpu.VMEM)
SM = pl.BlockSpec(memory_space=pltpu.SMEM)
ANY = pl.BlockSpec(memory_space=pl.ANY)
NB = 8
BW = 128
ST = NB * BW
GROUP = 32
SIDE = 4
TM_DEV = 8
PAN = 32
CHUNK = 256


def halves(x):
    hi = x.astype(BF)
    return hi, (x - hi.astype(F32)).astype(BF)
def mm(a, b, dims):
    ah, al = a if isinstance(a, tuple) else halves(a)
    bh, bl = b if isinstance(b, tuple) else halves(b)
    d = functools.partial(lax.dot_general, dimension_numbers=dims, preferred_element_type=F32)
    return d(ah, bh) + (d(ah, bl) + d(al, bh))
def eye(n):
    rows = lax.broadcasted_iota(jnp.int32, (n, n), 0)
    cols = lax.broadcasted_iota(jnp.int32, (n, n), 1)
    return jnp.where(rows == cols, 1.0, 0.0).astype(F32)


def chol_inverse(s_ref, n_ref):
    n_ref[...] = eye(BW)
    sub = lax.broadcasted_iota(jnp.int32, (8, BW), 0)
    lane = lax.broadcasted_iota(jnp.int32, (32, BW), 1)

    def panel(b, carry):
        k0 = pl.multiple_of(b * 32, 32)
        r = [s_ref[pl.ds(k0 + 8 * t, 8), :] for t in range(4)]
        n = [n_ref[pl.ds(k0 + 8 * t, 8), :] for t in range(4)]
        a = [pltpu.roll(x, lax.rem(BW - k0, BW), 1) for x in r]
        for h in range(4):
            c = {t: [jnp.broadcast_to(a[t][:, 8 * h + j : 8 * h + j + 1], (8, BW)) for j in range(8)] for t in range(h, 4)}
            piv = jnp.ones((8, BW), F32)
            for j in range(8):
                p = jnp.broadcast_to(c[h][j][j : j + 1, :], (8, BW))
                inv = 1.0 / p
                piv = jnp.where(sub == j, p, piv)
                own = [c[h][m][j : j + 1, :] for m in range(8)]
                ra, rr, rn = a[h][j : j + 1, :], r[h][j : j + 1, :], n[h][j : j + 1, :]
                for t in range(h, 4):
                    f = c[t][j] * inv
                    if t == h:
                        f = jnp.where(sub > j, f, 0.0)
                    for m in range(j + 1, 8):
                        c[t][m] = c[t][m] - f * own[m]
                    if h < 3:
                        a[t] = a[t] - f * ra
                    r[t] = r[t] - f * rr
                    n[t] = n[t] - f * rn
            scale = lax.rsqrt(piv)
            scale = scale * (1.5 - 0.5 * piv * scale * scale)
            r[h] = r[h] * scale
            n[h] = n[h] * scale
        for t in range(4):
            n_ref[pl.ds(k0 + 8 * t, 8), :] = n[t]

        @pl.when(b < 3)
        def _():
            rows = jnp.concatenate(r, axis=0)
            later = jnp.where(lane >= k0 + 32, rows, 0.0)
            both = jnp.concatenate([rows, jnp.concatenate(n, axis=0)], axis=1)
            lh = later.astype(BF).astype(F32)
            bh = both.astype(BF).astype(F32)
            left = jnp.concatenate([lh, lh, later - lh], axis=0).astype(BF)
            right = jnp.concatenate([bh, both - bh, bh], axis=0).astype(BF)
            change = lax.dot_general(left, right, TN, preferred_element_type=F32)
            s_ref[...] = s_ref[...] - change[:, :BW]
            n_ref[...] = n_ref[...] - change[:, BW:]

        return carry

    lax.fori_loop(0, 4, panel, 0)

def chol_inverse_2(s_ref, linv_ref, t_ref, n_ref):
    t_ref[...] = s_ref[:BW, :BW]
    chol_inverse(t_ref, n_ref)
    n1 = n_ref[...]
    n1h = halves(n1)
    low = mm(s_ref[BW:, :BW], n1h, NT)
    lowh = halves(low)
    t_ref[...] = s_ref[BW:, BW:] - mm(lowh, lowh, NT)
    cross = mm(lowh, n1h, NN)
    chol_inverse(t_ref, n_ref)
    n2 = n_ref[...]
    linv_ref[:BW, :BW] = n1
    linv_ref[:BW, BW:] = jnp.zeros((BW, BW), F32)
    linv_ref[BW:, :BW] = -mm(n2, cross, NN)
    linv_ref[BW:, BW:] = n2


def times_dyn_t(x_ref, pat, rows, e):
    out = []
    for c in range(NB):
        xs = jnp.concatenate([x_ref[pat[k, e, c]] for k in range(3)], axis=1)
        out.append(mm(xs, rows(c), NT))
    return out


def dyn_times(z_ref, pat, rows, e, c):
    zs = jnp.concatenate([z_ref[pat[k, e, c]].reshape(BW, PAN) for k in range(3)], axis=0)
    return mm(rows(c), zs, NN)


def is_block(found, block):
    return (found == block).astype(F32)


def put_blocks(ref, x):
    for d in range(NB):
        ref[d] = x[:, d * BW : (d + 1) * BW]


def pack(y):
    return [
        jnp.concatenate([y[s * 8 : s * 8 + 8, q * PAN : q * PAN + PAN] for s in range(4)], axis=1)
        for q in range(GROUP)
    ]


def unpack(rec_ref, z_ref):
    for s in range(4):
        part = rec_ref[:, :, s * PAN : s * PAN + PAN]
        z_ref[:, :, s * 8 : s * 8 + 8, :] = part.reshape(NB, 4, 8, PAN)


def factor_rows(blk, mat):
    at = jnp.broadcast_to(blk.astype(F32), (BW, BW)).T
    out = []
    for d in range(NB):
        before = (d + NB - 1) % NB
        out.append(jnp.where(at == d, mat[:, :BW], 0.0) + jnp.where(at == before, mat[:, BW:], 0.0))
    return out


class Gather:
    def __init__(self, place, src, buf, send, recv, swapped, ring=False):
        tm, row, obs = place
        x, core = row // 2, lax.rem(row, 2)
        self.core, self.buf, self.src = core, buf, src
        self.i, self.j = (obs, x) if swapped else (x, obs)
        self.send, self.recv, self.ring = send, recv, ring
        self.direct = (1, 3) if ring else (1, 2, 3)

        def device(i, j, c):
            xx, yy = (j, i) if swapped else (i, j)
            return (tm, 2 * xx + c, yy)

        self.device = device

    def copy(self, src, dst, n, device):
        return pltpu.make_async_remote_copy(
            src_ref=src, dst_ref=dst, send_sem=self.send.at[n], recv_sem=self.recv.at[n],
            device_id=device, device_id_type=MESH,
        )

    def first(self, d):
        piece = self.buf.at[self.core, self.i, self.j]
        j = lax.rem(self.j + d, SIDE)
        return self.copy(self.src if self.src is not None else piece, piece, d - 1, self.device(self.i, j, self.core))

    def second(self, d):
        block = self.buf.at[self.core, self.i]
        i = lax.rem(self.i + d, SIDE)
        return self.copy(block, block, 2 + d, self.device(i, self.j, self.core))

    def across(self, d):
        block = self.buf.at[self.core, lax.rem(self.i + SIDE - d, SIDE)]
        return self.copy(block, block, 6 + d, self.device(self.i, self.j, 1 - self.core))

    def phase1(self):
        for d in range(1, SIDE):
            self.first(d).start()

    def phase2(self):
        for d in range(1, SIDE):
            self.first(d).wait_recv()
        for d in self.direct:
            self.second(d).start()
        self.across(0).start()

    def onward(self, d):
        half = pl.ds(0, SIDE // 2) if d == 1 else pl.ds(SIDE // 2, SIDE // 2)
        part = self.buf.at[self.core, lax.rem(self.i + SIDE - d, SIDE), half]
        return self.copy(part, part, 4 if d == 1 else 10, self.device(lax.rem(self.i + d, SIDE), self.j, self.core))

    def pass_on(self):
        for d in (1, 3):
            self.second(d).wait_recv()
            self.onward(d).start()
        for d in (1, 3):
            self.across(d).start()

    def phase3(self):
        if self.ring:
            for d in (1, 3):
                self.onward(d).wait_recv()
            self.across(2).start()
            return
        for d in self.direct:
            self.second(d).wait_recv()
            self.across(d).start()

    def finish(self):
        for d in range(SIDE):
            self.across(d).wait_recv()

    def drain(self):
        for d in range(1, SIDE):
            self.first(d).wait_send()
        for d in self.direct:
            self.second(d).wait_send()
        if self.ring:
            for d in (1, 3):
                self.onward(d).wait_send()
        for d in range(SIDE):
            self.across(d).wait_send()


class Swap:
    def __init__(self, place, src, dst, sem, n, own):
        self.tm, row, obs = place
        self.me = row * SIDE + obs
        self.src, self.dst, self.own = src, dst, own
        self.send, self.recv = sem.at[2 * n], sem.at[2 * n + 1]
        self.rows = [lax.rem(row + d, NB) for d in range(NB)]
        self.cols = [lax.rem(obs + d, SIDE) for d in range(SIDE)]

    def start(self):
        for dr in range(NB):
            for do in range(SIDE):
                if dr + do > 0:
                    r, o = self.rows[dr], self.cols[do]
                    pltpu.make_async_remote_copy(
                        src_ref=self.src.at[r * SIDE + o], dst_ref=self.dst.at[self.me],
                        send_sem=self.send, recv_sem=self.recv,
                        device_id=(self.tm, r, o), device_id_type=MESH,
                    ).start()
        self.mine().start()

    def mine(self):
        return pltpu.make_async_copy(self.src.at[self.me], self.dst.at[self.me], self.own)

    def total(self):
        blocks = pl.ds(0, GROUP - 1)
        return pltpu.make_async_remote_copy(
            src_ref=self.src.at[blocks], dst_ref=self.dst.at[blocks],
            send_sem=self.send, recv_sem=self.recv,
            device_id=(self.tm, self.rows[1], self.cols[0]), device_id_type=MESH,
        )

    def finish(self):
        self.mine().wait()
        self.total().wait_recv()

    def drain(self):
        self.total().wait_send()


def kernel(
    pat, vals, offs_h, cov, blk_h, omat, odat_h,
    out_dyn, out_off, out_cov, out_fac, out_info,
    cov_v, obs_v, vi, vj, ga, gb, gs, phi, s1, t1, n1, linv_v, s2, linv2_v,
    g_v, k_v, u_v, o_v, xt, pk, rec, lamt, lamt_a, bz, ba, c_pan, ca, g2a, g2b, g2_v,
    pk2, rec2, pkl, recl, lamt2, lamt2_in, fac2, c2, vec, vec_in, lam, fac, z1, z2, kb_v, offs, blk, odat,
    obs_s, obs_r, gat_s, gat_r, swap, z_s, z_r, own,
):
    tm, row, obs = lax.axis_index("tm"), lax.axis_index("row"), lax.axis_index("obs")
    place = (tm, row, obs)
    x, core = row // 2, lax.rem(row, 2)
    me = row * SIDE + obs
    row0 = pl.multiple_of(me * PAN, PAN)
    lo = pl.multiple_of(obs * PAN, PAN)
    odd = lax.rem(tm, 2) == 1
    up = (lax.rem(tm + 1, TM_DEV), row, obs)
    down = (lax.rem(tm + TM_DEV - 1, TM_DEV), row, obs)

    def rows_i(c):
        return vi[c % 2, c // 2].reshape(BW, 3 * BW)

    def rows_j(c):
        return vj[c % 2, :, c // 2].reshape(BW, 3 * BW)

    def obs_copy(e, d):
        return pltpu.make_async_remote_copy(
            src_ref=omat.at[e], dst_ref=obs_v.at[e, obs], send_sem=obs_s.at[e, d - 1], recv_sem=obs_r.at[e, d - 1],
            device_id=(tm, row, lax.rem(obs + d, SIDE)), device_id_type=MESH,
        )

    def z_copy(n, src, dst, device):
        return pltpu.make_async_remote_copy(
            src_ref=src, dst_ref=dst, send_sem=z_s.at[n], recv_sem=z_r.at[n], device_id=device, device_id_type=MESH
        )

    gather_i = Gather(place, vals.at[0], vi, gat_s.at[0], gat_r.at[0], False, True)
    gather_j = Gather(place, vals.at[1], vj, gat_s.at[1], gat_r.at[1], True, True)
    gather_ga = Gather(place, None, ga, gat_s.at[2], gat_r.at[2], False)
    gather_gb = Gather(place, None, gb, gat_s.at[3], gat_r.at[3], True)
    gather_gs = Gather(place, None, gs, gat_s.at[6], gat_r.at[6], False)
    gather_2a = Gather(place, None, g2a, gat_s.at[4], gat_r.at[4], False)
    gather_2b = Gather(place, None, g2b, gat_s.at[5], gat_r.at[5], True)
    swap1 = Swap(place, pk, rec, swap, 0, own.at[4])
    swap2 = Swap(place, pk2, rec2, swap, 1, own.at[5])
    swap3 = Swap(place, pkl, recl, swap, 2, own.at[5])
    up_lam = z_copy(0, lamt, lamt_a, up)
    up_b = z_copy(1, bz, ba, up)
    def chunk(n):
        return pl.ds(n * CHUNK, CHUNK)

    up_cov = [z_copy(8 + n, c_pan.at[:, chunk(n)], ca.at[:, chunk(n)], up) for n in range(ST // CHUNK)]
    down_cov = [
        z_copy(4 + n, c2.at[:, chunk(n)], out_cov.at[0, :, chunk(n)], down) for n in range(ST // CHUNK)
    ]
    down_fac = z_copy(2, fac2, out_fac.at[0, :, 0 : 2 * BW], down)
    down_vec = z_copy(3, vec, vec_in, down)
    down_lam = z_copy(12, lamt2, lamt2_in, down)

    local_cov = pltpu.make_async_copy(cov, cov_v, own.at[0])
    local_i = pltpu.make_async_copy(vals.at[0], vi.at[core, x, obs], own.at[1])
    local_j = pltpu.make_async_copy(vals.at[1], vj.at[core, obs, x], own.at[2])
    local_obs = pltpu.make_async_copy(omat, obs_v.at[:, obs], own.at[3])
    tiny = [
        pltpu.make_async_copy(a, b, own.at[9 + n])
        for n, (a, b) in enumerate([(offs_h, offs), (odat_h, odat), (blk_h, blk)])
    ]
    local_obs.start()
    for one in tiny:
        one.start()
    local_cov.start()
    local_i.start()
    local_j.start()

    barrier = pltpu.get_barrier_semaphore()

    partners = [(tm, row, lax.rem(obs + d, SIDE)) for d in range(1, SIDE)]
    partners += [(tm, 2 * lax.rem(x + d, SIDE) + core, obs) for d in range(1, SIDE)]
    partners += [(tm, 2 * x + 1 - core, obs), up, down]
    for partner in partners:
        pl.semaphore_signal(barrier, inc=1, device_id=partner, device_id_type=MESH)
    pl.semaphore_wait(barrier, len(partners))

    for d in range(1, SIDE):
        obs_copy(1, d).start()
    gather_i.phase1()
    gather_j.phase1()

    local_obs.wait()
    for one in tiny:
        one.wait()
    for d in range(1, SIDE):
        obs_copy(1, d).wait_recv()
    for d, part in enumerate(factor_rows(blk[1:2, :], obs_v[1].reshape(BW, 2 * BW))):
        phi[1, :, d * BW : (d + 1) * BW] = part
    local_cov.wait()
    gain = mm(cov_v[0], phi[1], NT)
    ga[core, x, obs] = gain[0:16]
    small = jnp.concatenate([offs[...], odat[...]], axis=0)
    gb[core, obs, x] = gain[16:32]
    gs[core, x, obs] = jnp.zeros((8, BW), F32)
    gs[core, x, obs, 0:4, 0:PAN] = small
    gather_ga.phase1()
    gather_gb.phase1()
    for d in range(1, SIDE):
        obs_copy(0, d).start()
    gather_gs.phase1()
    gather_ga.phase2()
    gather_gb.phase2()
    local_i.wait()
    local_j.wait()
    gather_i.phase2()
    gather_j.phase2()
    gather_gs.phase2()
    gather_ga.phase3()
    gather_gb.phase3()
    for d in range(1, SIDE):
        obs_copy(0, d).wait_recv()
    for d, part in enumerate(factor_rows(blk[0:1, :], obs_v[0].reshape(BW, 2 * BW))):
        phi[0, :, d * BW : (d + 1) * BW] = part
    gather_ga.finish()
    gather_gb.finish()
    gather_i.pass_on()
    gather_j.pass_on()

    for c in range(NB):
        both = jnp.concatenate([ga[c % 2, c // 2], gb[c % 2, :, c // 2]], axis=1)
        g_v[c * BW : (c + 1) * BW, :] = both.reshape(BW, BW)
    g = halves(g_v[...])
    phi_j = halves(phi[1])
    s1[...] = eye(BW) + mm(phi_j, g, NN)
    chol_inverse(s1, linv_v)
    linv = halves(linv_v[...])
    k = mm(g, linv, NT)
    k_v[...] = k
    for c in range(NB):
        kb_v[c] = k[c * BW : (c + 1) * BW, :]
    kh = halves(k)
    p = cov_v[0] - mm(k_v[pl.ds(row0, PAN), :], kh, NT)
    gather_i.phase3()
    gather_j.phase3()
    gather_gs.phase3()
    gather_gs.finish()
    vecs = [
        jnp.concatenate([gs[c % 2, c // 2, o, :, 0:PAN] for o in range(SIDE)], axis=1) for c in range(NB)
    ]
    zeta_i = jnp.broadcast_to(vecs[0][2:3, :], (8, BW))
    zeta_j = jnp.broadcast_to(vecs[0][3:4, :], (8, BW))
    b_i = jnp.concatenate([jnp.broadcast_to(v[0:1, :], (8, BW)) for v in vecs], axis=1)
    b_j = jnp.concatenate([jnp.broadcast_to(v[1:2, :], (8, BW)) for v in vecs], axis=1)
    solved = mm(zeta_j - mm(b_i, phi_j, NT), linv, NT)
    xrow = b_i + mm(solved, kh, NT)
    gather_i.finish()

    for c in range(NB):
        t = mm(phi[1, :, c * BW : (c + 1) * BW], rows_i(c), NN)
        for d in range(NB):
            part = jnp.zeros((BW, BW), F32) if c == 0 else o_v[d]
            for n in range(3):
                part = part + is_block(pat[n, 0, c], d) * t[:, n * BW : (n + 1) * BW]
            o_v[d] = part
    for d in range(NB):
        u_v[d] = mm(linv, o_v[d], NN)
    t1[...] = u_v[row].T
    upper = t1[pl.ds(lo, PAN), :]
    drop = mm(upper, kh, NT)
    for c in range(NB):
        rows = rows_i(c)
        w = jnp.zeros((BW, BW), F32)
        for n in range(3):
            w = w + is_block(pat[n, 0, c], row) * rows[:, n * BW : (n + 1) * BW]
        t1[...] = w.T
        sl = slice(c * BW, (c + 1) * BW)
        xt[c] = jnp.concatenate([p[:, sl], t1[pl.ds(lo, PAN), :] - drop[:, sl], xrow[:, sl]], axis=0)
    gather_j.finish()
    y = jnp.concatenate(times_dyn_t(xt, pat, rows_j, 1), axis=1)
    for q, part in enumerate(pack(y[:PAN, :])):
        pk[q] = part
    swap1.start()
    lamt[...] = y[PAN : 2 * PAN, :]
    b_own = y[2 * PAN :, :] + b_j
    bz[...] = b_own

    @pl.when(jnp.logical_not(odd))
    def _():
        up_lam.start()
        up_b.start()

    for d in range(NB):
        o_v[d] = phi[0, :, d * BW : (d + 1) * BW]
    t1[...] = o_v[row].T
    prior = t1[pl.ds(lo, PAN), :]
    fac[:, :BW] = upper
    fac[:, BW : 2 * BW] = prior
    fac[:, 2 * BW :] = jnp.zeros((PAN, 2 * BW), F32)
    info = mm(solved, upper, NT) + mm(zeta_i, prior, NT)
    swap1.finish()

    def send_up(n):
        @pl.when(jnp.logical_not(odd))
        def _():
            up_cov[n].start()

    unpack(rec, z1)
    for c in range(NB):
        sl = slice(c * BW, (c + 1) * BW)
        c_pan[:, sl] = dyn_times(z1, pat, rows_j, 1, c).T + cov_v[1, :, sl]
        if c % 2 == 1:
            send_up(c // 2)

    def my_panel(full):
        put_blocks(o_v.at[:, 0:8, :], full)
        block = o_v[row, 0:8, :]
        return pltpu.roll(block, lax.rem(BW - lo, BW), 1)[0:1, 0:PAN]

    @pl.when(jnp.logical_not(odd))
    def _():
        pieces = pltpu.make_async_copy(fac.at[:, 0 : 2 * BW], out_fac.at[0, :, 2 * BW :], own.at[6])
        pieces.start()
        pieces.wait()
        down_lam.wait_recv()
        for q, part in enumerate(pack(lamt2_in[...])):
            pkl[q] = part
        swap3.start()
        down_vec.wait_recv()
        out_off[...] = vec_in[0:1, 0:PAN]
        out_info[...] = info[0:1, :] + vec_in[1:2, 0:PAN]
        swap3.finish()
        unpack(recl, z1)
        for c in range(NB):
            lam[:, c * BW : (c + 1) * BW] = z1[c].reshape(BW, PAN).T
        dyn_out = pltpu.make_async_copy(lam, out_dyn.at[0], own.at[8])
        dyn_out.start()
        dyn_out.wait()
        swap3.drain()
        for one in down_cov:
            one.wait_recv()
        down_fac.wait_recv()
        up_lam.wait_send()
        up_b.wait_send()
        for one in up_cov:
            one.wait_send()

    @pl.when(odd)
    def _():
        out_off[...] = my_panel(b_own)
        out_info[...] = info[0:1, :]
        ones = [
            pltpu.make_async_copy(c_pan, out_cov.at[0], own.at[6]),
            pltpu.make_async_copy(fac, out_fac.at[0], own.at[7]),
        ]
        for one in ones:
            one.start()
        up_lam.wait_recv()
        up_b.wait_recv()
        lam_parts = [jnp.zeros((PAN, BW), F32) for _ in range(NB)]
        ak = jnp.zeros((PAN, BW), F32)
        for n in range(3):
            b = pat[n, 1, row]
            block = vj[core, obs, x, :, n * BW : (n + 1) * BW]
            mine = halves(block)
            t = mm(mine, vi[lax.rem(b, 2), lax.div(b, 2)].reshape(BW, 3 * BW), NN)
            for m in range(3):
                at = pat[m, 0, b]
                for d in range(NB):
                    lam_parts[d] = lam_parts[d] + is_block(at, d) * t[:, m * BW : (m + 1) * BW]
            ak = ak + mm(mine, kb_v[b], NN)
        akh = halves(ak)
        for d in range(NB):
            lam[:, d * BW : (d + 1) * BW] = lam_parts[d] - mm(akh, u_v[d], NN)
        dyn_out = pltpu.make_async_copy(lam, out_dyn.at[0], own.at[8])
        dyn_out.start()

        u = jnp.concatenate([u_v[d] for d in range(NB)], axis=1)
        phi_b = halves(jnp.concatenate([u, phi[0]], axis=0))
        gain2 = jnp.zeros((PAN, 2 * BW), F32)
        for n in range(ST // CHUNK):
            up_cov[n].wait_recv()
            part = tuple(h[:, n * CHUNK : (n + 1) * CHUNK] for h in phi_b)
            gain2 = gain2 + mm(ca[:, chunk(n)], part, NT)
        g2a[core, x, obs] = gain2[:, :BW]
        g2b[core, obs, x] = gain2[:, BW:]
        gather_2a.phase1()
        gather_2b.phase1()
        la, bp = lamt_a[...], ba[...]
        start = jnp.concatenate([ca[...], la, bp], axis=0)
        across = mm(start[PAN:], phi_b, NT)
        seen = across[:PAN]
        resid = jnp.concatenate([solved, zeta_i], axis=1) - across[PAN:]
        gather_2a.phase2()
        gather_2b.phase2()
        gather_2a.phase3()
        gather_2b.phase3()
        gather_2a.finish()
        gather_2b.finish()
        for c in range(NB):
            g2_v[c * BW : (c + 1) * BW, :BW] = g2a[c % 2, c // 2].reshape(BW, BW)
            g2_v[c * BW : (c + 1) * BW, BW:] = g2b[c % 2, :, c // 2].reshape(BW, BW)
        g2 = halves(g2_v[...])
        s2[...] = eye(2 * BW) + mm(phi_b, g2, NN)
        chol_inverse_2(s2, linv2_v, t1, n1)
        linv2 = halves(linv2_v[...])
        ahead = mm(jnp.concatenate([g2_v[pl.ds(row0, PAN), :], seen, resid], axis=0), linv2, NT)
        fac2[...] = ahead[PAN : 2 * PAN]
        down_fac.start()
        solved2 = ahead[2 * PAN :]
        sign = jnp.where(lax.broadcasted_iota(jnp.int32, (2 * PAN + 8, 1), 0) < 2 * PAN, -1.0, 1.0)
        xs = start + mm(sign * mm(ahead, linv2, NN), g2, NT)
        put_blocks(xt, xs)
        h = jnp.concatenate(times_dyn_t(xt, pat, rows_i, 0), axis=1)
        put_blocks(xt, h - mm(mm(xs, u, NT), k_v[...], NT))
        y2 = jnp.concatenate(times_dyn_t(xt, pat, rows_j, 1), axis=1)
        for q, part in enumerate(pack(y2[:PAN, :])):
            pk2[q] = part
        swap2.start()
        lamt2[...] = y2[PAN : 2 * PAN, :]
        down_lam.start()
        vec[...] = jnp.zeros((8, BW), F32)
        vec[0:1, 0:PAN] = my_panel(y2[2 * PAN :, :] + b_own)
        vec[1:2, 0:PAN] = mm(solved2, fac2[...], NT)[0:1, :]
        down_vec.start()
        swap2.finish()
        unpack(rec2, z1)
        uz = jnp.zeros((BW, PAN), F32)
        for d in range(NB):
            uz = uz + mm(u_v[d], z1[d].reshape(BW, PAN), NN)
        kz = mm(k_v[...], uz, NN)
        for c in range(NB):
            part = dyn_times(z1, pat, rows_i, 0, c) - kz[c * BW : (c + 1) * BW, :]
            z2[c] = part.reshape(4, PAN, PAN)
        for c in range(NB):
            sl = slice(c * BW, (c + 1) * BW)
            c2[:, sl] = dyn_times(z2, pat, rows_j, 1, c).T + c_pan[:, sl]
            if c % 2 == 1:
                down_cov[c // 2].start()
        for one in ones:
            one.wait()
        dyn_out.wait()
        gather_2a.drain()
        gather_2b.drain()
        swap2.drain()
        for one in [down_fac, down_vec, down_lam] + down_cov:
            one.wait_send()

    for e in range(2):
        for d in range(1, SIDE):
            obs_copy(e, d).wait_send()
    for one in (gather_i, gather_j, gather_ga, gather_gb, gather_gs):
        one.drain()
    swap1.drain()


def vmem(*shape):
    return pltpu.VMEM(shape, F32)


def dma(*shape):
    return pltpu.SemaphoreType.DMA(shape)


SCRATCH = [
    vmem(2, PAN, ST), vmem(2, SIDE, PAN, 2 * BW),
    vmem(2, SIDE, SIDE, PAN, 3 * BW), vmem(2, SIDE, SIDE, PAN, 3 * BW),
    vmem(2, SIDE, SIDE, 16, BW), vmem(2, SIDE, SIDE, 16, BW), vmem(2, SIDE, SIDE, 8, BW),
    vmem(2, BW, ST),
    vmem(BW, BW), vmem(BW, BW), vmem(BW, BW), vmem(BW, BW),
    vmem(2 * BW, 2 * BW), vmem(2 * BW, 2 * BW),
    vmem(ST, BW), vmem(ST, BW), vmem(NB, BW, BW), vmem(NB, BW, BW), vmem(NB, 2 * PAN + 8, BW),
    vmem(GROUP, 8, BW), vmem(GROUP, 8, BW),
    vmem(PAN, ST), vmem(PAN, ST), vmem(8, ST), vmem(8, ST), vmem(PAN, ST), vmem(PAN, ST),
    vmem(2, SIDE, SIDE, PAN, BW), vmem(2, SIDE, SIDE, PAN, BW),
    vmem(ST, 2 * BW),
    vmem(GROUP, 8, BW), vmem(GROUP, 8, BW), vmem(GROUP, 8, BW), vmem(GROUP, 8, BW),
    vmem(PAN, ST), vmem(PAN, ST),
    vmem(PAN, 2 * BW), vmem(PAN, ST), vmem(8, BW), vmem(8, BW),
    vmem(PAN, ST), vmem(PAN, 4 * BW),
    vmem(NB, 4, PAN, PAN), vmem(NB, 4, PAN, PAN), vmem(NB, BW, BW),
    vmem(2, PAN), pltpu.VMEM((2, BW), jnp.int32), vmem(2, PAN),
    dma(2, 3), dma(2, 3), dma(7, 12), dma(7, 12), dma(6), dma(13), dma(13), dma(12),
]


def place_body(*refs):
    n = len(refs) // 2
    sems = refs[-1]
    copies = [pltpu.make_async_copy(refs[i], refs[n + i], sems.at[i]) for i in range(n)]
    for one in copies:
        one.start()
    for one in copies:
        one.wait()


def per_device(dyn_pattern, *rest):
    outs = [(1, PAN, ST), (1, PAN), (1, PAN, ST), (1, PAN, 4 * BW), (1, PAN)]
    found = pl.pallas_call(
        kernel,
        out_shape=[jax.ShapeDtypeStruct(s, F32) for s in outs],
        in_specs=[SM] + [ANY] * 6,
        out_specs=[ANY, VM, ANY, ANY, VM],
        scratch_shapes=SCRATCH,
        compiler_params=pltpu.CompilerParams(
            collective_id=0, has_side_effects=True, vmem_limit_bytes=60 << 20
        ),
    )(jnp.transpose(dyn_pattern, (2, 0, 1)), *rest)
    return pl.pallas_call(
        place_body,
        out_shape=[jax.ShapeDtypeStruct(s, F32) for s in outs],
        in_specs=[VM] * len(outs),
        out_specs=[ANY] * len(outs),
        scratch_shapes=[dma(len(outs))],
    )(*found)


def solution(mesh):
    placed = (
        P("tm", None, None),
        P("tm", ("row", "obs"), None),
        P("tm", ("row", "obs")),
        P("tm", ("row", "obs"), None),
        P("tm", None),
        P("tm", "obs", None),
        P("tm", "obs"),
    )
    return jax.shard_map(
        per_device,
        mesh=mesh,
        in_specs=placed,
        out_specs=(
            P("tm", ("row", "obs"), None),
            P("tm", ("row", "obs")),
            P("tm", ("row", "obs"), None),
            P("tm", ("row", "obs"), None),
            P("tm", ("row", "obs")),
        ),
        check_vma=False,
    )
```

```python
import functools

import jax
import jax.numpy as jnp
from jax import lax
from jax.experimental import pallas as pl
from jax.experimental.pallas import tpu as pltpu
from jax.sharding import PartitionSpec as P

F32 = jnp.float32
BF = jnp.bfloat16
NN = (((1,), (0,)), ((), ()))
NT = (((1,), (1,)), ((), ()))
TN = (((0,), (0,)), ((), ()))
MESH = pl.DeviceIdType.MESH
VM = pl.BlockSpec(memory_space=pltpu.VMEM)
SM = pl.BlockSpec(memory_space=pltpu.SMEM)
ANY = pl.BlockSpec(memory_space=pl.ANY)
NB = 8
BW = 128
ST = NB * BW
GROUP = 32
SIDE = 4
TM_DEV = 8
PAN = 32
CHUNK = 256


def halves(x):
    hi = x.astype(BF)
    return hi, (x - hi.astype(F32)).astype(BF)
def mm(a, b, dims):
    ah, al = a if isinstance(a, tuple) else halves(a)
    bh, bl = b if isinstance(b, tuple) else halves(b)
    d = functools.partial(lax.dot_general, dimension_numbers=dims, preferred_element_type=F32)
    return d(ah, bh) + (d(ah, bl) + d(al, bh))
def eye(n):
    rows = lax.broadcasted_iota(jnp.int32, (n, n), 0)
    cols = lax.broadcasted_iota(jnp.int32, (n, n), 1)
    return jnp.where(rows == cols, 1.0, 0.0).astype(F32)


def chol_inverse(s_ref, n_ref, ahead_of_last=None):
    n_ref[...] = eye(BW)
    sub = lax.broadcasted_iota(jnp.int32, (8, BW), 0)
    lane = lax.broadcasted_iota(jnp.int32, (32, BW), 1)

    def panel(b, carry):
        if ahead_of_last is not None:
            pl.when(b == 3)(ahead_of_last)
        k0 = pl.multiple_of(b * 32, 32)
        r = [s_ref[pl.ds(k0 + 8 * t, 8), :] for t in range(4)]
        n = [n_ref[pl.ds(k0 + 8 * t, 8), :] for t in range(4)]
        a = [pltpu.roll(x, lax.rem(BW - k0, BW), 1) for x in r]
        for h in range(4):
            c = {t: [jnp.broadcast_to(a[t][:, 8 * h + j : 8 * h + j + 1], (8, BW)) for j in range(8)] for t in range(h, 4)}
            piv = jnp.ones((8, BW), F32)
            for j in range(8):
                p = jnp.broadcast_to(c[h][j][j : j + 1, :], (8, BW))
                inv = 1.0 / p
                piv = jnp.where(sub == j, p, piv)
                own = [c[h][m][j : j + 1, :] for m in range(8)]
                ra, rr, rn = a[h][j : j + 1, :], r[h][j : j + 1, :], n[h][j : j + 1, :]
                for t in range(h, 4):
                    f = c[t][j] * inv
                    if t == h:
                        f = jnp.where(sub > j, f, 0.0)
                    for m in range(j + 1, 8):
                        c[t][m] = c[t][m] - f * own[m]
                    if h < 3:
                        a[t] = a[t] - f * ra
                    r[t] = r[t] - f * rr
                    n[t] = n[t] - f * rn
            scale = lax.rsqrt(piv)
            scale = scale * (1.5 - 0.5 * piv * scale * scale)
            r[h] = r[h] * scale
            n[h] = n[h] * scale
        for t in range(4):
            n_ref[pl.ds(k0 + 8 * t, 8), :] = n[t]

        @pl.when(b < 3)
        def _():
            rows = jnp.concatenate(r, axis=0)
            later = jnp.where(lane >= k0 + 32, rows, 0.0)
            both = jnp.concatenate([rows, jnp.concatenate(n, axis=0)], axis=1)
            lh = later.astype(BF).astype(F32)
            bh = both.astype(BF).astype(F32)
            left = jnp.concatenate([lh, lh, later - lh], axis=0).astype(BF)
            right = jnp.concatenate([bh, both - bh, bh], axis=0).astype(BF)
            change = lax.dot_general(left, right, TN, preferred_element_type=F32)
            s_ref[...] = s_ref[...] - change[:, :BW]
            n_ref[...] = n_ref[...] - change[:, BW:]

        return carry

    lax.fori_loop(0, 4, panel, 0)

def chol_inverse_2(s_ref, linv_ref, t_ref, n_ref):
    t_ref[...] = s_ref[:BW, :BW]
    chol_inverse(t_ref, n_ref)
    n1 = n_ref[...]
    n1h = halves(n1)
    low = mm(s_ref[BW:, :BW], n1h, NT)
    lowh = halves(low)
    t_ref[...] = s_ref[BW:, BW:] - mm(lowh, lowh, NT)
    cross = mm(lowh, n1h, NN)
    chol_inverse(t_ref, n_ref)
    n2 = n_ref[...]
    linv_ref[:BW, :BW] = n1
    linv_ref[:BW, BW:] = jnp.zeros((BW, BW), F32)
    linv_ref[BW:, :BW] = -mm(n2, cross, NN)
    linv_ref[BW:, BW:] = n2


def times_dyn_t(x_ref, pat, rows, e):
    out = []
    for c in range(NB):
        xs = jnp.concatenate([x_ref[pat[k, e, c]] for k in range(3)], axis=1)
        out.append(mm(xs, rows(c), NT))
    return out


def dyn_times(z_ref, pat, rows, e, c):
    zs = jnp.concatenate([z_ref[pat[k, e, c]].reshape(BW, PAN) for k in range(3)], axis=0)
    return mm(rows(c), zs, NN)


def is_block(found, block):
    return (found == block).astype(F32)


def put_blocks(ref, x):
    for d in range(NB):
        ref[d] = x[:, d * BW : (d + 1) * BW]


def pack(y):
    return [
        jnp.concatenate([y[s * 8 : s * 8 + 8, q * PAN : q * PAN + PAN] for s in range(4)], axis=1)
        for q in range(GROUP)
    ]


def unpack(rec_ref, z_ref):
    for s in range(4):
        part = rec_ref[:, :, s * PAN : s * PAN + PAN]
        z_ref[:, :, s * 8 : s * 8 + 8, :] = part.reshape(NB, 4, 8, PAN)


def factor_rows(blk, mat):
    at = jnp.broadcast_to(blk.astype(F32), (BW, BW)).T
    out = []
    for d in range(NB):
        before = (d + NB - 1) % NB
        out.append(jnp.where(at == d, mat[:, :BW], 0.0) + jnp.where(at == before, mat[:, BW:], 0.0))
    return out


class Gather:
    def __init__(self, place, src, buf, send, recv, swapped, ring=False):
        tm, row, obs = place
        x, core = row // 2, lax.rem(row, 2)
        self.core, self.buf, self.src = core, buf, src
        self.i, self.j = (obs, x) if swapped else (x, obs)
        self.send, self.recv, self.ring = send, recv, ring
        self.direct = (1, 3) if ring else (1, 2, 3)

        def device(i, j, c):
            xx, yy = (j, i) if swapped else (i, j)
            return (tm, 2 * xx + c, yy)

        self.device = device

    def copy(self, src, dst, n, device):
        return pltpu.make_async_remote_copy(
            src_ref=src, dst_ref=dst, send_sem=self.send.at[n], recv_sem=self.recv.at[n],
            device_id=device, device_id_type=MESH,
        )

    def first(self, d):
        piece = self.buf.at[self.core, self.i, self.j]
        j = lax.rem(self.j + d, SIDE)
        return self.copy(self.src if self.src is not None else piece, piece, d - 1, self.device(self.i, j, self.core))

    def second(self, d):
        block = self.buf.at[self.core, self.i]
        i = lax.rem(self.i + d, SIDE)
        return self.copy(block, block, 2 + d, self.device(i, self.j, self.core))

    def across(self, d):
        block = self.buf.at[self.core, lax.rem(self.i + SIDE - d, SIDE)]
        return self.copy(block, block, 6 + d, self.device(self.i, self.j, 1 - self.core))

    def phase1(self):
        for d in range(1, SIDE):
            self.first(d).start()

    def phase2(self):
        for d in range(1, SIDE):
            self.first(d).wait_recv()
        for d in self.direct:
            self.second(d).start()
        self.across(0).start()

    def onward(self, d):
        half = pl.ds(0, SIDE // 2) if d == 1 else pl.ds(SIDE // 2, SIDE // 2)
        part = self.buf.at[self.core, lax.rem(self.i + SIDE - d, SIDE), half]
        return self.copy(part, part, 4 if d == 1 else 10, self.device(lax.rem(self.i + d, SIDE), self.j, self.core))

    def pass_on(self):
        for d in (1, 3):
            self.second(d).wait_recv()
            self.onward(d).start()
        for d in (1, 3):
            self.across(d).start()

    def phase3(self):
        if self.ring:
            for d in (1, 3):
                self.onward(d).wait_recv()
            self.across(2).start()
            return
        for d in self.direct:
            self.second(d).wait_recv()
            self.across(d).start()

    def finish(self):
        for d in range(SIDE):
            self.across(d).wait_recv()

    def drain(self):
        for d in range(1, SIDE):
            self.first(d).wait_send()
        for d in self.direct:
            self.second(d).wait_send()
        if self.ring:
            for d in (1, 3):
                self.onward(d).wait_send()
        for d in range(SIDE):
            self.across(d).wait_send()


class Swap:
    def __init__(self, place, src, dst, sem, n, own):
        self.tm, row, obs = place
        self.me = row * SIDE + obs
        self.src, self.dst, self.own = src, dst, own
        self.send, self.recv = sem.at[2 * n], sem.at[2 * n + 1]
        self.rows = [lax.rem(row + d, NB) for d in range(NB)]
        self.cols = [lax.rem(obs + d, SIDE) for d in range(SIDE)]

    def start(self):
        for dr in range(NB):
            for do in range(SIDE):
                if dr + do > 0:
                    r, o = self.rows[dr], self.cols[do]
                    pltpu.make_async_remote_copy(
                        src_ref=self.src.at[r * SIDE + o], dst_ref=self.dst.at[self.me],
                        send_sem=self.send, recv_sem=self.recv,
                        device_id=(self.tm, r, o), device_id_type=MESH,
                    ).start()
        self.mine().start()

    def mine(self):
        return pltpu.make_async_copy(self.src.at[self.me], self.dst.at[self.me], self.own)

    def total(self):
        blocks = pl.ds(0, GROUP - 1)
        return pltpu.make_async_remote_copy(
            src_ref=self.src.at[blocks], dst_ref=self.dst.at[blocks],
            send_sem=self.send, recv_sem=self.recv,
            device_id=(self.tm, self.rows[1], self.cols[0]), device_id_type=MESH,
        )

    def finish(self):
        self.mine().wait()
        self.total().wait_recv()

    def drain(self):
        self.total().wait_send()


def kernel(
    pat, vals, offs_h, cov, blk_h, omat, odat_h,
    out_dyn, out_off, out_cov, out_fac, out_info,
    cov_v, obs_v, vi, vj, ga, gb, gs, phi, s1, t1, n1, linv_v, s2, linv2_v,
    g_v, k_v, u_v, o_v, xt, pk, rec, lamt, lamt_a, bz, ba, c_pan, ca, g2a, g2b, g2_v,
    pk2, rec2, pkl, recl, lamt2, lamt2_in, fac2, c2, vec, vec_in, lam, fac, z1, z2, kb_v, offs, blk, odat,
    obs_s, obs_r, gat_s, gat_r, swap, z_s, z_r, own,
):
    tm, row, obs = lax.axis_index("tm"), lax.axis_index("row"), lax.axis_index("obs")
    place = (tm, row, obs)
    x, core = row // 2, lax.rem(row, 2)
    me = row * SIDE + obs
    row0 = pl.multiple_of(me * PAN, PAN)
    lo = pl.multiple_of(obs * PAN, PAN)
    odd = lax.rem(tm, 2) == 1
    up = (lax.rem(tm + 1, TM_DEV), row, obs)
    down = (lax.rem(tm + TM_DEV - 1, TM_DEV), row, obs)

    def rows_i(c):
        return vi[c % 2, c // 2].reshape(BW, 3 * BW)

    def rows_j(c):
        return vj[c % 2, :, c // 2].reshape(BW, 3 * BW)

    def obs_copy(e, d):
        return pltpu.make_async_remote_copy(
            src_ref=omat.at[e], dst_ref=obs_v.at[e, obs], send_sem=obs_s.at[e, d - 1], recv_sem=obs_r.at[e, d - 1],
            device_id=(tm, row, lax.rem(obs + d, SIDE)), device_id_type=MESH,
        )

    def z_copy(n, src, dst, device):
        return pltpu.make_async_remote_copy(
            src_ref=src, dst_ref=dst, send_sem=z_s.at[n], recv_sem=z_r.at[n], device_id=device, device_id_type=MESH
        )

    gather_i = Gather(place, vals.at[0], vi, gat_s.at[0], gat_r.at[0], False, True)
    gather_j = Gather(place, vals.at[1], vj, gat_s.at[1], gat_r.at[1], True, True)
    gather_ga = Gather(place, None, ga, gat_s.at[2], gat_r.at[2], False)
    gather_gb = Gather(place, None, gb, gat_s.at[3], gat_r.at[3], True)
    gather_gs = Gather(place, None, gs, gat_s.at[6], gat_r.at[6], False)
    gather_2a = Gather(place, None, g2a, gat_s.at[4], gat_r.at[4], False)
    gather_2b = Gather(place, None, g2b, gat_s.at[5], gat_r.at[5], True)
    swap1 = Swap(place, pk, rec, swap, 0, own.at[4])
    swap2 = Swap(place, pk2, rec2, swap, 1, own.at[5])
    swap3 = Swap(place, pkl, recl, swap, 2, own.at[5])
    up_lam = z_copy(0, lamt, lamt_a, up)
    up_b = z_copy(1, bz, ba, up)
    def chunk(n):
        return pl.ds(n * CHUNK, CHUNK)

    up_cov = [z_copy(8 + n, c_pan.at[:, chunk(n)], ca.at[:, chunk(n)], up) for n in range(ST // CHUNK)]
    down_cov = [
        z_copy(4 + n, c2.at[:, chunk(n)], out_cov.at[0, :, chunk(n)], down) for n in range(ST // CHUNK)
    ]
    down_fac = z_copy(2, fac2, out_fac.at[0, :, 0 : 2 * BW], down)
    down_vec = z_copy(3, vec, vec_in, down)
    down_lam = z_copy(12, lamt2, lamt2_in, down)

    local_cov = pltpu.make_async_copy(cov, cov_v, own.at[0])
    local_i = pltpu.make_async_copy(vals.at[0], vi.at[core, x, obs], own.at[1])
    local_j = pltpu.make_async_copy(vals.at[1], vj.at[core, obs, x], own.at[2])
    local_obs = pltpu.make_async_copy(omat, obs_v.at[:, obs], own.at[3])
    tiny = [
        pltpu.make_async_copy(a, b, own.at[9 + n])
        for n, (a, b) in enumerate([(offs_h, offs), (odat_h, odat), (blk_h, blk)])
    ]
    local_obs.start()
    for one in tiny:
        one.start()
    local_cov.start()
    local_i.start()
    local_j.start()

    barrier = pltpu.get_barrier_semaphore()

    partners = [(tm, row, lax.rem(obs + d, SIDE)) for d in range(1, SIDE)]
    partners += [(tm, 2 * lax.rem(x + d, SIDE) + core, obs) for d in range(1, SIDE)]
    partners += [(tm, 2 * x + 1 - core, obs), up, down]
    for partner in partners:
        pl.semaphore_signal(barrier, inc=1, device_id=partner, device_id_type=MESH)
    pl.semaphore_wait(barrier, len(partners))

    for d in range(1, SIDE):
        obs_copy(1, d).start()
    gather_i.phase1()
    gather_j.phase1()

    local_obs.wait()
    for one in tiny:
        one.wait()
    for d in range(1, SIDE):
        obs_copy(1, d).wait_recv()
    for d, part in enumerate(factor_rows(blk[1:2, :], obs_v[1].reshape(BW, 2 * BW))):
        phi[1, :, d * BW : (d + 1) * BW] = part
    local_cov.wait()
    gain = mm(cov_v[0], phi[1], NT)
    ga[core, x, obs] = gain[0:16]
    small = jnp.concatenate([offs[...], odat[...]], axis=0)
    gb[core, obs, x] = gain[16:32]
    gs[core, x, obs] = jnp.zeros((8, BW), F32)
    gs[core, x, obs, 0:4, 0:PAN] = small
    gather_ga.phase1()
    gather_gb.phase1()
    gather_ga.phase2()
    gather_gb.phase2()
    gather_gs.phase1()
    local_i.wait()
    local_j.wait()
    gather_i.phase2()
    gather_j.phase2()
    gather_ga.phase3()
    gather_gb.phase3()
    for d in range(1, SIDE):
        obs_copy(0, d).start()
    gather_gs.phase2()
    gather_ga.finish()
    gather_gb.finish()
    gather_i.pass_on()
    gather_j.pass_on()

    for c in range(NB):
        both = jnp.concatenate([ga[c % 2, c // 2], gb[c % 2, :, c // 2]], axis=1)
        g_v[c * BW : (c + 1) * BW, :] = both.reshape(BW, BW)
    g = halves(g_v[...])
    phi_j = halves(phi[1])
    s1[...] = eye(BW) + mm(phi_j, g, NN)

    def hand_over():
        for one in (gather_i, gather_j, gather_gs):
            one.phase3()

    chol_inverse(s1, linv_v, hand_over)
    linv = halves(linv_v[...])
    k = mm(g, linv, NT)
    k_v[...] = k
    for c in range(NB):
        kb_v[c] = k[c * BW : (c + 1) * BW, :]
    kh = halves(k)
    p = cov_v[0] - mm(k_v[pl.ds(row0, PAN), :], kh, NT)
    gather_gs.finish()
    vecs = [
        jnp.concatenate([gs[c % 2, c // 2, o, :, 0:PAN] for o in range(SIDE)], axis=1) for c in range(NB)
    ]
    zeta_i = jnp.broadcast_to(vecs[0][2:3, :], (8, BW))
    zeta_j = jnp.broadcast_to(vecs[0][3:4, :], (8, BW))
    b_i = jnp.concatenate([jnp.broadcast_to(v[0:1, :], (8, BW)) for v in vecs], axis=1)
    b_j = jnp.concatenate([jnp.broadcast_to(v[1:2, :], (8, BW)) for v in vecs], axis=1)
    solved = mm(zeta_j - mm(b_i, phi_j, NT), linv, NT)
    xrow = b_i + mm(solved, kh, NT)
    gather_i.finish()

    for c in range(NB):
        t = mm(phi[1, :, c * BW : (c + 1) * BW], rows_i(c), NN)
        for d in range(NB):
            part = jnp.zeros((BW, BW), F32) if c == 0 else o_v[d]
            for n in range(3):
                part = part + is_block(pat[n, 0, c], d) * t[:, n * BW : (n + 1) * BW]
            o_v[d] = part
    for d in range(NB):
        u_v[d] = mm(linv, o_v[d], NN)
    t1[...] = u_v[row].T
    upper = t1[pl.ds(lo, PAN), :]
    drop = mm(upper, kh, NT)
    for c in range(NB):
        rows = rows_i(c)
        w = jnp.zeros((BW, BW), F32)
        for n in range(3):
            w = w + is_block(pat[n, 0, c], row) * rows[:, n * BW : (n + 1) * BW]
        t1[...] = w.T
        sl = slice(c * BW, (c + 1) * BW)
        xt[c] = jnp.concatenate([p[:, sl], t1[pl.ds(lo, PAN), :] - drop[:, sl], xrow[:, sl]], axis=0)
    gather_j.finish()
    y = jnp.concatenate(times_dyn_t(xt, pat, rows_j, 1), axis=1)
    for q, part in enumerate(pack(y[:PAN, :])):
        pk[q] = part
    swap1.start()
    lamt[...] = y[PAN : 2 * PAN, :]
    b_own = y[2 * PAN :, :] + b_j
    bz[...] = b_own

    @pl.when(jnp.logical_not(odd))
    def _():
        up_lam.start()
        up_b.start()

    for d in range(1, SIDE):
        obs_copy(0, d).wait_recv()
    for d, part in enumerate(factor_rows(blk[0:1, :], obs_v[0].reshape(BW, 2 * BW))):
        phi[0, :, d * BW : (d + 1) * BW] = part
    for d in range(NB):
        o_v[d] = phi[0, :, d * BW : (d + 1) * BW]
    t1[...] = o_v[row].T
    prior = t1[pl.ds(lo, PAN), :]
    fac[:, :BW] = upper
    fac[:, BW : 2 * BW] = prior
    fac[:, 2 * BW :] = jnp.zeros((PAN, 2 * BW), F32)
    info = mm(solved, upper, NT) + mm(zeta_i, prior, NT)
    swap1.finish()

    def send_up(n):
        @pl.when(jnp.logical_not(odd))
        def _():
            up_cov[n].start()

    unpack(rec, z1)
    for c in range(NB):
        sl = slice(c * BW, (c + 1) * BW)
        c_pan[:, sl] = dyn_times(z1, pat, rows_j, 1, c).T + cov_v[1, :, sl]
        if c % 2 == 1:
            send_up(c // 2)

    def my_panel(full):
        put_blocks(o_v.at[:, 0:8, :], full)
        block = o_v[row, 0:8, :]
        return pltpu.roll(block, lax.rem(BW - lo, BW), 1)[0:1, 0:PAN]

    @pl.when(jnp.logical_not(odd))
    def _():
        pieces = pltpu.make_async_copy(fac.at[:, 0 : 2 * BW], out_fac.at[0, :, 2 * BW :], own.at[6])
        pieces.start()
        pieces.wait()
        down_lam.wait_recv()
        for q, part in enumerate(pack(lamt2_in[...])):
            pkl[q] = part
        swap3.start()
        down_vec.wait_recv()
        out_off[...] = vec_in[0:1, 0:PAN]
        out_info[...] = info[0:1, :] + vec_in[1:2, 0:PAN]
        swap3.finish()
        unpack(recl, z1)
        for c in range(NB):
            lam[:, c * BW : (c + 1) * BW] = z1[c].reshape(BW, PAN).T
        dyn_out = pltpu.make_async_copy(lam, out_dyn.at[0], own.at[8])
        dyn_out.start()
        dyn_out.wait()
        swap3.drain()
        for one in down_cov:
            one.wait_recv()
        down_fac.wait_recv()
        up_lam.wait_send()
        up_b.wait_send()
        for one in up_cov:
            one.wait_send()

    @pl.when(odd)
    def _():
        out_off[...] = my_panel(b_own)
        out_info[...] = info[0:1, :]
        ones = [
            pltpu.make_async_copy(c_pan, out_cov.at[0], own.at[6]),
            pltpu.make_async_copy(fac, out_fac.at[0], own.at[7]),
        ]
        for one in ones:
            one.start()
        up_lam.wait_recv()
        up_b.wait_recv()
        lam_parts = [jnp.zeros((PAN, BW), F32) for _ in range(NB)]
        ak = jnp.zeros((PAN, BW), F32)
        for n in range(3):
            b = pat[n, 1, row]
            block = vj[core, obs, x, :, n * BW : (n + 1) * BW]
            mine = halves(block)
            t = mm(mine, vi[lax.rem(b, 2), lax.div(b, 2)].reshape(BW, 3 * BW), NN)
            for m in range(3):
                at = pat[m, 0, b]
                for d in range(NB):
                    lam_parts[d] = lam_parts[d] + is_block(at, d) * t[:, m * BW : (m + 1) * BW]
            ak = ak + mm(mine, kb_v[b], NN)
        akh = halves(ak)
        for d in range(NB):
            lam[:, d * BW : (d + 1) * BW] = lam_parts[d] - mm(akh, u_v[d], NN)
        dyn_out = pltpu.make_async_copy(lam, out_dyn.at[0], own.at[8])
        dyn_out.start()

        u = jnp.concatenate([u_v[d] for d in range(NB)], axis=1)
        phi_b = halves(jnp.concatenate([u, phi[0]], axis=0))
        gain2 = jnp.zeros((PAN, 2 * BW), F32)
        for n in range(ST // CHUNK):
            up_cov[n].wait_recv()
            part = tuple(h[:, n * CHUNK : (n + 1) * CHUNK] for h in phi_b)
            gain2 = gain2 + mm(ca[:, chunk(n)], part, NT)
        g2a[core, x, obs] = gain2[:, :BW]
        g2b[core, obs, x] = gain2[:, BW:]
        gather_2a.phase1()
        gather_2b.phase1()
        la, bp = lamt_a[...], ba[...]
        start = jnp.concatenate([ca[...], la, bp], axis=0)
        across = mm(start[PAN:], phi_b, NT)
        seen = across[:PAN]
        resid = jnp.concatenate([solved, zeta_i], axis=1) - across[PAN:]
        gather_2a.phase2()
        gather_2b.phase2()
        gather_2a.phase3()
        gather_2b.phase3()
        gather_2a.finish()
        gather_2b.finish()
        for c in range(NB):
            g2_v[c * BW : (c + 1) * BW, :BW] = g2a[c % 2, c // 2].reshape(BW, BW)
            g2_v[c * BW : (c + 1) * BW, BW:] = g2b[c % 2, :, c // 2].reshape(BW, BW)
        g2 = halves(g2_v[...])
        s2[...] = eye(2 * BW) + mm(phi_b, g2, NN)
        chol_inverse_2(s2, linv2_v, t1, n1)
        linv2 = halves(linv2_v[...])
        ahead = mm(jnp.concatenate([g2_v[pl.ds(row0, PAN), :], seen, resid], axis=0), linv2, NT)
        fac2[...] = ahead[PAN : 2 * PAN]
        down_fac.start()
        solved2 = ahead[2 * PAN :]
        sign = jnp.where(lax.broadcasted_iota(jnp.int32, (2 * PAN + 8, 1), 0) < 2 * PAN, -1.0, 1.0)
        xs = start + mm(sign * mm(ahead, linv2, NN), g2, NT)
        put_blocks(xt, xs)
        h = jnp.concatenate(times_dyn_t(xt, pat, rows_i, 0), axis=1)
        put_blocks(xt, h - mm(mm(xs, u, NT), k_v[...], NT))
        y2 = jnp.concatenate(times_dyn_t(xt, pat, rows_j, 1), axis=1)
        for q, part in enumerate(pack(y2[:PAN, :])):
            pk2[q] = part
        swap2.start()
        lamt2[...] = y2[PAN : 2 * PAN, :]
        down_lam.start()
        vec[...] = jnp.zeros((8, BW), F32)
        vec[0:1, 0:PAN] = my_panel(y2[2 * PAN :, :] + b_own)
        vec[1:2, 0:PAN] = mm(solved2, fac2[...], NT)[0:1, :]
        down_vec.start()
        swap2.finish()
        unpack(rec2, z1)
        uz = jnp.zeros((BW, PAN), F32)
        for d in range(NB):
            uz = uz + mm(u_v[d], z1[d].reshape(BW, PAN), NN)
        kz = mm(k_v[...], uz, NN)
        for c in range(NB):
            part = dyn_times(z1, pat, rows_i, 0, c) - kz[c * BW : (c + 1) * BW, :]
            z2[c] = part.reshape(4, PAN, PAN)
        for c in range(NB):
            sl = slice(c * BW, (c + 1) * BW)
            c2[:, sl] = dyn_times(z2, pat, rows_j, 1, c).T + c_pan[:, sl]
            if c % 2 == 1:
                down_cov[c // 2].start()
        for one in ones:
            one.wait()
        dyn_out.wait()
        gather_2a.drain()
        gather_2b.drain()
        swap2.drain()
        for one in [down_fac, down_vec, down_lam] + down_cov:
            one.wait_send()

    for e in range(2):
        for d in range(1, SIDE):
            obs_copy(e, d).wait_send()
    for one in (gather_i, gather_j, gather_ga, gather_gb, gather_gs):
        one.drain()
    swap1.drain()


def vmem(*shape):
    return pltpu.VMEM(shape, F32)


def dma(*shape):
    return pltpu.SemaphoreType.DMA(shape)


SCRATCH = [
    vmem(2, PAN, ST), vmem(2, SIDE, PAN, 2 * BW),
    vmem(2, SIDE, SIDE, PAN, 3 * BW), vmem(2, SIDE, SIDE, PAN, 3 * BW),
    vmem(2, SIDE, SIDE, 16, BW), vmem(2, SIDE, SIDE, 16, BW), vmem(2, SIDE, SIDE, 8, BW),
    vmem(2, BW, ST),
    vmem(BW, BW), vmem(BW, BW), vmem(BW, BW), vmem(BW, BW),
    vmem(2 * BW, 2 * BW), vmem(2 * BW, 2 * BW),
    vmem(ST, BW), vmem(ST, BW), vmem(NB, BW, BW), vmem(NB, BW, BW), vmem(NB, 2 * PAN + 8, BW),
    vmem(GROUP, 8, BW), vmem(GROUP, 8, BW),
    vmem(PAN, ST), vmem(PAN, ST), vmem(8, ST), vmem(8, ST), vmem(PAN, ST), vmem(PAN, ST),
    vmem(2, SIDE, SIDE, PAN, BW), vmem(2, SIDE, SIDE, PAN, BW),
    vmem(ST, 2 * BW),
    vmem(GROUP, 8, BW), vmem(GROUP, 8, BW), vmem(GROUP, 8, BW), vmem(GROUP, 8, BW),
    vmem(PAN, ST), vmem(PAN, ST),
    vmem(PAN, 2 * BW), vmem(PAN, ST), vmem(8, BW), vmem(8, BW),
    vmem(PAN, ST), vmem(PAN, 4 * BW),
    vmem(NB, 4, PAN, PAN), vmem(NB, 4, PAN, PAN), vmem(NB, BW, BW),
    vmem(2, PAN), pltpu.VMEM((2, BW), jnp.int32), vmem(2, PAN),
    dma(2, 3), dma(2, 3), dma(7, 12), dma(7, 12), dma(6), dma(13), dma(13), dma(12),
]


def place_body(*refs):
    n = len(refs) // 2
    sems = refs[-1]
    copies = [pltpu.make_async_copy(refs[i], refs[n + i], sems.at[i]) for i in range(n)]
    for one in copies:
        one.start()
    for one in copies:
        one.wait()


def per_device(dyn_pattern, *rest):
    outs = [(1, PAN, ST), (1, PAN), (1, PAN, ST), (1, PAN, 4 * BW), (1, PAN)]
    found = pl.pallas_call(
        kernel,
        out_shape=[jax.ShapeDtypeStruct(s, F32) for s in outs],
        in_specs=[SM] + [ANY] * 6,
        out_specs=[ANY, VM, ANY, ANY, VM],
        scratch_shapes=SCRATCH,
        compiler_params=pltpu.CompilerParams(
            collective_id=0, has_side_effects=True, vmem_limit_bytes=60 << 20
        ),
    )(jnp.transpose(dyn_pattern, (2, 0, 1)), *rest)
    return pl.pallas_call(
        place_body,
        out_shape=[jax.ShapeDtypeStruct(s, F32) for s in outs],
        in_specs=[VM] * len(outs),
        out_specs=[ANY] * len(outs),
        scratch_shapes=[dma(len(outs))],
    )(*found)


def solution(mesh):
    placed = (
        P("tm", None, None),
        P("tm", ("row", "obs"), None),
        P("tm", ("row", "obs")),
        P("tm", ("row", "obs"), None),
        P("tm", None),
        P("tm", "obs", None),
        P("tm", "obs"),
    )
    return jax.shard_map(
        per_device,
        mesh=mesh,
        in_specs=placed,
        out_specs=(
            P("tm", ("row", "obs"), None),
            P("tm", ("row", "obs")),
            P("tm", ("row", "obs"), None),
            P("tm", ("row", "obs"), None),
            P("tm", ("row", "obs")),
        ),
        check_vma=False,
    )
```

```python
import functools

import jax
import jax.numpy as jnp
from jax import lax
from jax.experimental import pallas as pl
from jax.experimental.pallas import tpu as pltpu
from jax.sharding import PartitionSpec as P

F32 = jnp.float32
BF = jnp.bfloat16
NN = (((1,), (0,)), ((), ()))
NT = (((1,), (1,)), ((), ()))
TN = (((0,), (0,)), ((), ()))
MESH = pl.DeviceIdType.MESH
VM = pl.BlockSpec(memory_space=pltpu.VMEM)
SM = pl.BlockSpec(memory_space=pltpu.SMEM)
ANY = pl.BlockSpec(memory_space=pl.ANY)
NB = 8
BW = 128
ST = NB * BW
GROUP = 32
SIDE = 4
TM_DEV = 8
PAN = 32
CHUNK = 256


def halves(x):
    hi = x.astype(BF)
    return hi, (x - hi.astype(F32)).astype(BF)
def mm(a, b, dims):
    ah, al = a if isinstance(a, tuple) else halves(a)
    bh, bl = b if isinstance(b, tuple) else halves(b)
    d = functools.partial(lax.dot_general, dimension_numbers=dims, preferred_element_type=F32)
    return d(ah, bh) + (d(ah, bl) + d(al, bh))
def eye(n):
    rows = lax.broadcasted_iota(jnp.int32, (n, n), 0)
    cols = lax.broadcasted_iota(jnp.int32, (n, n), 1)
    return jnp.where(rows == cols, 1.0, 0.0).astype(F32)


def chol_inverse(s_ref, n_ref, ahead_of_last=None):
    n_ref[...] = eye(BW)
    sub = lax.broadcasted_iota(jnp.int32, (8, BW), 0)
    lane = lax.broadcasted_iota(jnp.int32, (32, BW), 1)

    def panel(b, carry):
        if ahead_of_last is not None:
            pl.when(b == 3)(ahead_of_last)
        k0 = pl.multiple_of(b * 32, 32)
        r = [s_ref[pl.ds(k0 + 8 * t, 8), :] for t in range(4)]
        n = [n_ref[pl.ds(k0 + 8 * t, 8), :] for t in range(4)]
        a = [pltpu.roll(x, lax.rem(BW - k0, BW), 1) for x in r]
        for h in range(4):
            c = {t: [jnp.broadcast_to(a[t][:, 8 * h + j : 8 * h + j + 1], (8, BW)) for j in range(8)] for t in range(h, 4)}
            piv = jnp.ones((8, BW), F32)
            for j in range(8):
                p = jnp.broadcast_to(c[h][j][j : j + 1, :], (8, BW))
                inv = 1.0 / p
                piv = jnp.where(sub == j, p, piv)
                own = [c[h][m][j : j + 1, :] for m in range(8)]
                ra, rr, rn = a[h][j : j + 1, :], r[h][j : j + 1, :], n[h][j : j + 1, :]
                for t in range(h, 4):
                    f = c[t][j] * inv
                    if t == h:
                        f = jnp.where(sub > j, f, 0.0)
                    for m in range(j + 1, 8):
                        c[t][m] = c[t][m] - f * own[m]
                    if h < 3:
                        a[t] = a[t] - f * ra
                    r[t] = r[t] - f * rr
                    n[t] = n[t] - f * rn
            scale = lax.rsqrt(piv)
            scale = scale * (1.5 - 0.5 * piv * scale * scale)
            r[h] = r[h] * scale
            n[h] = n[h] * scale
        for t in range(4):
            n_ref[pl.ds(k0 + 8 * t, 8), :] = n[t]

        @pl.when(b < 3)
        def _():
            rows = jnp.concatenate(r, axis=0)
            later = jnp.where(lane >= k0 + 32, rows, 0.0)
            both = jnp.concatenate([rows, jnp.concatenate(n, axis=0)], axis=1)
            lh = later.astype(BF).astype(F32)
            bh = both.astype(BF).astype(F32)
            left = jnp.concatenate([lh, lh, later - lh], axis=0).astype(BF)
            right = jnp.concatenate([bh, both - bh, bh], axis=0).astype(BF)
            change = lax.dot_general(left, right, TN, preferred_element_type=F32)
            s_ref[...] = s_ref[...] - change[:, :BW]
            n_ref[...] = n_ref[...] - change[:, BW:]

        return carry

    lax.fori_loop(0, 4, panel, 0)

def chol_inverse_2(s_ref, linv_ref, t_ref, n_ref):
    t_ref[...] = s_ref[:BW, :BW]
    chol_inverse(t_ref, n_ref)
    n1 = n_ref[...]
    n1h = halves(n1)
    low = mm(s_ref[BW:, :BW], n1h, NT)
    lowh = halves(low)
    t_ref[...] = s_ref[BW:, BW:] - mm(lowh, lowh, NT)
    cross = mm(lowh, n1h, NN)
    chol_inverse(t_ref, n_ref)
    n2 = n_ref[...]
    linv_ref[:BW, :BW] = n1
    linv_ref[:BW, BW:] = jnp.zeros((BW, BW), F32)
    linv_ref[BW:, :BW] = -mm(n2, cross, NN)
    linv_ref[BW:, BW:] = n2


def times_dyn_t(x_ref, pat, rows, e):
    out = []
    for c in range(NB):
        xs = jnp.concatenate([x_ref[pat[k, e, c]] for k in range(3)], axis=1)
        out.append(mm(xs, rows(c), NT))
    return out


def dyn_times(z_ref, pat, rows, e, c):
    zs = jnp.concatenate([z_ref[pat[k, e, c]].reshape(BW, PAN) for k in range(3)], axis=0)
    return mm(rows(c), zs, NN)


def is_block(found, block):
    return (found == block).astype(F32)


def put_blocks(ref, x):
    for d in range(NB):
        ref[d] = x[:, d * BW : (d + 1) * BW]


def pack(y):
    return [
        jnp.concatenate([y[s * 8 : s * 8 + 8, q * PAN : q * PAN + PAN] for s in range(4)], axis=1)
        for q in range(GROUP)
    ]


def unpack(rec_ref, z_ref):
    for s in range(4):
        part = rec_ref[:, :, s * PAN : s * PAN + PAN]
        z_ref[:, :, s * 8 : s * 8 + 8, :] = part.reshape(NB, 4, 8, PAN)


def factor_rows(blk, mat):
    at = jnp.broadcast_to(blk.astype(F32), (BW, BW)).T
    out = []
    for d in range(NB):
        before = (d + NB - 1) % NB
        out.append(jnp.where(at == d, mat[:, :BW], 0.0) + jnp.where(at == before, mat[:, BW:], 0.0))
    return out


class Gather:
    def __init__(self, place, src, buf, send, recv, swapped, ring=False):
        tm, row, obs = place
        x, core = row // 2, lax.rem(row, 2)
        self.core, self.buf, self.src = core, buf, src
        self.i, self.j = (obs, x) if swapped else (x, obs)
        self.send, self.recv, self.ring = send, recv, ring
        self.direct = (1, 3) if ring else (1, 2, 3)

        def device(i, j, c):
            xx, yy = (j, i) if swapped else (i, j)
            return (tm, 2 * xx + c, yy)

        self.device = device

    def copy(self, src, dst, n, device):
        return pltpu.make_async_remote_copy(
            src_ref=src, dst_ref=dst, send_sem=self.send.at[n], recv_sem=self.recv.at[n],
            device_id=device, device_id_type=MESH,
        )

    def first(self, d):
        piece = self.buf.at[self.core, self.i, self.j]
        j = lax.rem(self.j + d, SIDE)
        return self.copy(self.src if self.src is not None else piece, piece, d - 1, self.device(self.i, j, self.core))

    def second(self, d):
        block = self.buf.at[self.core, self.i]
        i = lax.rem(self.i + d, SIDE)
        return self.copy(block, block, 2 + d, self.device(i, self.j, self.core))

    def across(self, d):
        block = self.buf.at[self.core, lax.rem(self.i + SIDE - d, SIDE)]
        return self.copy(block, block, 6 + d, self.device(self.i, self.j, 1 - self.core))

    def phase1(self):
        for d in range(1, SIDE):
            self.first(d).start()

    def phase2(self):
        for d in range(1, SIDE):
            self.first(d).wait_recv()
        for d in self.direct:
            self.second(d).start()
        self.across(0).start()

    def onward(self, d):
        half = pl.ds(0, SIDE // 2) if d == 1 else pl.ds(SIDE // 2, SIDE // 2)
        part = self.buf.at[self.core, lax.rem(self.i + SIDE - d, SIDE), half]
        return self.copy(part, part, 4 if d == 1 else 10, self.device(lax.rem(self.i + d, SIDE), self.j, self.core))

    def pass_on(self):
        for d in (1, 3):
            self.second(d).wait_recv()
            self.onward(d).start()
        for d in (1, 3):
            self.across(d).start()

    def phase3(self):
        if self.ring:
            for d in (1, 3):
                self.onward(d).wait_recv()
            self.across(2).start()
            return
        for d in self.direct:
            self.second(d).wait_recv()
            self.across(d).start()

    def finish(self):
        for d in range(SIDE):
            self.across(d).wait_recv()

    def drain(self):
        for d in range(1, SIDE):
            self.first(d).wait_send()
        for d in self.direct:
            self.second(d).wait_send()
        if self.ring:
            for d in (1, 3):
                self.onward(d).wait_send()
        for d in range(SIDE):
            self.across(d).wait_send()


class Swap:
    def __init__(self, place, src, dst, sem, n, own):
        self.tm, row, obs = place
        self.me = row * SIDE + obs
        self.src, self.dst, self.own = src, dst, own
        self.send, self.recv = sem.at[2 * n], sem.at[2 * n + 1]
        self.rows = [lax.rem(row + d, NB) for d in range(NB)]
        self.cols = [lax.rem(obs + d, SIDE) for d in range(SIDE)]

    def start(self):
        for dr in range(NB):
            for do in range(SIDE):
                if dr + do > 0:
                    r, o = self.rows[dr], self.cols[do]
                    pltpu.make_async_remote_copy(
                        src_ref=self.src.at[r * SIDE + o], dst_ref=self.dst.at[self.me],
                        send_sem=self.send, recv_sem=self.recv,
                        device_id=(self.tm, r, o), device_id_type=MESH,
                    ).start()
        self.mine().start()

    def mine(self):
        return pltpu.make_async_copy(self.src.at[self.me], self.dst.at[self.me], self.own)

    def total(self):
        blocks = pl.ds(0, GROUP - 1)
        return pltpu.make_async_remote_copy(
            src_ref=self.src.at[blocks], dst_ref=self.dst.at[blocks],
            send_sem=self.send, recv_sem=self.recv,
            device_id=(self.tm, self.rows[1], self.cols[0]), device_id_type=MESH,
        )

    def finish(self):
        self.mine().wait()
        self.total().wait_recv()

    def drain(self):
        self.total().wait_send()


def kernel(
    pat, vals, offs_h, cov, blk_h, omat, odat_h,
    out_dyn, out_off, out_cov, out_fac, out_info,
    cov_v, obs_v, vi, vj, ga, gb, gs, phi, s1, t1, n1, linv_v, s2, linv2_v,
    g_v, k_v, u_v, o_v, xt, pk, rec, lamt, lamt_a, bz, ba, c_pan, ca, g2a, g2b, g2_v,
    pk2, rec2, pkl, recl, lamt2, lamt2_in, fac2, c2, vec, vec_in, lam, fac, z1, z2, kb_v, offs, blk, odat,
    obs_s, obs_r, gat_s, gat_r, swap, z_s, z_r, own,
):
    tm, row, obs = lax.axis_index("tm"), lax.axis_index("row"), lax.axis_index("obs")
    place = (tm, row, obs)
    x, core = row // 2, lax.rem(row, 2)
    me = row * SIDE + obs
    row0 = pl.multiple_of(me * PAN, PAN)
    lo = pl.multiple_of(obs * PAN, PAN)
    odd = lax.rem(tm, 2) == 1
    up = (lax.rem(tm + 1, TM_DEV), row, obs)
    down = (lax.rem(tm + TM_DEV - 1, TM_DEV), row, obs)

    def rows_i(c):
        return vi[c % 2, c // 2].reshape(BW, 3 * BW)

    def rows_j(c):
        return vj[c % 2, :, c // 2].reshape(BW, 3 * BW)

    def obs_copy(e, d):
        return pltpu.make_async_remote_copy(
            src_ref=omat.at[e], dst_ref=obs_v.at[e, obs], send_sem=obs_s.at[e, d - 1], recv_sem=obs_r.at[e, d - 1],
            device_id=(tm, row, lax.rem(obs + d, SIDE)), device_id_type=MESH,
        )

    def z_copy(n, src, dst, device):
        return pltpu.make_async_remote_copy(
            src_ref=src, dst_ref=dst, send_sem=z_s.at[n], recv_sem=z_r.at[n], device_id=device, device_id_type=MESH
        )

    gather_i = Gather(place, vals.at[0], vi, gat_s.at[0], gat_r.at[0], False, True)
    gather_j = Gather(place, vals.at[1], vj, gat_s.at[1], gat_r.at[1], True, True)
    gather_ga = Gather(place, None, ga, gat_s.at[2], gat_r.at[2], False)
    gather_gb = Gather(place, None, gb, gat_s.at[3], gat_r.at[3], True)
    gather_gs = Gather(place, None, gs, gat_s.at[6], gat_r.at[6], False)
    gather_2a = Gather(place, None, g2a, gat_s.at[4], gat_r.at[4], False)
    gather_2b = Gather(place, None, g2b, gat_s.at[5], gat_r.at[5], True)
    swap1 = Swap(place, pk, rec, swap, 0, own.at[4])
    swap2 = Swap(place, pk2, rec2, swap, 1, own.at[5])
    swap3 = Swap(place, pkl, recl, swap, 2, own.at[5])
    up_lam = z_copy(0, lamt, lamt_a, up)
    up_b = z_copy(1, bz, ba, up)
    def chunk(n):
        return pl.ds(n * CHUNK, CHUNK)

    up_cov = [z_copy(8 + n, c_pan.at[:, chunk(n)], ca.at[:, chunk(n)], up) for n in range(ST // CHUNK)]
    down_cov = [
        z_copy(4 + n, c2.at[:, chunk(n)], out_cov.at[0, :, chunk(n)], down) for n in range(ST // CHUNK)
    ]
    down_fac = z_copy(2, fac2, out_fac.at[0, :, 0 : 2 * BW], down)
    down_vec = z_copy(3, vec, vec_in, down)
    down_lam = z_copy(12, lamt2, lamt2_in, down)

    local_cov = pltpu.make_async_copy(cov, cov_v, own.at[0])
    local_i = pltpu.make_async_copy(vals.at[0], vi.at[core, x, obs], own.at[1])
    local_j = pltpu.make_async_copy(vals.at[1], vj.at[core, obs, x], own.at[2])
    local_obs = pltpu.make_async_copy(omat, obs_v.at[:, obs], own.at[3])
    tiny = [
        pltpu.make_async_copy(a, b, own.at[9 + n])
        for n, (a, b) in enumerate([(offs_h, offs), (odat_h, odat), (blk_h, blk)])
    ]
    local_obs.start()
    for one in tiny:
        one.start()
    local_cov.start()
    local_i.start()
    local_j.start()

    barrier = pltpu.get_barrier_semaphore()

    partners = [(tm, row, lax.rem(obs + d, SIDE)) for d in range(1, SIDE)]
    partners += [(tm, 2 * lax.rem(x + d, SIDE) + core, obs) for d in range(1, SIDE)]
    partners += [(tm, 2 * x + 1 - core, obs), up, down]
    for partner in partners:
        pl.semaphore_signal(barrier, inc=1, device_id=partner, device_id_type=MESH)
    pl.semaphore_wait(barrier, len(partners))

    for d in range(1, SIDE):
        obs_copy(1, d).start()
    gather_i.phase1()
    gather_j.phase1()

    local_obs.wait()
    for one in tiny:
        one.wait()
    for d in range(1, SIDE):
        obs_copy(1, d).wait_recv()
    for d, part in enumerate(factor_rows(blk[1:2, :], obs_v[1].reshape(BW, 2 * BW))):
        phi[1, :, d * BW : (d + 1) * BW] = part
    local_cov.wait()
    gain = mm(cov_v[0], phi[1], NT)
    ga[core, x, obs] = gain[0:16]
    small = jnp.concatenate([offs[...], odat[...]], axis=0)
    gb[core, obs, x] = gain[16:32]
    gs[core, x, obs] = jnp.zeros((8, BW), F32)
    gs[core, x, obs, 0:4, 0:PAN] = small
    gather_ga.phase1()
    gather_gb.phase1()
    gather_ga.phase2()
    gather_gb.phase2()
    gather_gs.phase1()
    local_i.wait()
    local_j.wait()
    gather_i.phase2()
    gather_j.phase2()
    gather_ga.phase3()
    gather_gb.phase3()
    for d in range(1, SIDE):
        obs_copy(0, d).start()
    gather_gs.phase2()
    gather_ga.finish()
    gather_gb.finish()
    gather_i.pass_on()
    gather_j.pass_on()

    for c in range(NB):
        both = jnp.concatenate([ga[c % 2, c // 2], gb[c % 2, :, c // 2]], axis=1)
        g_v[c * BW : (c + 1) * BW, :] = both.reshape(BW, BW)
    g = halves(g_v[...])
    phi_j = halves(phi[1])
    s1[...] = eye(BW) + mm(phi_j, g, NN)

    def hand_over():
        for one in (gather_i, gather_j, gather_gs):
            one.phase3()

    chol_inverse(s1, linv_v, hand_over)
    linv = halves(linv_v[...])
    k = mm(g, linv, NT)
    k_v[...] = k
    for c in range(NB):
        kb_v[c] = k[c * BW : (c + 1) * BW, :]
    kh = halves(k)
    p = cov_v[0] - mm(k_v[pl.ds(row0, PAN), :], kh, NT)
    gather_gs.finish()
    vecs = [
        jnp.concatenate([gs[c % 2, c // 2, o, :, 0:PAN] for o in range(SIDE)], axis=1) for c in range(NB)
    ]
    zeta_i = jnp.broadcast_to(vecs[0][2:3, :], (8, BW))
    zeta_j = jnp.broadcast_to(vecs[0][3:4, :], (8, BW))
    b_i = jnp.concatenate([jnp.broadcast_to(v[0:1, :], (8, BW)) for v in vecs], axis=1)
    b_j = jnp.concatenate([jnp.broadcast_to(v[1:2, :], (8, BW)) for v in vecs], axis=1)
    solved = mm(zeta_j - mm(b_i, phi_j, NT), linv, NT)
    xrow = b_i + mm(solved, kh, NT)
    gather_i.finish()

    for c in range(NB):
        t = mm(phi[1, :, c * BW : (c + 1) * BW], rows_i(c), NN)
        for d in range(NB):
            part = jnp.zeros((BW, BW), F32) if c == 0 else o_v[d]
            for n in range(3):
                part = part + is_block(pat[n, 0, c], d) * t[:, n * BW : (n + 1) * BW]
            o_v[d] = part
    for d in range(NB):
        u_v[d] = mm(linv, o_v[d], NN)
    t1[...] = u_v[row].T
    upper = t1[pl.ds(lo, PAN), :]
    drop = mm(upper, kh, NT)
    for c in range(NB):
        rows = rows_i(c)
        w = jnp.zeros((BW, BW), F32)
        for n in range(3):
            w = w + is_block(pat[n, 0, c], row) * rows[:, n * BW : (n + 1) * BW]
        t1[...] = w.T
        sl = slice(c * BW, (c + 1) * BW)
        xt[c] = jnp.concatenate([p[:, sl], t1[pl.ds(lo, PAN), :] - drop[:, sl], xrow[:, sl]], axis=0)
    gather_j.finish()
    y = jnp.concatenate(times_dyn_t(xt, pat, rows_j, 1), axis=1)
    for q, part in enumerate(pack(y[:PAN, :])):
        pk[q] = part
    swap1.start()
    lamt[...] = y[PAN : 2 * PAN, :]
    b_own = y[2 * PAN :, :] + b_j
    bz[...] = b_own

    @pl.when(jnp.logical_not(odd))
    def _():
        up_lam.start()
        up_b.start()

    for d in range(1, SIDE):
        obs_copy(0, d).wait_recv()
    for d, part in enumerate(factor_rows(blk[0:1, :], obs_v[0].reshape(BW, 2 * BW))):
        phi[0, :, d * BW : (d + 1) * BW] = part
    for d in range(NB):
        o_v[d] = phi[0, :, d * BW : (d + 1) * BW]
    t1[...] = o_v[row].T
    prior = t1[pl.ds(lo, PAN), :]
    fac[:, :BW] = upper
    fac[:, BW : 2 * BW] = prior
    fac[:, 2 * BW :] = jnp.zeros((PAN, 2 * BW), F32)
    info = mm(solved, upper, NT) + mm(zeta_i, prior, NT)
    swap1.finish()

    def send_up(n):
        @pl.when(jnp.logical_not(odd))
        def _():
            up_cov[n].start()

    unpack(rec, z1)
    for c in range(NB):
        sl = slice(c * BW, (c + 1) * BW)
        c_pan[:, sl] = dyn_times(z1, pat, rows_j, 1, c).T + cov_v[1, :, sl]
        if c % 2 == 1:
            send_up(c // 2)

    def my_panel(full):
        put_blocks(o_v.at[:, 0:8, :], full)
        block = o_v[row, 0:8, :]
        return pltpu.roll(block, lax.rem(BW - lo, BW), 1)[0:1, 0:PAN]

    @pl.when(jnp.logical_not(odd))
    def _():
        pieces = pltpu.make_async_copy(fac.at[:, 0 : 2 * BW], out_fac.at[0, :, 2 * BW :], own.at[6])
        pieces.start()
        pieces.wait()
        down_lam.wait_recv()
        for q, part in enumerate(pack(lamt2_in[...])):
            pkl[q] = part
        swap3.start()
        down_vec.wait_recv()
        out_off[...] = vec_in[0:1, 0:PAN]
        out_info[...] = info[0:1, :] + vec_in[1:2, 0:PAN]
        swap3.finish()
        unpack(recl, z1)
        for c in range(NB):
            lam[:, c * BW : (c + 1) * BW] = z1[c].reshape(BW, PAN).T
        dyn_out = pltpu.make_async_copy(lam, out_dyn.at[0], own.at[8])
        dyn_out.start()
        dyn_out.wait()
        swap3.drain()
        for one in down_cov:
            one.wait_recv()
        down_fac.wait_recv()
        up_lam.wait_send()
        up_b.wait_send()
        for one in up_cov:
            one.wait_send()

    @pl.when(odd)
    def _():
        out_off[...] = my_panel(b_own)
        out_info[...] = info[0:1, :]
        ones = [
            pltpu.make_async_copy(c_pan, out_cov.at[0], own.at[6]),
            pltpu.make_async_copy(fac, out_fac.at[0], own.at[7]),
        ]
        for one in ones:
            one.start()
        up_lam.wait_recv()
        up_b.wait_recv()
        lam_parts = [jnp.zeros((PAN, BW), F32) for _ in range(NB)]
        ak = jnp.zeros((PAN, BW), F32)
        for n in range(3):
            b = pat[n, 1, row]
            block = vj[core, obs, x, :, n * BW : (n + 1) * BW]
            mine = halves(block)
            t = mm(mine, vi[lax.rem(b, 2), lax.div(b, 2)].reshape(BW, 3 * BW), NN)
            for m in range(3):
                at = pat[m, 0, b]
                for d in range(NB):
                    lam_parts[d] = lam_parts[d] + is_block(at, d) * t[:, m * BW : (m + 1) * BW]
            ak = ak + mm(mine, kb_v[b], NN)
        akh = halves(ak)
        for d in range(NB):
            lam[:, d * BW : (d + 1) * BW] = lam_parts[d] - mm(akh, u_v[d], NN)
        dyn_out = pltpu.make_async_copy(lam, out_dyn.at[0], own.at[8])
        dyn_out.start()

        u = jnp.concatenate([u_v[d] for d in range(NB)], axis=1)
        phi_b = halves(jnp.concatenate([u, phi[0]], axis=0))
        gain2 = jnp.zeros((PAN, 2 * BW), F32)
        for n in range(ST // CHUNK):
            up_cov[n].wait_recv()
            part = tuple(h[:, n * CHUNK : (n + 1) * CHUNK] for h in phi_b)
            gain2 = gain2 + mm(ca[:, chunk(n)], part, NT)
        g2a[core, x, obs] = gain2[:, :BW]
        g2b[core, obs, x] = gain2[:, BW:]
        gather_2a.phase1()
        gather_2b.phase1()
        la, bp = lamt_a[...], ba[...]
        start = jnp.concatenate([ca[...], la, bp], axis=0)
        across = mm(start[PAN:], phi_b, NT)
        seen = across[:PAN]
        resid = jnp.concatenate([solved, zeta_i], axis=1) - across[PAN:]
        gather_2a.phase2()
        gather_2b.phase2()
        gather_2a.phase3()
        gather_2b.phase3()
        gather_2a.finish()
        gather_2b.finish()
        for c in range(NB):
            g2_v[c * BW : (c + 1) * BW, :BW] = g2a[c % 2, c // 2].reshape(BW, BW)
            g2_v[c * BW : (c + 1) * BW, BW:] = g2b[c % 2, :, c // 2].reshape(BW, BW)
        g2 = halves(g2_v[...])
        s2[...] = eye(2 * BW) + mm(phi_b, g2, NN)
        chol_inverse_2(s2, linv2_v, t1, n1)
        linv2 = halves(linv2_v[...])
        ahead = mm(jnp.concatenate([g2_v[pl.ds(row0, PAN), :], seen, resid], axis=0), linv2, NT)
        fac2[...] = ahead[PAN : 2 * PAN]
        down_fac.start()
        solved2 = ahead[2 * PAN :]
        sign = jnp.where(lax.broadcasted_iota(jnp.int32, (2 * PAN + 8, 1), 0) < 2 * PAN, -1.0, 1.0)
        xs = start + mm(sign * mm(ahead, linv2, NN), g2, NT)
        put_blocks(xt, xs)
        h = jnp.concatenate(times_dyn_t(xt, pat, rows_i, 0), axis=1)
        put_blocks(xt, h - mm(mm(xs, u, NT), k_v[...], NT))
        y2 = jnp.concatenate(times_dyn_t(xt, pat, rows_j, 1), axis=1)
        lamt2[...] = y2[PAN : 2 * PAN, :]
        down_lam.start()
        for q, part in enumerate(pack(y2[:PAN, :])):
            pk2[q] = part
        swap2.start()
        vec[...] = jnp.zeros((8, BW), F32)
        vec[0:1, 0:PAN] = my_panel(y2[2 * PAN :, :] + b_own)
        vec[1:2, 0:PAN] = mm(solved2, fac2[...], NT)[0:1, :]
        down_vec.start()
        swap2.finish()
        unpack(rec2, z1)
        uz = jnp.zeros((BW, PAN), F32)
        for d in range(NB):
            uz = uz + mm(u_v[d], z1[d].reshape(BW, PAN), NN)
        kz = mm(k_v[...], uz, NN)
        for c in range(NB):
            part = dyn_times(z1, pat, rows_i, 0, c) - kz[c * BW : (c + 1) * BW, :]
            z2[c] = part.reshape(4, PAN, PAN)
        for c in range(NB):
            sl = slice(c * BW, (c + 1) * BW)
            c2[:, sl] = dyn_times(z2, pat, rows_j, 1, c).T + c_pan[:, sl]
            if c % 2 == 1:
                down_cov[c // 2].start()
        for one in ones:
            one.wait()
        dyn_out.wait()
        gather_2a.drain()
        gather_2b.drain()
        swap2.drain()
        for one in [down_fac, down_vec, down_lam] + down_cov:
            one.wait_send()

    for e in range(2):
        for d in range(1, SIDE):
            obs_copy(e, d).wait_send()
    for one in (gather_i, gather_j, gather_ga, gather_gb, gather_gs):
        one.drain()
    swap1.drain()


def vmem(*shape):
    return pltpu.VMEM(shape, F32)


def dma(*shape):
    return pltpu.SemaphoreType.DMA(shape)


SCRATCH = [
    vmem(2, PAN, ST), vmem(2, SIDE, PAN, 2 * BW),
    vmem(2, SIDE, SIDE, PAN, 3 * BW), vmem(2, SIDE, SIDE, PAN, 3 * BW),
    vmem(2, SIDE, SIDE, 16, BW), vmem(2, SIDE, SIDE, 16, BW), vmem(2, SIDE, SIDE, 8, BW),
    vmem(2, BW, ST),
    vmem(BW, BW), vmem(BW, BW), vmem(BW, BW), vmem(BW, BW),
    vmem(2 * BW, 2 * BW), vmem(2 * BW, 2 * BW),
    vmem(ST, BW), vmem(ST, BW), vmem(NB, BW, BW), vmem(NB, BW, BW), vmem(NB, 2 * PAN + 8, BW),
    vmem(GROUP, 8, BW), vmem(GROUP, 8, BW),
    vmem(PAN, ST), vmem(PAN, ST), vmem(8, ST), vmem(8, ST), vmem(PAN, ST), vmem(PAN, ST),
    vmem(2, SIDE, SIDE, PAN, BW), vmem(2, SIDE, SIDE, PAN, BW),
    vmem(ST, 2 * BW),
    vmem(GROUP, 8, BW), vmem(GROUP, 8, BW), vmem(GROUP, 8, BW), vmem(GROUP, 8, BW),
    vmem(PAN, ST), vmem(PAN, ST),
    vmem(PAN, 2 * BW), vmem(PAN, ST), vmem(8, BW), vmem(8, BW),
    vmem(PAN, ST), vmem(PAN, 4 * BW),
    vmem(NB, 4, PAN, PAN), vmem(NB, 4, PAN, PAN), vmem(NB, BW, BW),
    vmem(2, PAN), pltpu.VMEM((2, BW), jnp.int32), vmem(2, PAN),
    dma(2, 3), dma(2, 3), dma(7, 12), dma(7, 12), dma(6), dma(13), dma(13), dma(12),
]


def place_body(*refs):
    n = len(refs) // 2
    sems = refs[-1]
    copies = [pltpu.make_async_copy(refs[i], refs[n + i], sems.at[i]) for i in range(n)]
    for one in copies:
        one.start()
    for one in copies:
        one.wait()


def per_device(dyn_pattern, *rest):
    outs = [(1, PAN, ST), (1, PAN), (1, PAN, ST), (1, PAN, 4 * BW), (1, PAN)]
    found = pl.pallas_call(
        kernel,
        out_shape=[jax.ShapeDtypeStruct(s, F32) for s in outs],
        in_specs=[SM] + [ANY] * 6,
        out_specs=[ANY, VM, ANY, ANY, VM],
        scratch_shapes=SCRATCH,
        compiler_params=pltpu.CompilerParams(
            collective_id=0, has_side_effects=True, vmem_limit_bytes=60 << 20
        ),
    )(jnp.transpose(dyn_pattern, (2, 0, 1)), *rest)
    return pl.pallas_call(
        place_body,
        out_shape=[jax.ShapeDtypeStruct(s, F32) for s in outs],
        in_specs=[VM] * len(outs),
        out_specs=[ANY] * len(outs),
        scratch_shapes=[dma(len(outs))],
    )(*found)


def solution(mesh):
    placed = (
        P("tm", None, None),
        P("tm", ("row", "obs"), None),
        P("tm", ("row", "obs")),
        P("tm", ("row", "obs"), None),
        P("tm", None),
        P("tm", "obs", None),
        P("tm", "obs"),
    )
    return jax.shard_map(
        per_device,
        mesh=mesh,
        in_specs=placed,
        out_specs=(
            P("tm", ("row", "obs"), None),
            P("tm", ("row", "obs")),
            P("tm", ("row", "obs"), None),
            P("tm", ("row", "obs"), None),
            P("tm", ("row", "obs")),
        ),
        check_vma=False,
    )
```
